32 devices in a mesh: row: 8 (over y, x, core), col: 4 (over z).
Axes of the slice: x: 2, y: 2, z: 4, core: 2. Of those that a mesh axis runs over, the one named last changes fastest.
Arguments:
- resid: float32 [32, 960, 1024], P('row', 'col'), may hold values from -6 to 6
- cotangent: float32 [32, 960, 1024], P('row', 'col'), may hold values from -6 to 6
- prefix: int32 [32], P('row'), may hold values from 102 to 512, as said below
- slot: int32 [32], P('row'), may hold values from 0 to 3, as said below
- chosen: int32 [4, 8, 768], P(None, 'row'), may hold values from 0 to 1023, as said below
- norm1_gain: float32 [960], replicated, may hold values from 0.25 to 1.75
- norm2_gain: float32 [960], replicated, may hold values from 0.25 to 1.75
- router: float32 [960], replicated, may hold values from -0.125 to 0.125
- w_query: bfloat16 [960, 960], P('row', 'col'), may hold values from -0.1875 to 0.1875
- w_key: bfloat16 [960, 320], P('row', 'col'), may hold values from -0.1875 to 0.1875
- w_value: bfloat16 [960, 320], P('row', 'col'), may hold values from -0.1875 to 0.1875
- w_out: bfloat16 [960, 960], P('row', 'col'), may hold values from -2 to 2
- w_gate: bfloat16 [960, 2560], P('row', 'col'), may hold values from -0.1875 to 0.1875
- w_up: bfloat16 [960, 2560], P('row', 'col'), may hold values from -0.1875 to 0.1875
- w_down: bfloat16 [2560, 960], P('row', 'col'), may hold values from -0.25 to 0.25
Outputs:
- block_out: float32 [32, 960, 1024], P('row', 'col')
- resid_grad: float32 [32, 960, 1024], P('row', 'col')
- norm1_gain_grad: float32 [960], P('col')
- norm2_gain_grad: float32 [960], P('col')
- router_grad: float32 [960], P('col')
- w_query_grad: float32 [960, 960], P('row', 'col')
- w_key_grad: float32 [960, 320], P('row', 'col')
- w_value_grad: float32 [960, 320], P('row', 'col')
- w_out_grad: float32 [960, 960], P('row', 'col')
- w_gate_grad: float32 [960, 2560], P('row', 'col')
- w_up_grad: float32 [960, 2560], P('row', 'col')
- w_down_grad: float32 [2560, 960], P('row', 'col')
The draws below stay inside these ranges and needn't reach their ends.
Inputs may be any that keep to these rules, and one draw needn't show every extreme that they name: Some sequence has a prefix of exactly 512 tokens and some one of exactly 102. `slot`: the 4 sequences stored on one index of row take the micro-batches 0 to 3, one each. `chosen`: for each micro-batch and row index the 768 positions are distinct.
All inputs are finite; a program needn't handle non-finite values.
Results may differ from the reference program's by a relative error of at most 0.039.
Values may be sent and summed in bfloat16 or wider, within the bound.
No kernel may reach another device: no remote copies, remote signals or barrier semaphores. Data moves between devices by JAX's collectives and lax.ppermute only.
A program may use at most 256 MiB of HBM per device.

```python
import math
import jax
import jax.numpy as jnp
from jax import lax

H = 15
KVH = 5
HD = 64
D = 960
FF = 2560
L = 1024
MICRO = 4
SEQS = 32
PICK = 768


def draw_prefix(key, part):
    lowest = L // 10
    highest = L // 2
    drawn_lengths = jax.random.randint(key, (SEQS,), lowest, highest + 1, dtype=jnp.int32)
    ordering = jax.random.permutation(jax.random.fold_in(key, 7), SEQS)
    return drawn_lengths.at[ordering[0]].set(highest).at[ordering[1]].set(lowest)


def draw_slot(key, part):
    row_keys = jax.random.split(key, SEQS // MICRO)
    orders = jax.vmap(lambda row_key: jax.random.permutation(row_key, MICRO))(row_keys)
    return orders.reshape(SEQS).astype(jnp.int32)


def draw_chosen(key, part):
    many_keys = jax.random.split(key, SEQS)
    positions = jax.vmap(lambda one_key: jax.random.permutation(one_key, L)[:PICK])(many_keys)
    return positions.reshape(MICRO, SEQS // MICRO, PICK).astype(jnp.int32)


def shard_levels(rng, dims, cuts, low, high):
    loudness = 1.0
    for position, blocks in cuts:
        draws = jax.random.uniform(jax.random.fold_in(jax.random.fold_in(rng, 6), position), (blocks,), jnp.float32, low / len(cuts), high / len(cuts))
        loudness = loudness * jnp.repeat(jnp.exp(draws), dims[position] // blocks).reshape((-1,) + (1,) * (len(dims) - 1 - position))
    return loudness


def scatter_about(stream_key, dims, width, reach, cuts=(), held_as=jnp.bfloat16):
    array = jax.random.normal(stream_key, dims, jnp.float32) * width
    if len(cuts) > 0:
        array = shard_levels(stream_key, dims, cuts, -0.22, 0.18) * array
    return jnp.clip(array, min=-reach, max=reach).astype(held_as)


def setup_inputs(seed: int = 0) -> dict:
    arg_keys = jax.random.split(jax.random.key(seed), 16)
    return {
        "resid": scatter_about(arg_keys[0], (SEQS, D, L), 1.0, 6.0, ((0, 8), (1, 4)), jnp.float32),
        "cotangent": scatter_about(arg_keys[1], (SEQS, D, L), 1.0, 6.0, ((0, 8), (1, 4)), jnp.float32),
        "prefix": draw_prefix(jax.random.fold_in(arg_keys[15], 71), 0),
        "slot": draw_slot(jax.random.fold_in(arg_keys[15], 71), 0),
        "chosen": draw_chosen(jax.random.fold_in(arg_keys[15], 71), 0),
        "norm1_gain": jnp.clip(1.0 + 0.15 * jax.random.normal(arg_keys[5], (D,), jnp.float32), 0.25, 1.75),
        "norm2_gain": jnp.clip(1.0 + 0.15 * jax.random.normal(arg_keys[6], (D,), jnp.float32), 0.25, 1.75),
        "router": scatter_about(arg_keys[7], (D,), (2 * D) ** -0.5, 0.125, (), jnp.float32),
        "w_query": scatter_about(arg_keys[8], (D, D), D ** -0.5, 0.1875, ((0, 8), (1, 4))),
        "w_key": scatter_about(arg_keys[9], (D, KVH * HD), D ** -0.5, 0.1875, ((0, 8), (1, 4))),
        "w_value": scatter_about(arg_keys[10], (D, KVH * HD), D ** -0.5, 0.1875, ((0, 8), (1, 4))),
        "w_out": scatter_about(arg_keys[11], (D, D), (D // 128) ** -0.5, 2.0, ((0, 8), (1, 4))),
        "w_gate": scatter_about(arg_keys[12], (D, FF), D ** -0.5, 0.1875, ((0, 8), (1, 4))),
        "w_up": scatter_about(arg_keys[13], (D, FF), D ** -0.5, 0.1875, ((0, 8), (1, 4))),
        "w_down": scatter_about(arg_keys[14], (FF, D), (FF // 4) ** -0.5, 0.25, ((0, 8), (1, 4))),
    }


EPSILON = 1e-05
ROPE_BASE = 10000.0

@jax.custom_vjp
def low(v):
    return lax.optimization_barrier(v.astype(jnp.bfloat16)).astype(jnp.float32)

@jax.custom_vjp
def low_back(v):
    return v

def low_keep(v):
    return (low(v), None)

def low_pass(kept, grad):
    return (grad,)

def back_keep(v):
    return (v, None)

def back_low(kept, grad):
    return (low(grad),)
low.defvjp(low_keep, low_pass)
low_back.defvjp(back_keep, back_low)

def matmul(left_side, right_side):
    return jnp.dot(left_side, right_side, precision=lax.Precision.HIGHEST, preferred_element_type=jnp.float32)

def rms_norm(values, gain_vec):
    inverse_rms = lax.rsqrt(lax.optimization_barrier(jnp.mean(values * values, axis=-1, keepdims=True)) + EPSILON)
    return values * inverse_rms * gain_vec

def rotate(values, positions):
    half_width = values.shape[-1] // 2
    frequency = jnp.exp(jnp.arange(half_width, dtype=jnp.float32) * (-2.0 * math.log(ROPE_BASE) / values.shape[-1]))
    angles = positions.astype(jnp.float32)[:, None] * frequency[None, :]
    cosine_table = jnp.cos(angles)[:, None, :]
    sine_table = jnp.sin(angles)[:, None, :]
    first_half = values[..., :half_width]
    second = values[..., half_width:]
    return jnp.concatenate([first_half * cosine_table - second * sine_table, second * cosine_table + first_half * sine_table], axis=-1)

def block_layer(params, resid, selected, prefix_len):
    gain_one, gain_two, router, w_query, w_key, w_value, w_out, w_gate, w_up, w_down = params
    length = resid.shape[0]
    positions = jnp.arange(length, dtype=jnp.int32)
    normed_one = low(rms_norm(resid, gain_one))
    queries = low(rotate(low(low_back(matmul(normed_one, w_query))).reshape(length, H, HD), positions))
    key_rows = low(rotate(low(low_back(matmul(normed_one, w_key))).reshape(length, KVH, HD), positions))
    value_rows = low(low_back(matmul(normed_one, w_value))).reshape(length, KVH, HD)
    grouped = queries.reshape(length, KVH, H // KVH, HD)
    scores = jnp.einsum('qkgd,tkd->kgqt', grouped, key_rows, precision=lax.Precision.HIGHEST, preferred_element_type=jnp.float32) * HD ** (-0.5)
    scores = low_back(scores)
    allowed = (positions[None, :] <= positions[:, None]) | (positions[None, :] < prefix_len)
    scores = jnp.where(allowed, scores, -1e+30)
    weights = low(jax.nn.softmax(scores, axis=-1))
    attended = jnp.einsum('kgqt,tkd->qkgd', weights, value_rows, precision=lax.Precision.HIGHEST, preferred_element_type=jnp.float32).reshape(length, H * HD)
    attended = low(low_back(attended))
    branch_attn = low_back(matmul(attended, w_out))
    hidden = resid + branch_attn
    normed_two = low(rms_norm(hidden, gain_two))
    gate_proj = low_back(matmul(normed_two, w_gate))
    up_proj = low_back(matmul(normed_two, w_up))
    active = low(jax.nn.silu(gate_proj) * up_proj)
    branch_ffn = low_back(matmul(active, w_down))
    router_logit = matmul(resid, router[:, None])[:, 0]
    gate_share = selected * jax.nn.sigmoid(router_logit)
    return resid + gate_share[:, None] * (branch_attn + branch_ffn)

def reference(resid, cotangent, prefix, slot, chosen, norm1_gain, norm2_gain, router, w_query, w_key, w_value, w_out, w_gate, w_up, w_down):
    params = (norm1_gain, norm2_gain, router) + tuple((weight.astype(jnp.float32) for weight in (w_query, w_key, w_value, w_out, w_gate, w_up, w_down)))
    positions = jnp.arange(L, dtype=jnp.int32)

    def seq_step(totals, seq_index):
        row_index = seq_index // MICRO
        chosen_rows = chosen[slot[seq_index], row_index]
        selected = jnp.any(positions[:, None] == chosen_rows[None, :], axis=1).astype(jnp.float32)
        prefix_len = prefix[seq_index]

        def forward(param_set, resid_seq):
            return block_layer(param_set, resid_seq, selected, prefix_len)
        output, pullback = jax.vjp(forward, params, resid[seq_index].T)
        gradients, resid_grad = pullback(cotangent[seq_index].T)
        totals = jax.tree.map(lambda summed, fresh_grad: summed + fresh_grad, totals, gradients)
        return (totals, (output.T, resid_grad.T))
    zero_grads = jax.tree.map(jnp.zeros_like, params)
    totals, (block_out, resid_grad) = lax.scan(seq_step, zero_grads, jnp.arange(SEQS, dtype=jnp.int32))
    return (block_out, resid_grad) + tuple(totals)
```

```python
import functools
import math

import jax
import jax.numpy as jnp
from jax import lax
from jax.experimental import pallas as pl
from jax.experimental.pallas import tpu as pltpu
from jax.sharding import PartitionSpec as P

H = 15
KVH = 5
HD = 64
GROUP = H // KVH
QBLOCK = 256

EPSILON = 1e-05
ROPE_BASE = 10000.0
NEG = -1e30

BF = jnp.bfloat16
F32 = jnp.float32
MIB = 1 << 20


def dot_nn(a, b):
    return lax.dot_general(a, b, (((1,), (0,)), ((), ())), preferred_element_type=F32)


def dot_tn(a, b):
    return lax.dot_general(a, b, (((0,), (0,)), ((), ())), preferred_element_type=F32)


def dot_nt(a, b):
    return lax.dot_general(a, b, (((1,), (1,)), ((), ())), preferred_element_type=F32)


def params(limit=56):
    return pltpu.CompilerParams(
        dimension_semantics=("arbitrary",), vmem_limit_bytes=limit * MIB
    )


def cost(flops, nbytes, exps=0):
    return pl.CostEstimate(
        flops=int(flops), bytes_accessed=int(nbytes), transcendentals=int(exps)
    )


def struct(shape, dtype):
    return jax.ShapeDtypeStruct(shape, dtype)


def whole(shape):
    return pl.BlockSpec(shape, lambda i: (0,) * len(shape))


def pick_columns(rank_column, picks):
    place = lax.broadcasted_iota(jnp.int32, (rank_column.shape[0], picks), 1)
    return jnp.where(rank_column == place, 1.0, 0.0).astype(BF)


def pick_rows(rank_row, picks):
    place = lax.broadcasted_iota(jnp.int32, (picks, rank_row.shape[1]), 0)
    return jnp.where(rank_row == place, 1.0, 0.0).astype(BF)


def turn(first, second, cosine, sine, direction):
    signed = sine * direction
    return first * cosine - second * signed, second * cosine + first * signed


def gather_body(values, rank, out):
    chosen = pick_columns(rank[0], out.shape[2])
    out[0] = dot_nn(values[0].astype(BF), chosen).astype(BF)


def gather_tokens(values, rank_column, picks):
    count, width, length = values.shape
    return pl.pallas_call(
        gather_body,
        grid=(count,),
        in_specs=[
            pl.BlockSpec((1, width, length), lambda i: (i, 0, 0)),
            pl.BlockSpec((1, length, 1), lambda i: (i, 0, 0)),
        ],
        out_specs=pl.BlockSpec((1, width, picks), lambda i: (i, 0, 0)),
        out_shape=struct((count, width, picks), BF),
        compiler_params=params(),
        cost_estimate=cost(2 * count * width * length * picks, 6 * values.size),
        name="gather_tokens",
    )(values, rank_column)


def scatter_body(base, values, rank, out):
    chosen = pick_rows(rank[0], values.shape[2])
    out[0] = base[0] + dot_nn(values[0], chosen)


def scatter_tokens(base, values, rank_row):
    count, width, length = base.shape
    picks = values.shape[2]
    return pl.pallas_call(
        scatter_body,
        grid=(count,),
        in_specs=[
            pl.BlockSpec((1, width, length), lambda i: (i, 0, 0)),
            pl.BlockSpec((1, width, picks), lambda i: (i, 0, 0)),
            pl.BlockSpec((1, 1, length), lambda i: (i, 0, 0)),
        ],
        out_specs=pl.BlockSpec((1, width, length), lambda i: (i, 0, 0)),
        out_shape=struct(base.shape, F32),
        compiler_params=params(),
        cost_estimate=cost(2 * count * width * length * picks, 10 * base.size),
        name="scatter_tokens",
    )(base, values, rank_row)


def project_body(
    x, rank, gain, router, cos_k, sin_k, cos_q, sin_q, w,
    picked, prob, q_out, kt_out, k_out, vt_out, v_out,
    normed, normed_picked, q_raw, kv_raw,
):
    step = pl.program_id(0)
    width = x.shape[0]
    q_part = q_raw.shape[0] // w_count(w, width)
    kv_part = (w.shape[2] - q_part) // 2

    @pl.when(step == 0)
    def _():
        full = x[...].astype(F32)
        inverse = lax.rsqrt(jnp.sum(full * full, axis=0, keepdims=True) / width + EPSILON)
        normed[...] = (full * inverse * gain[...]).astype(BF)
        chosen = pick_columns(rank[...], picked.shape[1])
        part = dot_nn(x[...], chosen)
        picked[...] = part.astype(BF)
        inverse = lax.rsqrt(jnp.sum(part * part, axis=0, keepdims=True) / width + EPSILON)
        normed_picked[...] = (part * inverse * gain[...]).astype(BF)
        logit = jnp.sum(part * router[...], axis=0, keepdims=True)
        prob[...] = jax.nn.sigmoid(logit)

    q_raw[pl.ds(pl.multiple_of(step * q_part, 8), q_part)] = dot_tn(
        w[0, :, :q_part], normed_picked[...]
    ).astype(BF)
    kv = dot_tn(w[0, :, q_part:], normed[...]).astype(BF)
    kv_raw[0, pl.ds(pl.multiple_of(step * kv_part, 8), kv_part)] = kv[:kv_part]
    kv_raw[1, pl.ds(pl.multiple_of(step * kv_part, 8), kv_part)] = kv[kv_part:]

    @pl.when(step == pl.num_programs(0) - 1)
    def _():
        half = HD // 2
        for head in range(H):
            at = head * HD
            a, b = turn(
                q_raw[at : at + half].astype(F32),
                q_raw[at + half : at + HD].astype(F32),
                cos_q[...], sin_q[...], 1.0,
            )
            scale = HD ** (-0.5)
            q_out[at : at + half] = (a.astype(BF).astype(F32) * scale).astype(BF)
            q_out[at + half : at + HD] = (b.astype(BF).astype(F32) * scale).astype(BF)
        for head in range(KVH):
            at = head * HD
            a, b = turn(
                kv_raw[0, at : at + half].astype(F32),
                kv_raw[0, at + half : at + HD].astype(F32),
                cos_k[...], sin_k[...], 1.0,
            )
            turned = jnp.concatenate([a, b], axis=0)
            kt_out[at : at + HD] = turned.astype(BF)
            k_out[head] = turned.T.astype(BF)
            value = kv_raw[1, at : at + HD]
            vt_out[at : at + HD] = value
            v_out[head] = value.astype(F32).T.astype(BF)


def w_count(w, width):
    whole_width = width + 2 * (width * KVH // H)
    return whole_width // w.shape[2]


def project(x, rank_column, gain, router, tables_k, tables_q, w):
    width, length = x.shape
    picks = tables_q[0].shape[1]
    blocks, _, part = w.shape
    kv = KVH * HD
    half = HD // 2
    return pl.pallas_call(
        project_body,
        grid=(blocks,),
        in_specs=[
            whole((width, length)),
            whole((length, 1)),
            whole((width, 1)),
            whole((width, 1)),
            whole((half, length)),
            whole((half, length)),
            whole((half, picks)),
            whole((half, picks)),
            pl.BlockSpec((1, width, part), lambda i: (i, 0, 0)),
        ],
        out_specs=[
            whole((width, picks)),
            whole((1, picks)),
            whole((width, picks)),
            whole((kv, length)),
            whole((KVH, length, HD)),
            whole((kv, length)),
            whole((KVH, length, HD)),
        ],
        out_shape=[
            struct((width, picks), BF),
            struct((1, picks), F32),
            struct((width, picks), BF),
            struct((kv, length), BF),
            struct((KVH, length, HD), BF),
            struct((kv, length), BF),
            struct((KVH, length, HD), BF),
        ],
        scratch_shapes=[
            pltpu.VMEM((width, length), BF),
            pltpu.VMEM((width, picks), BF),
            pltpu.VMEM((width, picks), BF),
            pltpu.VMEM((2, kv, length), BF),
        ],
        compiler_params=params(),
        cost_estimate=cost(
            2 * width * (length * picks + picks * width + length * 2 * kv),
            2 * (w.size + 4 * x.size),
        ),
        name="project",
    )(x, rank_column, gain, router, *tables_k, *tables_q, w)


def reach_of(block, length, picks):
    return max((block + 1) * QBLOCK + length - picks, length // 2)


def clear_of(block):
    return block * QBLOCK


def block_scores(q, k, limit, block, reach):
    scores = dot_nn(k[:reach], q)
    clear = clear_of(block)
    tail = scores[clear:] if clear else scores
    key = lax.broadcasted_iota(jnp.int32, tail.shape, 0) + clear
    tail = jnp.where(key <= limit, tail, NEG)
    return jnp.concatenate([scores[:clear], tail], axis=0) if clear else tail


def attend_body(q, k, vt, limit, out, total):
    length = k.shape[1]
    picks = q.shape[1]
    for block in range(picks // QBLOCK):
        at = block * QBLOCK
        reach = reach_of(block, length, picks)
        for head in range(GROUP):
            rows = slice(head * HD, (head + 1) * HD)
            scores = block_scores(
                q[rows, at : at + QBLOCK], k[0], limit[:, at : at + QBLOCK], block, reach
            )
            top = jnp.max(scores, axis=0, keepdims=True)
            weight = jnp.exp(scores - top)
            mass = jnp.sum(weight, axis=0, keepdims=True)
            mixed = dot_nn(vt[:, :reach], weight.astype(BF))
            out[rows, at : at + QBLOCK] = (mixed / mass).astype(BF)
            total[0, head : head + 1, at : at + QBLOCK] = top + jnp.log(mass)


def attend(q, k, vt, limit):
    width, picks = q.shape
    length = k.shape[1]
    part = GROUP * HD
    return pl.pallas_call(
        attend_body,
        grid=(KVH,),
        in_specs=[
            pl.BlockSpec((part, picks), lambda i: (i, 0)),
            pl.BlockSpec((1, length, HD), lambda i: (i, 0, 0)),
            pl.BlockSpec((HD, length), lambda i: (i, 0)),
            whole((1, picks)),
        ],
        out_specs=[
            pl.BlockSpec((part, picks), lambda i: (i, 0)),
            pl.BlockSpec((1, GROUP, picks), lambda i: (i, 0, 0)),
        ],
        out_shape=[struct((width, picks), BF), struct((KVH, GROUP, picks), F32)],
        compiler_params=params(),
        cost_estimate=cost(
            16 * width * length * picks, 4 * width * picks, H * length * picks
        ),
        name="attend",
    )(q, k, vt, limit)


def attend_back_body(
    q, k, kt, v, limit, total, grad, mixed, cos_k, sin_k, cos_q, sin_q,
    gq_out, gk_out, gv_out, gk, gv,
):
    length = k.shape[1]
    picks = q.shape[1]
    half = HD // 2
    gk[...] = jnp.zeros_like(gk)
    gv[...] = jnp.zeros_like(gv)
    for block in range(picks // QBLOCK):
        at = block * QBLOCK
        cols = slice(at, at + QBLOCK)
        reach = reach_of(block, length, picks)
        for head in range(GROUP):
            rows = slice(head * HD, (head + 1) * HD)
            q_part = q[rows, cols]
            g_part = grad[rows, cols]
            scores = block_scores(q_part, k[0], limit[:, cols], block, reach)
            weight = jnp.exp(scores - total[0, head : head + 1, cols])
            delta = jnp.sum(
                g_part.astype(F32) * mixed[rows, cols].astype(F32), axis=0, keepdims=True
            )
            pull = dot_nn(v[0, :reach], g_part)
            back = (weight * (pull - delta)).astype(BF)
            gq = dot_nn(kt[:, :reach], back) * HD ** (-0.5)
            a, b = turn(gq[:half], gq[half:], cos_q[:, cols], sin_q[:, cols], -1.0)
            gq_out[head * HD : head * HD + half, cols] = a.astype(BF)
            gq_out[head * HD + half : (head + 1) * HD, cols] = b.astype(BF)
            gk[:reach] += dot_nt(back, q_part)
            gv[:reach] += dot_nt(weight.astype(BF), g_part)
    turned = gk[...].T
    a, b = turn(turned[:half], turned[half:], cos_k[...], sin_k[...], -1.0)
    gk_out[:half] = a.astype(BF)
    gk_out[half:] = b.astype(BF)
    gv_out[...] = gv[...].T.astype(BF)


def attend_back(q, k, kt, v, limit, total, grad, mixed, tables_k, tables_q):
    width, picks = q.shape
    length = k.shape[1]
    part = GROUP * HD
    half = HD // 2
    wide = pl.BlockSpec((part, picks), lambda i: (i, 0))
    tall = pl.BlockSpec((1, length, HD), lambda i: (i, 0, 0))
    flat = pl.BlockSpec((HD, length), lambda i: (i, 0))
    return pl.pallas_call(
        attend_back_body,
        grid=(KVH,),
        in_specs=[
            wide, tall, flat, tall, whole((1, picks)),
            pl.BlockSpec((1, GROUP, picks), lambda i: (i, 0, 0)),
            wide, wide,
            whole((half, length)), whole((half, length)),
            whole((half, picks)), whole((half, picks)),
        ],
        out_specs=[wide, flat, flat],
        out_shape=[
            struct((width, picks), BF),
            struct((KVH * HD, length), BF),
            struct((KVH * HD, length), BF),
        ],
        scratch_shapes=[pltpu.VMEM((length, HD), F32), pltpu.VMEM((length, HD), F32)],
        compiler_params=params(),
        cost_estimate=cost(
            40 * width * length * picks, 8 * width * picks, H * length * picks
        ),
        name="attend_back",
    )(q, k, kt, v, limit, total, grad, mixed, *tables_k, *tables_q)


def merge_body(mixed, picked, cot, prob, gain, w, branch, inverse_out, normed, grad_ffn, hidden, square):
    step = pl.program_id(0)
    width = mixed.shape[0]
    part = w.shape[2]
    rows = pl.ds(pl.multiple_of(step * part, 8), part)

    @pl.when(step == 0)
    def _():
        square[...] = jnp.zeros_like(square)
        grad_ffn[...] = (prob[...] * cot[...].astype(F32)).astype(BF)

    value = dot_tn(w[0], mixed[...])
    branch[...] = value
    total = picked[rows, :].astype(F32) + value
    hidden[rows, :] = total
    square[...] += jnp.sum(total * total, axis=0, keepdims=True)

    @pl.when(step == pl.num_programs(0) - 1)
    def _():
        inverse = lax.rsqrt(square[...] / width + EPSILON)
        inverse_out[...] = inverse
        normed[...] = (hidden[...] * inverse * gain[...]).astype(BF)


def merge(mixed, picked, cot, prob, gain, w):
    width, picks = mixed.shape
    blocks, _, part = w.shape
    return pl.pallas_call(
        merge_body,
        grid=(blocks,),
        in_specs=[
            whole((width, picks)),
            whole((width, picks)),
            whole((width, picks)),
            whole((1, picks)),
            whole((width, 1)),
            pl.BlockSpec((1, width, part), lambda i: (i, 0, 0)),
        ],
        out_specs=[
            pl.BlockSpec((part, picks), lambda i: (i, 0)),
            whole((1, picks)),
            whole((width, picks)),
            whole((width, picks)),
        ],
        out_shape=[
            struct((width, picks), F32),
            struct((1, picks), F32),
            struct((width, picks), BF),
            struct((width, picks), BF),
        ],
        scratch_shapes=[pltpu.VMEM((width, picks), F32), pltpu.VMEM((1, picks), F32)],
        compiler_params=params(),
        cost_estimate=cost(2 * width * width * picks, 14 * width * picks + 2 * w.size),
        name="merge",
    )(mixed, picked, cot, prob, gain, w)


def ffn_body(
    normed, grad_ffn, branch, picked, cot, prob, inverse, gain, router, w_gate, w_up, w_down,
    delta_out, grad_attn, rest_out, logit_out, gain_out, router_out, gw_gate, gw_up, gw_down,
    forward, backward,
):
    step = pl.program_id(0)
    width = normed.shape[0]
    columns, _, part = w_down.shape

    @pl.when(step == 0)
    def _():
        forward[...] = jnp.zeros_like(forward)
        backward[...] = jnp.zeros_like(backward)

    tokens = normed[...]
    gate = dot_tn(w_gate[0], tokens)
    up = dot_tn(w_up[0], tokens)
    pull = dot_nn(w_down[0], grad_ffn[:part])
    for c in range(1, columns):
        pull += dot_nn(w_down[c], grad_ffn[c * part : (c + 1) * part])
    sigmoid = jax.nn.sigmoid(gate)
    silu = gate * sigmoid
    active = (silu * up).astype(BF)
    grad_gate = (pull * up * sigmoid * (1.0 + gate * (1.0 - sigmoid))).astype(BF)
    grad_up = (pull * silu).astype(BF)
    for c in range(columns):
        rows = slice(c * part, (c + 1) * part)
        forward[rows] += dot_tn(w_down[c], active)
        gw_down[c] = dot_nt(active, grad_ffn[rows]).astype(BF)
    backward[...] += dot_nn(w_gate[0], grad_gate) + dot_nn(w_up[0], grad_up)
    gw_gate[0] = dot_nt(tokens, grad_gate).astype(BF)
    gw_up[0] = dot_nt(tokens, grad_up).astype(BF)

    @pl.when(step == pl.num_programs(0) - 1)
    def _():
        share = prob[...]
        both = branch[...] + forward[...]
        delta_out[...] = (share * both).astype(BF)
        cot_full = cot[...].astype(F32)
        slope = share * (1.0 - share) * jnp.sum(cot_full * both, axis=0, keepdims=True)
        logit_out[...] = slope
        token = picked[...].astype(F32)
        router_out[...] = jnp.sum(slope * token, axis=1, keepdims=True)
        hidden = token + branch[...]
        inv = inverse[...]
        grad_norm = backward[...]
        gain_out[...] = jnp.sum(grad_norm * hidden * inv, axis=1, keepdims=True)
        unit = grad_norm * gain[...]
        along = jnp.sum(unit * hidden, axis=0, keepdims=True) / width
        grad_hidden = inv * unit - hidden * (inv * inv * inv * along)
        grad_attn[...] = (grad_hidden + share * cot_full).astype(BF)
        rest_out[...] = (grad_hidden + slope * router[...]).astype(BF)


def ffn(normed, grad_ffn, branch, picked, cot, prob, inverse, gain, router, w_gate, w_up, w_down):
    width, picks = normed.shape
    blocks, _, hidden = w_gate.shape
    columns, _, part = w_down.shape
    tall = pl.BlockSpec((1, width, hidden), lambda i: (i, 0, 0))
    flat = pl.BlockSpec((columns, hidden, part), lambda i: (0, i, 0))
    full = whole((width, picks))
    row = whole((1, picks))
    column = whole((width, 1))
    return pl.pallas_call(
        ffn_body,
        grid=(blocks,),
        in_specs=[full, full, full, full, full, row, row, column, column, tall, tall, flat],
        out_specs=[full, full, full, row, column, column, tall, tall, flat],
        out_shape=[
            struct((width, picks), BF),
            struct((width, picks), BF),
            struct((width, picks), BF),
            struct((1, picks), F32),
            struct((width, 1), F32),
            struct((width, 1), F32),
            struct(w_gate.shape, BF),
            struct(w_up.shape, BF),
            struct(w_down.shape, BF),
        ],
        scratch_shapes=[pltpu.VMEM((width, picks), F32), pltpu.VMEM((width, picks), F32)],
        compiler_params=params(60),
        cost_estimate=cost(
            18 * width * w_gate.size // width * picks, 12 * w_gate.size + 20 * width * picks
        ),
        name="ffn",
    )(normed, grad_ffn, branch, picked, cot, prob, inverse, gain, router, w_gate, w_up, w_down)


def merge_back_body(mixed, grad, w, gw, grad_mixed, total):
    step = pl.program_id(0)
    part = w.shape[2]
    rows = pl.ds(pl.multiple_of(step * part, 8), part)
    piece = grad[rows, :]
    gw[0] = dot_nt(mixed[...], piece).astype(BF)
    value = dot_nn(w[0], piece)

    @pl.when(step == 0)
    def _():
        total[...] = value

    @pl.when(step > 0)
    def _():
        total[...] += value

    @pl.when(step == pl.num_programs(0) - 1)
    def _():
        grad_mixed[...] = total[...].astype(BF)


def merge_back(mixed, grad, w):
    width, picks = mixed.shape
    blocks, _, part = w.shape
    block = pl.BlockSpec((1, width, part), lambda i: (i, 0, 0))
    return pl.pallas_call(
        merge_back_body,
        grid=(blocks,),
        in_specs=[whole((width, picks)), whole((width, picks)), block],
        out_specs=[block, whole((width, picks))],
        out_shape=[struct(w.shape, BF), struct((width, picks), BF)],
        scratch_shapes=[pltpu.VMEM((width, picks), F32)],
        compiler_params=params(),
        cost_estimate=cost(4 * width * width * picks, 6 * width * picks + 4 * w.size),
        name="merge_back",
    )(mixed, grad, w)


def project_back_body(
    x, rank, gain, gq, gk, gv, rest, w,
    gw, out, gain_out,
    normed, gq_full, total,
):
    step = pl.program_id(0)
    width = x.shape[0]
    count = w_count(w, width)
    q_part = width // count
    kv_part = (w.shape[2] - q_part) // 2

    def inverse():
        full = x[...].astype(F32)
        return lax.rsqrt(jnp.sum(full * full, axis=0, keepdims=True) / width + EPSILON)

    @pl.when(step == 0)
    def _():
        normed[...] = (x[...].astype(F32) * inverse() * gain[...]).astype(BF)
        chosen = pick_rows(rank[...], gq.shape[1])
        gq_full[...] = dot_nn(gq[...], chosen).astype(BF)
        total[...] = jnp.zeros_like(total)

    q_rows = pl.ds(pl.multiple_of(step * q_part, 8), q_part)
    kv_rows = pl.ds(pl.multiple_of(step * kv_part, 8), kv_part)
    grads = jnp.concatenate([gq_full[q_rows, :], gk[kv_rows, :], gv[kv_rows, :]], axis=0)
    total[...] += dot_nn(w[0], grads)
    gw[0] = dot_nt(normed[...], grads).astype(BF)

    @pl.when(step == pl.num_programs(0) - 1)
    def _():
        full = x[...].astype(F32)
        inv = inverse()
        grad_norm = total[...]
        gain_out[...] = jnp.sum(grad_norm * full * inv, axis=1, keepdims=True)
        unit = grad_norm * gain[...]
        along = jnp.sum(unit * full, axis=0, keepdims=True) / width
        chosen = pick_rows(rank[...], gq.shape[1])
        out[...] = (
            inv * unit - full * (inv * inv * inv * along) + dot_nn(rest[...], chosen)
        ).astype(BF)


def project_back(x, rank_row, gain, gq, gk, gv, rest, w):
    width, length = x.shape
    picks = gq.shape[1]
    blocks, _, part = w.shape
    kv = KVH * HD
    block = pl.BlockSpec((1, width, part), lambda i: (i, 0, 0))
    return pl.pallas_call(
        project_back_body,
        grid=(blocks,),
        in_specs=[
            whole((width, length)),
            whole((1, length)),
            whole((width, 1)),
            whole((width, picks)),
            whole((kv, length)),
            whole((kv, length)),
            whole((width, picks)),
            block,
        ],
        out_specs=[block, whole((width, length)), whole((width, 1))],
        out_shape=[
            struct(w.shape, BF),
            struct((width, length), BF),
            struct((width, 1), F32),
        ],
        scratch_shapes=[
            pltpu.VMEM((width, length), BF),
            pltpu.VMEM((width, length), BF),
            pltpu.VMEM((width, length), F32),
        ],
        compiler_params=params(),
        cost_estimate=cost(
            4 * width * length * (picks + width + 2 * kv), 10 * x.size + 4 * w.size
        ),
        name="project_back",
    )(x, rank_row, gain, gq, gk, gv, rest, w)


def rope_tables(positions):
    half = HD // 2
    frequency = jnp.exp(jnp.arange(half, dtype=F32) * (-2.0 * math.log(ROPE_BASE) / HD))
    angles = frequency[:, None] * positions.astype(F32)[None, :]
    return jnp.cos(angles), jnp.sin(angles)


def sequence_step(x, cot, rank, prefix_len, gain_one, gain_two, router, w_qkv, w_out, w_gate, w_up, w_down):
    width, length = x.shape
    picks = cot.shape[1]
    place = jnp.arange(picks, dtype=jnp.int32)
    every = jnp.arange(length, dtype=jnp.int32)
    spot = jnp.sum(jnp.where(rank[None, :] == place[:, None], every[None, :], 0), axis=1)
    limit = jnp.maximum(spot, prefix_len - 1)[None, :]
    tables_k = rope_tables(every)
    tables_q = rope_tables(spot)
    gain_one, gain_two, router = gain_one[:, None], gain_two[:, None], router[:, None]
    picked, prob, q, kt, k, vt, v = project(
        x, rank[:, None], gain_one, router, tables_k, tables_q, w_qkv
    )
    mixed, total = attend(q, k, vt, limit)
    branch, inverse, normed, grad_ffn = merge(mixed, picked, cot, prob, gain_two, w_out)
    delta, grad_attn, rest, _, gain_two_grad, router_grad, gw_gate, gw_up, gw_down = ffn(
        normed, grad_ffn, branch, picked, cot, prob, inverse, gain_two, router, w_gate, w_up, w_down
    )
    gw_out, grad_mixed = merge_back(mixed, grad_attn, w_out)
    gq, gk, gv = attend_back(q, k, kt, v, limit, total, grad_mixed, mixed, tables_k, tables_q)
    gw_qkv, back, gain_one_grad = project_back(
        x, rank[None, :], gain_one, gq, gk, gv, rest, w_qkv
    )
    vectors = jnp.concatenate([gain_one_grad, gain_two_grad, router_grad], axis=1)
    return delta, back, vectors, (gw_qkv, gw_out, gw_gate, gw_up, gw_down)


def bits_of(count):
    return count.bit_length() - 1


def swap(value, axis, bit):
    count = lax.axis_size(axis)
    return lax.ppermute(value, axis, [(i, i ^ (1 << bit)) for i in range(count)])


def own_bit(axis, bit):
    return (lax.axis_index(axis) >> bit) & 1


def join_bit(value, axis, bit, at):
    other = swap(value, axis, bit)
    mine = own_bit(axis, bit) == 0
    return jnp.stack([jnp.where(mine, value, other), jnp.where(mine, other, value)], axis=at)


def route(flip):
    bits = list(range(1, bits_of(lax.axis_size("row"))))
    return bits if flip else bits[::-1]


def gather_weight(value, flip):
    col_bits = bits_of(lax.axis_size("col"))
    row_bits = bits_of(lax.axis_size("row"))
    rows, cols = value.shape
    for done, bit in enumerate(range(col_bits)[::-1]):
        value = join_bit(value, "col", bit, done)
    taken = []
    for bit in route(flip) + [0]:
        at = col_bits + sum(1 for other in taken if other > bit)
        value = join_bit(value, "row", bit, at)
        taken.append(bit)
    return value.reshape(1 << col_bits, rows << row_bits, cols)


def halve_bit(value, axis, bit, at):
    mine = own_bit(axis, bit)
    keep = lax.dynamic_index_in_dim(value, mine, at, keepdims=False)
    send = lax.dynamic_index_in_dim(value, 1 - mine, at, keepdims=False)
    other = swap(send, axis, bit)
    return (keep.astype(F32) + other.astype(F32)).astype(BF)


def scatter_weight(value, flip):
    col_bits = bits_of(lax.axis_size("col"))
    row_bits = bits_of(lax.axis_size("row"))
    columns, rows, cols = value.shape
    value = value.reshape((2,) * (col_bits + row_bits) + (rows >> row_bits, cols))
    left = list(range(row_bits))[::-1]
    for bit in [0] + route(flip)[::-1]:
        value = halve_bit(value, "row", bit, col_bits + left.index(bit))
        left.remove(bit)
    for done, bit in enumerate(range(col_bits)):
        value = halve_bit(value, "col", bit, col_bits - 1 - done)
    return value.astype(F32)


def to_owner(value):
    count = lax.axis_size("col")
    copies = count // value.shape[0]
    if copies > 1:
        value = jnp.concatenate([value] * copies, axis=0)
    moved = lax.all_to_all(value, "col", split_axis=0, concat_axis=1, tiled=True)
    return moved[0]


def from_owner(value, sequences):
    count = lax.axis_size("col")
    value = value.reshape(count, value.shape[0] // count, value.shape[1])
    moved = lax.all_to_all(value, "col", split_axis=0, concat_axis=0, tiled=True)
    return moved[:sequences]


def on_device(
    resid, cotangent, prefix, slot, chosen, norm1_gain, norm2_gain, router,
    w_query, w_key, w_value, w_out, w_gate, w_up, w_down,
):
    col_count = lax.axis_size("col")
    column = lax.axis_index("col")
    sequences, part, length = resid.shape
    picks = chosen.shape[2]
    copies = col_count // sequences
    own = lax.rem(column, sequences)

    x = to_owner(resid.astype(BF))
    w_qkv = gather_weight(jnp.concatenate([w_query, w_key, w_value], axis=1), False)
    w_out_all = gather_weight(w_out, True)
    w_gate_all = gather_weight(w_gate, False)
    w_up_all = gather_weight(w_up, True)
    w_down_all = gather_weight(w_down, False)

    every = jnp.arange(length, dtype=jnp.int32)
    chosen_of = chosen[:, 0][slot]
    selected = jnp.any(every[None, :, None] == chosen_of[:, None, :], axis=2)
    before = (every[:, None] < every[None, :]).astype(BF)
    places = jnp.dot(selected.astype(BF), before, preferred_element_type=F32)
    rank = jnp.where(selected, places.astype(jnp.int32), -1)

    cot = to_owner(gather_tokens(cotangent, rank[:, :, None], picks))

    delta, back, vectors, grads = sequence_step(
        x, cot,
        lax.dynamic_index_in_dim(rank, own, 0, keepdims=False),
        lax.dynamic_index_in_dim(prefix, own, 0, keepdims=False),
        norm1_gain, norm2_gain, router,
        w_qkv, w_out_all, w_gate_all, w_up_all, w_down_all,
    )
    if copies > 1:
        vectors = vectors / copies
        grads = tuple((g.astype(F32) / copies).astype(BF) for g in grads)
    gw_qkv, gw_out, gw_gate, gw_up, gw_down = grads

    block_out = scatter_tokens(resid, from_owner(delta, sequences), rank[:, None, :])
    gw_gate = scatter_weight(gw_gate, False)
    gw_up = scatter_weight(gw_up, True)
    gw_down = scatter_weight(gw_down, False)
    gw_out = scatter_weight(gw_out, True)
    resid_grad = cotangent + from_owner(back, sequences).astype(F32)
    gw_qkv = scatter_weight(gw_qkv, False)
    vectors = lax.psum(vectors.T, ("row", "col"))
    vectors = lax.dynamic_slice_in_dim(vectors, column * part, part, 1)
    kv_part = w_key.shape[1]
    return (
        block_out, resid_grad, vectors[0], vectors[1], vectors[2],
        gw_qkv[:, :part], gw_qkv[:, part : part + kv_part], gw_qkv[:, part + kv_part :],
        gw_out, gw_gate, gw_up, gw_down,
    )


def solution(mesh):
    block = P("row", "col")
    placed = (
        P("row", "col", None), P("row", "col", None), P("row"), P("row"), P(None, "row", None),
        P(), P(), P(),
        block, block, block, block, block, block, block,
    )
    given = (
        P("row", "col", None), P("row", "col", None), P("col"), P("col"), P("col"),
        block, block, block, block, block, block, block,
    )
    return jax.shard_map(
        on_device, mesh=mesh, in_specs=placed, out_specs=given, check_vma=False
    )
```

```python
import functools
import math

import jax
import jax.numpy as jnp
from jax import lax
from jax.experimental import pallas as pl
from jax.experimental.pallas import tpu as pltpu
from jax.sharding import PartitionSpec as P

H = 15
KVH = 5
HD = 64
GROUP = H // KVH
QBLOCK = 256

EPSILON = 1e-05
ROPE_BASE = 10000.0
NEG = -1e30
VECTOR_ROWS = 8

BF = jnp.bfloat16
F32 = jnp.float32
MIB = 1 << 20


def dot_nn(a, b):
    return lax.dot_general(a, b, (((1,), (0,)), ((), ())), preferred_element_type=F32)


def dot_tn(a, b):
    return lax.dot_general(a, b, (((0,), (0,)), ((), ())), preferred_element_type=F32)


def dot_nt(a, b):
    return lax.dot_general(a, b, (((1,), (1,)), ((), ())), preferred_element_type=F32)


def params(limit=56):
    return pltpu.CompilerParams(
        dimension_semantics=("arbitrary",), vmem_limit_bytes=limit * MIB
    )


def cost(flops, nbytes, exps=0):
    return pl.CostEstimate(
        flops=int(flops) // 32,
        bytes_accessed=int(nbytes) // 32,
        transcendentals=int(exps) // 32,
    )


def struct(shape, dtype):
    return jax.ShapeDtypeStruct(shape, dtype)


def whole(shape):
    return pl.BlockSpec(shape, lambda i, *_: (0,) * len(shape))


def pick_columns(rank_column, picks):
    place = lax.broadcasted_iota(jnp.int32, (rank_column.shape[0], picks), 1)
    return jnp.where(rank_column == place, 1.0, 0.0).astype(BF)


def pick_rows(rank_row, picks):
    place = lax.broadcasted_iota(jnp.int32, (picks, rank_row.shape[1]), 0)
    return jnp.where(rank_row == place, 1.0, 0.0).astype(BF)


def turn(first, second, cosine, sine, direction):
    signed = sine * direction
    return first * cosine - second * signed, second * cosine + first * signed


def gather_body(values, rank, out):
    chosen = pick_columns(rank[0], out.shape[2])
    out[0] = dot_nn(values[0].astype(BF), chosen).astype(BF)


def gather_tokens(values, rank_column, picks):
    count, width, length = values.shape
    return pl.pallas_call(
        gather_body,
        grid=(count,),
        in_specs=[
            pl.BlockSpec((1, width, length), lambda i: (i, 0, 0)),
            pl.BlockSpec((1, length, 1), lambda i: (i, 0, 0)),
        ],
        out_specs=pl.BlockSpec((1, width, picks), lambda i: (i, 0, 0)),
        out_shape=struct((count, width, picks), BF),
        compiler_params=params(),
        cost_estimate=cost(2 * count * width * length * picks, 6 * values.size),
        name="gather_tokens",
    )(values, rank_column)


def scatter_body(base, values, rank, out):
    chosen = pick_rows(rank[0], values.shape[2])
    out[0] = base[0] + dot_nn(values[0], chosen)


def scatter_tokens(base, values, rank_row):
    count, width, length = base.shape
    picks = values.shape[2]
    return pl.pallas_call(
        scatter_body,
        grid=(count,),
        in_specs=[
            pl.BlockSpec((1, width, length), lambda i: (i, 0, 0)),
            pl.BlockSpec((1, width, picks), lambda i: (i, 0, 0)),
            pl.BlockSpec((1, 1, length), lambda i: (i, 0, 0)),
        ],
        out_specs=pl.BlockSpec((1, width, length), lambda i: (i, 0, 0)),
        out_shape=struct(base.shape, F32),
        compiler_params=params(),
        cost_estimate=cost(2 * count * width * length * picks, 10 * base.size),
        name="scatter_tokens",
    )(base, values, rank_row)


def project_body(who, x, rank, gain, router, cos_k, sin_k, cos_q, sin_q, *refs):
    pieces = refs[:-12]
    (
        picked, prob, q_out, kt_out, k_out, vt_out, v_out, w,
        normed, normed_picked, q_raw, kv_raw,
    ) = refs[-12:]
    step = pl.program_id(0)
    block = step ^ who[0]
    width = x.shape[0]
    q_part = width // pl.num_programs(0)
    kv_part = KVH * HD // pl.num_programs(0)
    if len(pieces) == 1:
        w[0] = pieces[0][0]
    else:
        even = who[2] == 0
        count = len(pieces) // 2
        for k, (own, other) in enumerate(zip(pieces[:count], pieces[count:])):
            first, second = own[0].astype(F32), other[0].astype(F32)
            both = [jnp.where(even, first, second), jnp.where(even, second, first)]
            height = 2 * first.shape[0]
            place = pl.ds(pl.multiple_of((who[1] ^ k) * height, 16), height)
            w[0, place] = jnp.concatenate(both, axis=0).astype(BF)

    @pl.when(step == 0)
    def _():
        full = x[...].astype(F32)
        inverse = lax.rsqrt(jnp.sum(full * full, axis=0, keepdims=True) / width + EPSILON)
        normed[...] = (full * inverse * gain[...]).astype(BF)
        chosen = pick_columns(rank[...], picked.shape[1])
        part = dot_nn(x[...], chosen)
        picked[...] = part.astype(BF)
        inverse = lax.rsqrt(jnp.sum(part * part, axis=0, keepdims=True) / width + EPSILON)
        normed_picked[...] = (part * inverse * gain[...]).astype(BF)
        logit = jnp.sum(part * router[...], axis=0, keepdims=True)
        prob[...] = jax.nn.sigmoid(logit)

    q_raw[pl.ds(pl.multiple_of(block * q_part, 8), q_part)] = dot_tn(
        w[0, :, :q_part], normed_picked[...]
    ).astype(BF)
    kv = dot_tn(w[0, :, q_part : q_part + 2 * kv_part], normed[...]).astype(BF)
    kv_raw[0, pl.ds(pl.multiple_of(block * kv_part, 8), kv_part)] = kv[:kv_part]
    kv_raw[1, pl.ds(pl.multiple_of(block * kv_part, 8), kv_part)] = kv[kv_part:]

    @pl.when(step == pl.num_programs(0) - 1)
    def _():
        half = HD // 2
        for head in range(H):
            at = head * HD
            a, b = turn(
                q_raw[at : at + half].astype(F32),
                q_raw[at + half : at + HD].astype(F32),
                cos_q[...], sin_q[...], 1.0,
            )
            scale = HD ** (-0.5)
            q_out[at : at + half] = (a.astype(BF).astype(F32) * scale).astype(BF)
            q_out[at + half : at + HD] = (b.astype(BF).astype(F32) * scale).astype(BF)
        for head in range(KVH):
            at = head * HD
            a, b = turn(
                kv_raw[0, at : at + half].astype(F32),
                kv_raw[0, at + half : at + HD].astype(F32),
                cos_k[...], sin_k[...], 1.0,
            )
            turned = jnp.concatenate([a, b], axis=0)
            kt_out[at : at + HD] = turned.astype(BF)
            k_out[head] = turned.T.astype(BF)
            value = kv_raw[1, at : at + HD]
            vt_out[at : at + HD] = value
            v_out[head] = value.astype(F32).T.astype(BF)


def project(who, x, rank_column, gain, router, tables_k, tables_q, pieces):
    width, length = x.shape
    picks = tables_q[0].shape[1]
    blocks, height, part = pieces[0].shape
    kv = KVH * HD
    half = HD // 2
    return pl.pallas_call(
        project_body,
        grid_spec=pltpu.PrefetchScalarGridSpec(
        num_scalar_prefetch=1,
        grid=(blocks,),
        in_specs=[
            whole((width, length)),
            whole((length, 1)),
            whole((width, 1)),
            whole((width, 1)),
            whole((half, length)),
            whole((half, length)),
            whole((half, picks)),
            whole((half, picks)),
        ]
        + [pl.BlockSpec((1, height, part), lambda i, who: (i, 0, 0))] * len(pieces),
        out_specs=[
            whole((width, picks)),
            whole((1, picks)),
            whole((width, picks)),
            whole((kv, length)),
            whole((KVH, length, HD)),
            whole((kv, length)),
            whole((KVH, length, HD)),
            pl.BlockSpec((1, width, part), lambda i, who: (i ^ who[0], 0, 0)),
        ],
        scratch_shapes=[
            pltpu.VMEM((width, length), BF),
            pltpu.VMEM((width, picks), BF),
            pltpu.VMEM((width, picks), BF),
            pltpu.VMEM((2, kv, length), BF),
        ],
        ),
        out_shape=[
            struct((width, picks), BF),
            struct((1, picks), F32),
            struct((width, picks), BF),
            struct((kv, length), BF),
            struct((KVH, length, HD), BF),
            struct((kv, length), BF),
            struct((KVH, length, HD), BF),
            struct((blocks, width, part), BF),
        ],
        compiler_params=params(),
        cost_estimate=cost(
            2 * width * (length * picks + picks * width + length * 2 * kv),
            2 * (2 * blocks * width * part + 4 * x.size),
        ),
        name="project",
    )(who, x, rank_column, gain, router, *tables_k, *tables_q, *pieces)


def reach_of(block, length, picks):
    return max((block + 1) * QBLOCK + length - picks, length // 2)


def clear_of(block):
    return block * QBLOCK


def block_scores(q, k, limit, block, reach):
    scores = dot_nn(k[:reach], q)
    clear = clear_of(block)
    tail = scores[clear:] if clear else scores
    key = lax.broadcasted_iota(jnp.int32, tail.shape, 0) + clear
    tail = jnp.where(key <= limit, tail, NEG)
    return jnp.concatenate([scores[:clear], tail], axis=0) if clear else tail


def attend_body(q, k, vt, limit, out, total):
    length = k.shape[1]
    picks = q.shape[1]
    for block in range(picks // QBLOCK):
        at = block * QBLOCK
        reach = reach_of(block, length, picks)
        for head in range(GROUP):
            rows = slice(head * HD, (head + 1) * HD)
            scores = block_scores(
                q[rows, at : at + QBLOCK], k[0], limit[:, at : at + QBLOCK], block, reach
            )
            top = jnp.max(scores, axis=0, keepdims=True)
            weight = jnp.exp(scores - top)
            mass = jnp.sum(weight, axis=0, keepdims=True)
            mixed = dot_nn(vt[:, :reach], weight.astype(BF))
            out[rows, at : at + QBLOCK] = (mixed / mass).astype(BF)
            total[0, head : head + 1, at : at + QBLOCK] = top + jnp.log(mass)


def attend(q, k, vt, limit):
    width, picks = q.shape
    length = k.shape[1]
    part = GROUP * HD
    return pl.pallas_call(
        attend_body,
        grid=(KVH,),
        in_specs=[
            pl.BlockSpec((part, picks), lambda i: (i, 0)),
            pl.BlockSpec((1, length, HD), lambda i: (i, 0, 0)),
            pl.BlockSpec((HD, length), lambda i: (i, 0)),
            whole((1, picks)),
        ],
        out_specs=[
            pl.BlockSpec((part, picks), lambda i: (i, 0)),
            pl.BlockSpec((1, GROUP, picks), lambda i: (i, 0, 0)),
        ],
        out_shape=[struct((width, picks), BF), struct((KVH, GROUP, picks), F32)],
        compiler_params=params(),
        cost_estimate=cost(
            16 * width * length * picks, 4 * width * picks, H * length * picks
        ),
        name="attend",
    )(q, k, vt, limit)


def attend_back_body(
    q, k, kt, v, limit, total, grad, mixed, cos_k, sin_k, cos_q, sin_q,
    gq_out, gk_out, gv_out, gk, gv,
):
    length = k.shape[1]
    picks = q.shape[1]
    half = HD // 2
    gk[...] = jnp.zeros_like(gk)
    gv[...] = jnp.zeros_like(gv)
    for block in range(picks // QBLOCK):
        at = block * QBLOCK
        cols = slice(at, at + QBLOCK)
        reach = reach_of(block, length, picks)
        for head in range(GROUP):
            rows = slice(head * HD, (head + 1) * HD)
            q_part = q[rows, cols]
            g_part = grad[rows, cols]
            scores = block_scores(q_part, k[0], limit[:, cols], block, reach)
            weight = jnp.exp(scores - total[0, head : head + 1, cols])
            delta = jnp.sum(
                g_part.astype(F32) * mixed[rows, cols].astype(F32), axis=0, keepdims=True
            )
            pull = dot_nn(v[0, :reach], g_part)
            back = (weight * (pull - delta)).astype(BF)
            gq = dot_nn(kt[:, :reach], back) * HD ** (-0.5)
            a, b = turn(gq[:half], gq[half:], cos_q[:, cols], sin_q[:, cols], -1.0)
            gq_out[head * HD : head * HD + half, cols] = a.astype(BF)
            gq_out[head * HD + half : (head + 1) * HD, cols] = b.astype(BF)
            gk[:reach] += dot_nt(back, q_part)
            gv[:reach] += dot_nt(weight.astype(BF), g_part)
    turned = gk[...].T
    a, b = turn(turned[:half], turned[half:], cos_k[...], sin_k[...], -1.0)
    gk_out[:half] = a.astype(BF)
    gk_out[half:] = b.astype(BF)
    gv_out[...] = gv[...].T.astype(BF)


def attend_back(q, k, kt, v, limit, total, grad, mixed, tables_k, tables_q):
    width, picks = q.shape
    length = k.shape[1]
    part = GROUP * HD
    half = HD // 2
    wide = pl.BlockSpec((part, picks), lambda i: (i, 0))
    tall = pl.BlockSpec((1, length, HD), lambda i: (i, 0, 0))
    flat = pl.BlockSpec((HD, length), lambda i: (i, 0))
    return pl.pallas_call(
        attend_back_body,
        grid=(KVH,),
        in_specs=[
            wide, tall, flat, tall, whole((1, picks)),
            pl.BlockSpec((1, GROUP, picks), lambda i: (i, 0, 0)),
            wide, wide,
            whole((half, length)), whole((half, length)),
            whole((half, picks)), whole((half, picks)),
        ],
        out_specs=[wide, flat, flat],
        out_shape=[
            struct((width, picks), BF),
            struct((KVH * HD, length), BF),
            struct((KVH * HD, length), BF),
        ],
        scratch_shapes=[pltpu.VMEM((length, HD), F32), pltpu.VMEM((length, HD), F32)],
        compiler_params=params(),
        cost_estimate=cost(
            40 * width * length * picks, 8 * width * picks, H * length * picks
        ),
        name="attend_back",
    )(q, k, kt, v, limit, total, grad, mixed, *tables_k, *tables_q)


def merge_body(mixed, picked, gain, w, branch, inverse_out, normed, hidden, square):
    step = pl.program_id(0)
    width = mixed.shape[0]
    part = width // pl.num_programs(0)
    rows = pl.ds(pl.multiple_of(step * part, 8), part)

    @pl.when(step == 0)
    def _():
        square[...] = jnp.zeros_like(square)

    value = dot_tn(w[0, :, w.shape[2] - part :], mixed[...])
    branch[...] = value
    total = picked[rows, :].astype(F32) + value
    hidden[rows, :] = total
    square[...] += jnp.sum(total * total, axis=0, keepdims=True)

    @pl.when(step == pl.num_programs(0) - 1)
    def _():
        inverse = lax.rsqrt(square[...] / width + EPSILON)
        inverse_out[...] = inverse
        normed[...] = (hidden[...] * inverse * gain[...]).astype(BF)


def merge(mixed, picked, gain, w):
    width, picks = mixed.shape
    blocks, _, wide = w.shape
    part = width // blocks
    return pl.pallas_call(
        merge_body,
        grid=(blocks,),
        in_specs=[
            whole((width, picks)),
            whole((width, picks)),
            whole((width, 1)),
            pl.BlockSpec((1, width, wide), lambda i: (i, 0, 0)),
        ],
        out_specs=[
            pl.BlockSpec((part, picks), lambda i: (i, 0)),
            whole((1, picks)),
            whole((width, picks)),
        ],
        out_shape=[
            struct((width, picks), F32),
            struct((1, picks), F32),
            struct((width, picks), BF),
        ],
        scratch_shapes=[pltpu.VMEM((width, picks), F32), pltpu.VMEM((1, picks), F32)],
        compiler_params=params(),
        cost_estimate=cost(2 * width * width * picks, 14 * width * picks + 2 * w.size),
        name="merge",
    )(mixed, picked, gain, w)


def down_half(part):
    return -(-part // 32) * 16


def ffn_weights(who, first, sources, w_gate, w_up, w_down, done):
    step, steps = pl.program_id(0), pl.num_programs(0)
    slot = lax.rem(step, 2)
    width = w_gate.shape[1]

    def copies(step, at):
        block = (step + first) ^ who[0]
        if len(sources) == 2:
            some = [
                (sources[0].at[0, block], w_gate.at[at]),
                (sources[0].at[1, block], w_up.at[at]),
                (sources[1].at[block], w_down.at[at]),
            ]
        else:
            (source,) = sources
            pairs, _, columns, _, _ = source.shape
            height, part = width // pairs, width // columns
            half = down_half(part)
            some = []
            for i in range(pairs):
                place = slice(i * height, (i + 1) * height)
                some.append((source.at[i, 0, block, :height], w_gate.at[at, place]))
                some.append((source.at[i, 1, block, :height], w_up.at[at, place]))
            for c in range(columns):
                top = slice(c * part, c * part + half)
                some.append((source.at[block, 0, c, height : height + half], w_down.at[at, top]))
                end = slice(c * part + half, (c + 1) * part)
                rest = slice(height + 2 * half - part, height + half)
                some.append((source.at[block, 1, c, rest], w_down.at[at, end]))
        return [
            pltpu.make_async_copy(source, target, done.at[at, i])
            for i, (source, target) in enumerate(some)
        ]

    @pl.when(step == 0)
    def _():
        for copy in copies(step, slot):
            copy.start()

    @pl.when(step + 1 < steps)
    def _():
        for copy in copies(step + 1, 1 - slot):
            copy.start()

    for copy in copies(step, slot):
        copy.wait()
    return slot


def ffn_scratch(width, sources):
    hidden = sources[0].shape[-1]
    count = 3
    if len(sources) == 1:
        count = 2 * (sources[0].shape[0] + sources[0].shape[2])
    return [pltpu.VMEM((2, width, hidden), BF)] * 3 + [pltpu.SemaphoreType.DMA((2, count))]


def ffn_body(many, who, normed, branch, prob, *refs):
    sources, refs = refs[:many], refs[many:]
    gate_out, up_out, active_out, delta, both_out, forward, *buffers = refs
    w_gate, w_up, w_down, _ = buffers
    slot = ffn_weights(who, 0, sources, *buffers)

    @pl.when(pl.program_id(0) == 0)
    def _():
        forward[...] = branch[...]

    tokens = normed[...]
    gate = dot_tn(w_gate[slot], tokens)
    up = dot_tn(w_up[slot], tokens)
    active = (gate * jax.nn.sigmoid(gate) * up).astype(BF)
    gate_out[0] = gate.astype(BF)
    up_out[0] = up.astype(BF)
    active_out[0] = active
    forward[...] += dot_nn(w_down[slot], active)

    @pl.when(pl.program_id(0) == pl.num_programs(0) - 1)
    def _():
        both = forward[...]
        delta[...] = (prob[...] * both).astype(BF)
        both_out[...] = both.astype(BF)


def ffn(who, normed, branch, prob, blocks, hidden, sources):
    width, picks = normed.shape
    full, row = whole((width, picks)), whole((1, picks))
    far = pl.BlockSpec(memory_space=pl.ANY)
    kept = pl.BlockSpec((1, hidden, picks), lambda i, who: (i, 0, 0))
    kept_shape = struct((blocks, hidden, picks), BF)
    low = struct((width, picks), BF)
    return pl.pallas_call(
        functools.partial(ffn_body, len(sources)),
        grid_spec=pltpu.PrefetchScalarGridSpec(
            num_scalar_prefetch=1,
            grid=(blocks,),
            in_specs=[full, full, row] + [far] * len(sources),
            out_specs=[kept] * 3 + [full, full],
            scratch_shapes=[pltpu.VMEM((width, picks), F32)] + ffn_scratch(width, sources),
        ),
        out_shape=[kept_shape] * 3 + [low, low],
        compiler_params=params(60),
        cost_estimate=cost(
            6 * width * hidden * blocks * picks, 6 * width * hidden * blocks + 8 * width * picks
        ),
        name="ffn",
    )(who, normed, branch, prob, *sources)


def down_grad_body(who, grad_ffn, active, keep, send):
    here, columns, half, lanes = keep.shape
    part = grad_ffn.shape[0] // columns
    even = who[2] == 0
    for c in range(columns):
        value = dot_nt(grad_ffn[c * part : (c + 1) * part], active[0])
        low, high = value[:half].astype(BF), value[part - half :].astype(BF)
        mine, other = jnp.where(even, low, high), jnp.where(even, high, low)
        for i in range(here):
            at = i ^ lax.rem(who[1], here) if here > 1 else 0
            keep[at, c ^ who[0]] = mine[:, i * lanes : (i + 1) * lanes]
            send[at, c ^ who[0]] = other[:, i * lanes : (i + 1) * lanes]


def down_grad(who, grad_ffn, active, pairs, columns):
    width, picks = grad_ffn.shape
    blocks, hidden, _ = active.shape
    here = pairs // blocks
    tile = (columns, down_half(width // columns), hidden // here)
    block = pl.BlockSpec(
        (here,) + tile, lambda i, who: (i ^ who[0] ^ lax.div(who[1], here), 0, 0, 0)
    )
    return pl.pallas_call(
        down_grad_body,
        grid_spec=pltpu.PrefetchScalarGridSpec(
            num_scalar_prefetch=1,
            grid=(blocks,),
            in_specs=[
                whole((width, picks)),
                pl.BlockSpec((1, hidden, picks), lambda i, who: (i, 0, 0)),
            ],
            out_specs=[block, block],
        ),
        out_shape=[struct((pairs,) + tile, BF)] * 2,
        compiler_params=params(),
        cost_estimate=cost(2 * blocks * hidden * width * picks, 6 * blocks * hidden * width),
        name="down_grad",
    )(who, grad_ffn, active)


def ffn_back_body(first, last, many, who, normed, grad_ffn, gate_in, up_in, *refs):
    sources, refs = refs[:many], refs[many:]
    if first:
        carried, refs = refs[0], refs[1:]
    if last:
        (branch, both_in, picked, cot, prob, inverse, gain, router), refs = refs[:8], refs[8:]
    keep_pair, send_pair, refs = refs[0], refs[1], refs[2:]
    outs, backward, buffers = refs[:-5], refs[-5], refs[-4:]
    w_gate, w_up, w_down, _ = buffers
    slot = ffn_weights(who, first, sources, *buffers)
    width = normed.shape[0]
    even = who[2] == 0

    @pl.when(pl.program_id(0) == 0)
    def _():
        backward[...] = carried[...] if first else jnp.zeros_like(backward)

    pull = dot_tn(w_down[slot], grad_ffn[...])
    gate = gate_in[0].astype(F32)
    sigmoid = jax.nn.sigmoid(gate)
    silu = gate * sigmoid
    grad_gate = (pull * up_in[0].astype(F32) * (sigmoid + silu * (1.0 - sigmoid))).astype(BF)
    grad_up = (pull * silu).astype(BF)
    backward[...] += dot_nn(w_gate[slot], grad_gate) + dot_nn(w_up[slot], grad_up)
    tokens = normed[...]
    for_gate = dot_nt(tokens, grad_gate).astype(BF)
    for_up = dot_nt(tokens, grad_up).astype(BF)
    pieces, _, height, _ = keep_pair.shape
    for i in range(pieces):
        place = slice(i * height, (i + 1) * height)
        at = i ^ who[1] if pieces > 1 else 0
        keep_pair[at, 0] = jnp.where(even, for_gate[place], for_up[place])
        send_pair[at, 0] = jnp.where(even, for_up[place], for_gate[place])

    @pl.when(pl.program_id(0) == pl.num_programs(0) - 1)
    def _():
        if not last:
            outs[0][...] = backward[...]
            return
        grad_attn, rest_out, gain_out, router_out = outs
        share = prob[...]
        cot_full = cot[...].astype(F32)
        slope = share * (1.0 - share) * jnp.sum(
            cot_full * both_in[...].astype(F32), axis=0, keepdims=True
        )
        token = picked[...].astype(F32)
        router_out[...] = jnp.sum(slope * token, axis=1, keepdims=True)
        hidden = token + branch[...]
        inv = inverse[...]
        grad_norm = backward[...]
        gain_out[...] = jnp.sum(grad_norm * hidden * inv, axis=1, keepdims=True)
        unit = grad_norm * gain[...]
        along = jnp.sum(unit * hidden, axis=0, keepdims=True) / width
        grad_hidden = inv * unit - hidden * (inv * inv * inv * along)
        grad_attn[...] = (grad_hidden + share * cot_full).astype(BF)
        rest_out[...] = (grad_hidden + slope * router[...]).astype(BF)


def ffn_back(who, first, count, last, pieces, normed, grad_ffn, gate, up, sources, carried, tail):
    width, picks = normed.shape
    hidden = gate.shape[1]
    height = width // pieces
    full, row, column = whole((width, picks)), whole((1, picks)), whole((width, 1))
    far = pl.BlockSpec(memory_space=pl.ANY)
    kept = pl.BlockSpec((1, hidden, picks), lambda i, who: (i + first, 0, 0))
    tall = pl.BlockSpec((pieces, 1, height, hidden), lambda i, who: (0, i, 0, 0))
    tall_shape = struct((pieces, count, height, hidden), BF)
    low, thin = struct((width, picks), BF), struct((width, 1), F32)
    extra = ([carried] if first else []) + (list(tail) if last else [])
    extra_specs = ([full] if first else []) + ([full] * 4 + [row] * 2 + [column] * 2 if last else [])
    return pl.pallas_call(
        functools.partial(ffn_back_body, first, last, len(sources)),
        grid_spec=pltpu.PrefetchScalarGridSpec(
            num_scalar_prefetch=1,
            grid=(count,),
            in_specs=[full, full, kept, kept] + [far] * len(sources) + extra_specs,
            out_specs=[tall, tall] + ([full, full, column, column] if last else [full]),
            scratch_shapes=[pltpu.VMEM((width, picks), F32)] + ffn_scratch(width, sources),
        ),
        out_shape=[tall_shape, tall_shape]
        + ([low, low, thin, thin] if last else [struct((width, picks), F32)]),
        compiler_params=params(60),
        cost_estimate=cost(
            10 * width * hidden * count * picks, 10 * width * hidden * count + 12 * width * picks
        ),
        name="ffn_back",
    )(who, normed, grad_ffn, gate, up, *sources, *extra)


def merge_back_body(mixed, grad, w, gw, grad_mixed, total):
    step = pl.program_id(0)
    part = gw.shape[2]
    rows = pl.ds(pl.multiple_of(step * part, 8), part)
    piece = grad[rows, :]
    gw[0] = dot_nt(mixed[...], piece).astype(BF)
    value = dot_nn(w[0, :, w.shape[2] - part :], piece)

    @pl.when(step == 0)
    def _():
        total[...] = value

    @pl.when(step > 0)
    def _():
        total[...] += value

    @pl.when(step == pl.num_programs(0) - 1)
    def _():
        grad_mixed[...] = total[...].astype(BF)


def merge_back(mixed, grad, w):
    width, picks = mixed.shape
    blocks, _, wide = w.shape
    part = width // blocks
    block = pl.BlockSpec((1, width, part), lambda i: (i, 0, 0))
    wide_block = pl.BlockSpec((1, width, wide), lambda i: (i, 0, 0))
    return pl.pallas_call(
        merge_back_body,
        grid=(blocks,),
        in_specs=[whole((width, picks)), whole((width, picks)), wide_block],
        out_specs=[block, whole((width, picks))],
        out_shape=[struct((blocks, width, part), BF), struct((width, picks), BF)],
        scratch_shapes=[pltpu.VMEM((width, picks), F32)],
        compiler_params=params(),
        cost_estimate=cost(4 * width * width * picks, 6 * width * picks + 4 * w.size),
        name="merge_back",
    )(mixed, grad, w)


def mixing_grad_body(
    who, x, rank, gain, gq, gk, gv, gw_out,
    keep, send, grads_out,
    normed, gq_full,
):
    step = pl.program_id(0)
    width = x.shape[0]
    q_part = width // pl.num_programs(0)
    kv_part = KVH * HD // pl.num_programs(0)
    even = who[2] == 0

    @pl.when(step == 0)
    def _():
        full = x[...].astype(F32)
        inverse = lax.rsqrt(jnp.sum(full * full, axis=0, keepdims=True) / width + EPSILON)
        normed[...] = (full * inverse * gain[...]).astype(BF)
        gq_full[...] = dot_nn(gq[...], pick_rows(rank[...], gq.shape[1])).astype(BF)

    q_rows = pl.ds(pl.multiple_of(step * q_part, 8), q_part)
    kv_rows = pl.ds(pl.multiple_of(step * kv_part, 8), kv_part)
    grads = jnp.concatenate([gq_full[q_rows, :], gk[kv_rows, :], gv[kv_rows, :]], axis=0)
    grads_out[0] = grads
    value = dot_nt(normed[...], grads)
    value = jnp.concatenate([value, gw_out[0].astype(F32)], axis=1)
    pairs = keep.shape[0]
    rows = width // (2 * pairs)
    for pair in range(pairs):
        low = value[2 * pair * rows : (2 * pair + 1) * rows]
        high = value[(2 * pair + 1) * rows : (2 * pair + 2) * rows]
        keep[pair ^ who[1], 0, :rows] = jnp.where(even, low, high).astype(BF)
        send[pair ^ who[1], 0, :rows] = jnp.where(even, high, low).astype(BF)


def mixing_grad(who, x, rank_row, gain, gq, gk, gv, gw_out, pairs):
    width, length = x.shape
    picks = gq.shape[1]
    blocks, _, out_part = gw_out.shape
    kv = KVH * HD
    part = (width + 2 * kv) // blocks
    rows = width // (2 * pairs) + VECTOR_ROWS
    split = pl.BlockSpec((pairs, 1, rows, part + out_part), lambda i, who: (0, i ^ who[0], 0, 0))
    split_shape = struct((pairs, blocks, rows, part + out_part), BF)
    return pl.pallas_call(
        mixing_grad_body,
        grid_spec=pltpu.PrefetchScalarGridSpec(
            num_scalar_prefetch=1,
            grid=(blocks,),
            in_specs=[
                whole((width, length)),
                whole((1, length)),
                whole((width, 1)),
                whole((width, picks)),
                whole((kv, length)),
                whole((kv, length)),
                pl.BlockSpec((1, width, out_part), lambda i, who: (i, 0, 0)),
            ],
            out_specs=[split, split, pl.BlockSpec((1, part, length), lambda i, who: (i, 0, 0))],
            scratch_shapes=[pltpu.VMEM((width, length), BF), pltpu.VMEM((width, length), BF)],
        ),
        out_shape=[split_shape, split_shape, struct((blocks, part, length), BF)],
        compiler_params=params(),
        cost_estimate=cost(2 * width * length * (picks + width + 2 * kv), 10 * x.size),
        name="mixing_grad",
    )(who, x, rank_row, gain, gq, gk, gv, gw_out)


def project_back_body(x, rank, gain, grads, rest, w, out, gain_out, total):
    step = pl.program_id(0)
    width = x.shape[0]
    part = grads.shape[1]

    @pl.when(step == 0)
    def _():
        total[...] = jnp.zeros_like(total)

    total[...] += dot_nn(w[0, :, :part], grads[0])

    @pl.when(step == pl.num_programs(0) - 1)
    def _():
        full = x[...].astype(F32)
        inv = lax.rsqrt(jnp.sum(full * full, axis=0, keepdims=True) / width + EPSILON)
        grad_norm = total[...]
        gain_out[...] = jnp.sum(grad_norm * full * inv, axis=1, keepdims=True)
        unit = grad_norm * gain[...]
        along = jnp.sum(unit * full, axis=0, keepdims=True) / width
        chosen = pick_rows(rank[...], rest.shape[1])
        out[...] = (
            inv * unit - full * (inv * inv * inv * along) + dot_nn(rest[...], chosen)
        ).astype(BF)


def project_back(x, rank_row, gain, grads, rest, w):
    width, length = x.shape
    picks = rest.shape[1]
    blocks, part, _ = grads.shape
    return pl.pallas_call(
        project_back_body,
        grid=(blocks,),
        in_specs=[
            whole((width, length)),
            whole((1, length)),
            whole((width, 1)),
            pl.BlockSpec((1, part, length), lambda i: (i, 0, 0)),
            whole((width, picks)),
            pl.BlockSpec((1,) + w.shape[1:], lambda i: (i, 0, 0)),
        ],
        out_specs=[whole((width, length)), whole((width, 1))],
        out_shape=[struct((width, length), BF), struct((width, 1), F32)],
        scratch_shapes=[pltpu.VMEM((width, length), F32)],
        compiler_params=params(),
        cost_estimate=cost(2 * width * length * (picks + blocks * part), 10 * x.size + 2 * w.size),
        name="project_back",
    )(x, rank_row, gain, grads, rest, w)


def hold(*values):
    return lax.optimization_barrier(values)


def swap(value):
    count = lax.axis_size("row")
    return lax.ppermute(value, "row", [(i, i ^ 1) for i in range(count)])


def partner(value, axis, k):
    count = lax.axis_size(axis)
    far = k if axis == "col" else 2 * k
    return lax.ppermute(value, axis, [(i, i ^ far) for i in range(count)])


def collect(value, axis, partners):
    return [partner(value, axis, k) if k else value for k in partners]


def spread(values, axis):
    return [values[0]] + [partner(value, axis, k) for k, value in enumerate(values) if k]


def add_up(values):
    return sum(value.astype(F32) for value in values)


def pair_up(keep, got):
    return [add_up((a, b)).astype(BF) for a, b in zip(keep, got)]


def to_owner(value):
    copies = lax.axis_size("col") // value.shape[0]
    if copies > 1:
        value = jnp.concatenate([value] * copies, axis=0)
    moved = lax.all_to_all(value, "col", split_axis=0, concat_axis=1, tiled=True)
    return moved[0]


def from_owner(value, sequences):
    count = lax.axis_size("col")
    value = value.reshape(count, value.shape[0] // count, value.shape[1])
    moved = lax.all_to_all(value, "col", split_axis=0, concat_axis=0, tiled=True)
    return moved[:sequences]


def rope_tables(positions):
    half = HD // 2
    frequency = jnp.exp(jnp.arange(half, dtype=F32) * (-2.0 * math.log(ROPE_BASE) / HD))
    angles = frequency[:, None] * positions.astype(F32)[None, :]
    return jnp.cos(angles), jnp.sin(angles)


def on_device(
    resid, cotangent, prefix, slot, chosen, norm1_gain, norm2_gain, router,
    w_query, w_key, w_value, w_out, w_gate, w_up, w_down,
):
    col_count, row_count = lax.axis_size("col"), lax.axis_size("row")
    column = lax.axis_index("col")
    sequences, part, length = resid.shape
    width = part * col_count
    picks = chosen.shape[2]
    copies = col_count // sequences
    own = lax.rem(column, sequences)
    rows, hidden = w_gate.shape
    down_rows = w_down.shape[0]
    pairs = row_count // 2
    mixing_part = part + 2 * w_key.shape[1] + part

    own_pair_index = lax.axis_index("row") >> 1
    core = lax.axis_index("row") & 1
    even = core == 0
    who = jnp.stack([column, own_pair_index, core]).astype(jnp.int32)
    aligned = 2 * rows % 16 == 0

    half = col_count // 2

    mine = jnp.where(even, w_gate, w_up)
    other = swap(jnp.where(even, w_up, w_gate))
    pair = jnp.concatenate([jnp.where(even, mine, other), jnp.where(even, other, mine)], axis=0)
    down_rows_kept = down_half(part)
    turned = w_down.T
    low, high = turned[:down_rows_kept], turned[part - down_rows_kept :]
    mine, other = jnp.where(even, low, high), swap(jnp.where(even, high, low))
    down = jnp.concatenate([jnp.where(even, mine, other), jnp.where(even, other, mine)], axis=1)
    mixing = jnp.concatenate([w_query, w_key, w_value, w_out], axis=1)
    if aligned:
        sources = lax.all_gather(jnp.concatenate([pair, down], axis=0), ("row", "col"), axis=0)
        sources = (sources.reshape((pairs, 2, col_count) + sources.shape[1:]),)
    else:
        pair_all = lax.all_gather(pair, ("row", "col"), axis=0)
        pair_all = pair_all.reshape(pairs, 2, col_count, 2 * rows, hidden).transpose(1, 2, 0, 3, 4)
        down_all = lax.all_gather(down, ("row", "col"), axis=0)
        down_all = down_all.reshape((col_count, pairs // col_count, 2, col_count) + down.shape)
        down_all = jnp.concatenate(
            [down_all[:, :, 0], down_all[:, :, 1, :, 2 * down_rows_kept - part :]], axis=3
        )
        sources = (
            pair_all.reshape(2, col_count, width, hidden),
            down_all.transpose(0, 2, 3, 1, 4).reshape(col_count, width, hidden),
        )
    mixing, x = hold(collect(mixing, "col", range(col_count)), resid.astype(BF))
    mixing = jnp.stack(mixing)

    every = jnp.arange(length, dtype=jnp.int32)
    chosen_of = chosen[:, 0][slot]
    selected = jnp.any(every[None, :, None] == chosen_of[:, None, :], axis=2)
    before = (every[:, None] < every[None, :]).astype(BF)
    places = jnp.dot(selected.astype(BF), before, preferred_element_type=F32)
    ranks = jnp.where(selected, places.astype(jnp.int32), -1)
    rank = lax.dynamic_index_in_dim(ranks, own, 0, keepdims=False)
    prefix_len = lax.dynamic_index_in_dim(prefix, own, 0, keepdims=False)
    place = jnp.arange(picks, dtype=jnp.int32)
    spot = jnp.sum(jnp.where(rank[None, :] == place[:, None], every[None, :], 0), axis=1)
    limit = jnp.maximum(spot, prefix_len - 1)[None, :]
    tables_k = rope_tables(every)
    tables_q = rope_tables(spot)
    gain_one, gain_two, router = norm1_gain[:, None], norm2_gain[:, None], router[:, None]
    cot = gather_tokens(cotangent, ranks[:, :, None], picks)

    x, mixing, cot, limit, tables_k, tables_q = hold(
        to_owner(x), collect(mixing, "row", range(pairs)), cot, limit, tables_k, tables_q
    )
    cot = to_owner(cot)
    mixing_other, mixing = hold([swap(piece) for piece in mixing], mixing)
    if aligned:
        mixing = mixing + mixing_other
    else:
        order = jnp.arange(pairs) ^ own_pair_index
        mixing = jnp.stack([jnp.stack(mixing), jnp.stack(mixing_other)])[jnp.stack([core, 1 - core])]
        mixing = [mixing[:, order].transpose(2, 1, 0, 3, 4).reshape(col_count, width, mixing_part)]
    picked, prob, q, kt, k, vt, v, mixing = project(
        who, x, rank[:, None], gain_one, router, tables_k, tables_q, mixing
    )
    mixed, mass = attend(q, k, vt, limit)
    (branch, inverse, normed), cot = hold(merge(mixed, picked, gain_two, mixing), cot)
    gate, up, active, delta, both = ffn(who, normed, branch, prob, col_count, hidden, sources)
    grad_ffn = (prob * cot.astype(F32)).astype(BF)
    (keep_down, send_down), delta, gate = hold(
        down_grad(who, grad_ffn, active, pairs, col_count), delta, gate
    )
    delta = from_owner(delta, sequences)
    pieces = pairs if aligned else 1
    back_args = (pieces, normed, grad_ffn, gate, up, sources)
    tail = (branch, both, picked, cot, prob, inverse, gain_two, router)

    def by_pairs(value):
        if aligned:
            return value
        value = value[0].reshape(half, pairs, 2 * rows, hidden).transpose(1, 0, 2, 3)
        return value[jnp.arange(pairs) ^ own_pair_index]

    got_down, (keep_low, send_low, carried), keep_down = hold(
        swap(send_down), ffn_back(who, 0, half, False, *back_args, None, None), keep_down
    )
    sum_down = pair_up(keep_down, got_down)
    sum_down, send_low, keep_low, carried = hold(sum_down, send_low, keep_low, carried)
    sum_down = spread(sum_down, "row")
    got_low, (keep_high, send_high, grad_attn, rest, gain_two_grad, router_grad), keep_low = hold(
        swap(send_low), ffn_back(who, half, half, True, *back_args, carried, tail), keep_low
    )
    sum_low = pair_up(by_pairs(keep_low), by_pairs(got_low))
    sum_low, send_high, keep_high, grad_attn = hold(sum_low, send_high, keep_high, grad_attn)
    got_high, sum_down, (gw_out, grad_mixed), keep_high = hold(
        swap(send_high), sum_down, merge_back(mixed, grad_attn, mixing), keep_high
    )
    sum_high = pair_up(by_pairs(keep_high), by_pairs(got_high))
    sum_down = list(add_up(sum_down).astype(BF))
    sum_high, sum_down, grad_mixed = hold(sum_high, sum_down, grad_mixed)
    sum_low, delta, (gq, gk, gv), sum_high, sum_down = hold(
        spread(sum_low, "row"),
        delta,
        attend_back(q, k, kt, v, limit, mass, grad_mixed, mixed, tables_k, tables_q),
        sum_high,
        spread(sum_down, "col"),
    )
    sum_low = list(add_up(sum_low).astype(BF))
    sum_down = add_up(sum_down)
    sum_low, sum_high, gq = hold(sum_low, sum_high, gq)
    sum_high, sum_low, (keep_mixing, send_mixing, grads) = hold(
        spread(sum_high, "row"),
        spread(sum_low, "col"),
        mixing_grad(who, x, rank[None, :], gain_one, gq, gk, gv, gw_out, pairs),
    )
    sum_high = list(add_up(sum_high).astype(BF))
    sum_high, send_mixing, keep_mixing, grads = hold(sum_high, send_mixing, keep_mixing, grads)
    got_mixing, (back, gain_one_grad), keep_mixing = hold(
        swap(send_mixing),
        project_back(x, rank[None, :], gain_one, grads, rest, mixing),
        keep_mixing,
    )
    back = from_owner(back, sequences)
    sum_pair = add_up(sum_low + [partner(value, "col", half + k) for k, value in enumerate(sum_high)])

    lanes = sum_down.shape[1] // 2
    first, second = sum_down[:, :lanes], sum_down[:, lanes:]
    mine, other = jnp.where(even, first, second), jnp.where(even, second, first)
    other = swap(other.astype(BF)).astype(F32)
    top, end = jnp.where(even, mine, other), jnp.where(even, other, mine)
    gw_down = jnp.concatenate([top, end[2 * down_rows_kept - part :]], axis=0).T

    vectors = jnp.concatenate([gain_one_grad, gain_two_grad, router_grad], axis=1).T.astype(BF)
    vectors = vectors.reshape(3, col_count, part).transpose(1, 0, 2)
    vectors = vectors[jnp.arange(col_count) ^ column]
    vectors = jnp.pad(vectors, ((0, 0), (0, VECTOR_ROWS - 3), (0, mixing_part - part)))
    other = swap(vectors)
    vectors = jnp.broadcast_to(vectors[None], (pairs,) + vectors.shape)
    other = jnp.broadcast_to(other[None], vectors.shape)
    keep_mixing = lax.dynamic_update_slice(keep_mixing, vectors, (0, 0, rows, 0))
    got_mixing = lax.dynamic_update_slice(got_mixing, other, (0, 0, rows, 0))
    sum_mixing = pair_up(keep_mixing, got_mixing)
    sum_mixing, block_out = hold(
        spread(sum_mixing, "row"), scatter_tokens(resid, delta, ranks[:, None, :])
    )
    sum_mixing = add_up(sum_mixing).astype(BF)
    gw_mixing = add_up(spread(list(sum_mixing), "col"))

    sum_pair = sum_pair.reshape(2, rows, hidden)
    mine = jnp.where(even, sum_pair[0], sum_pair[1])
    other = jnp.where(even, sum_pair[1], sum_pair[0]).astype(BF)
    other = swap(other).astype(F32)
    gw_gate, gw_up = jnp.where(even, mine, other), jnp.where(even, other, mine)
    if copies > 1:
        gw_gate, gw_up, gw_down, gw_mixing = (
            a / copies for a in (gw_gate, gw_up, gw_down, gw_mixing)
        )

    resid_grad = cotangent + back.astype(F32)
    kv_part = w_key.shape[1]
    ends = (part, part + kv_part, part + 2 * kv_part)
    return (
        block_out, resid_grad,
        gw_mixing[rows, :part], gw_mixing[rows + 1, :part], gw_mixing[rows + 2, :part],
        gw_mixing[:rows, : ends[0]], gw_mixing[:rows, ends[0] : ends[1]],
        gw_mixing[:rows, ends[1] : ends[2]], gw_mixing[:rows, ends[2] :],
        gw_gate, gw_up, gw_down,
    )


def solution(mesh):
    block = P("row", "col")
    placed = (
        P("row", "col", None), P("row", "col", None), P("row"), P("row"), P(None, "row", None),
        P(), P(), P(),
        block, block, block, block, block, block, block,
    )
    given = (
        P("row", "col", None), P("row", "col", None), P("col"), P("col"), P("col"),
        block, block, block, block, block, block, block,
    )
    return jax.shard_map(
        on_device, mesh=mesh, in_specs=placed, out_specs=given, check_vma=False
    )
```

```python
import functools
import math

import jax
import jax.numpy as jnp
from jax import lax
from jax.experimental import pallas as pl
from jax.experimental.pallas import tpu as pltpu
from jax.sharding import PartitionSpec as P

H = 15
KVH = 5
HD = 64
GROUP = H // KVH
QBLOCK = 256

EPSILON = 1e-05
ROPE_BASE = 10000.0
NEG = -1e30
VECTOR_ROWS = 8

BF = jnp.bfloat16
F32 = jnp.float32
MIB = 1 << 20


def dot_nn(a, b):
    return lax.dot_general(a, b, (((1,), (0,)), ((), ())), preferred_element_type=F32)


def dot_tn(a, b):
    return lax.dot_general(a, b, (((0,), (0,)), ((), ())), preferred_element_type=F32)


def dot_nt(a, b):
    return lax.dot_general(a, b, (((1,), (1,)), ((), ())), preferred_element_type=F32)


def params(limit=56):
    return pltpu.CompilerParams(
        dimension_semantics=("arbitrary",), vmem_limit_bytes=limit * MIB
    )


def cost(flops, nbytes, exps=0):
    return pl.CostEstimate(
        flops=int(flops) // 32,
        bytes_accessed=int(nbytes) // 32,
        transcendentals=int(exps) // 32,
    )


def struct(shape, dtype):
    return jax.ShapeDtypeStruct(shape, dtype)


def whole(shape):
    return pl.BlockSpec(shape, lambda i, *_: (0,) * len(shape))


def pick_columns(rank_column, picks):
    place = lax.broadcasted_iota(jnp.int32, (rank_column.shape[0], picks), 1)
    return jnp.where(rank_column == place, 1.0, 0.0).astype(BF)


def pick_rows(rank_row, picks):
    place = lax.broadcasted_iota(jnp.int32, (picks, rank_row.shape[1]), 0)
    return jnp.where(rank_row == place, 1.0, 0.0).astype(BF)


def turn(first, second, cosine, sine, direction):
    signed = sine * direction
    return first * cosine - second * signed, second * cosine + first * signed


def gather_body(values, rank, out):
    chosen = pick_columns(rank[0], out.shape[2])
    out[0] = dot_nn(values[0].astype(BF), chosen).astype(BF)


def gather_tokens(values, rank_column, picks):
    count, width, length = values.shape
    return pl.pallas_call(
        gather_body,
        grid=(count,),
        in_specs=[
            pl.BlockSpec((1, width, length), lambda i: (i, 0, 0)),
            pl.BlockSpec((1, length, 1), lambda i: (i, 0, 0)),
        ],
        out_specs=pl.BlockSpec((1, width, picks), lambda i: (i, 0, 0)),
        out_shape=struct((count, width, picks), BF),
        compiler_params=params(),
        cost_estimate=cost(2 * count * width * length * picks, 6 * values.size),
        name="gather_tokens",
    )(values, rank_column)


def scatter_body(base, values, rank, out):
    chosen = pick_rows(rank[0], values.shape[2])
    out[0] = base[0] + dot_nn(values[0], chosen)


def scatter_tokens(base, values, rank_row):
    count, width, length = base.shape
    picks = values.shape[2]
    return pl.pallas_call(
        scatter_body,
        grid=(count,),
        in_specs=[
            pl.BlockSpec((1, width, length), lambda i: (i, 0, 0)),
            pl.BlockSpec((1, width, picks), lambda i: (i, 0, 0)),
            pl.BlockSpec((1, 1, length), lambda i: (i, 0, 0)),
        ],
        out_specs=pl.BlockSpec((1, width, length), lambda i: (i, 0, 0)),
        out_shape=struct(base.shape, F32),
        compiler_params=params(),
        cost_estimate=cost(2 * count * width * length * picks, 10 * base.size),
        name="scatter_tokens",
    )(base, values, rank_row)


def project_body(who, x, rank, gain, router, cos_k, sin_k, cos_q, sin_q, *refs):
    pieces = refs[:-12]
    (
        picked, prob, q_out, kt_out, k_out, vt_out, v_out, w,
        normed, normed_picked, q_raw, kv_raw,
    ) = refs[-12:]
    step = pl.program_id(0)
    block = step ^ who[0]
    width = x.shape[0]
    q_part = width // pl.num_programs(0)
    kv_part = KVH * HD // pl.num_programs(0)
    if len(pieces) == 1:
        w[0] = pieces[0][0]
    else:
        even = who[2] == 0
        count = len(pieces) // 2
        for k, (own, other) in enumerate(zip(pieces[:count], pieces[count:])):
            first, second = own[0].astype(F32), other[0].astype(F32)
            both = [jnp.where(even, first, second), jnp.where(even, second, first)]
            height = 2 * first.shape[0]
            place = pl.ds(pl.multiple_of((who[1] ^ k) * height, 16), height)
            w[0, place] = jnp.concatenate(both, axis=0).astype(BF)

    @pl.when(step == 0)
    def _():
        full = x[...].astype(F32)
        inverse = lax.rsqrt(jnp.sum(full * full, axis=0, keepdims=True) / width + EPSILON)
        normed[...] = (full * inverse * gain[...]).astype(BF)
        chosen = pick_columns(rank[...], picked.shape[1])
        part = dot_nn(x[...], chosen)
        picked[...] = part.astype(BF)
        inverse = lax.rsqrt(jnp.sum(part * part, axis=0, keepdims=True) / width + EPSILON)
        normed_picked[...] = (part * inverse * gain[...]).astype(BF)
        logit = jnp.sum(part * router[...], axis=0, keepdims=True)
        prob[...] = jax.nn.sigmoid(logit)

    q_raw[pl.ds(pl.multiple_of(block * q_part, 8), q_part)] = dot_tn(
        w[0, :, :q_part], normed_picked[...]
    ).astype(BF)
    kv = dot_tn(w[0, :, q_part : q_part + 2 * kv_part], normed[...]).astype(BF)
    kv_raw[0, pl.ds(pl.multiple_of(block * kv_part, 8), kv_part)] = kv[:kv_part]
    kv_raw[1, pl.ds(pl.multiple_of(block * kv_part, 8), kv_part)] = kv[kv_part:]

    @pl.when(step == pl.num_programs(0) - 1)
    def _():
        half = HD // 2
        for head in range(H):
            at = head * HD
            a, b = turn(
                q_raw[at : at + half].astype(F32),
                q_raw[at + half : at + HD].astype(F32),
                cos_q[...], sin_q[...], 1.0,
            )
            scale = HD ** (-0.5)
            q_out[at : at + half] = (a.astype(BF).astype(F32) * scale).astype(BF)
            q_out[at + half : at + HD] = (b.astype(BF).astype(F32) * scale).astype(BF)
        for head in range(KVH):
            at = head * HD
            a, b = turn(
                kv_raw[0, at : at + half].astype(F32),
                kv_raw[0, at + half : at + HD].astype(F32),
                cos_k[...], sin_k[...], 1.0,
            )
            turned = jnp.concatenate([a, b], axis=0)
            kt_out[at : at + HD] = turned.astype(BF)
            k_out[head] = turned.T.astype(BF)
            value = kv_raw[1, at : at + HD]
            vt_out[at : at + HD] = value
            v_out[head] = value.astype(F32).T.astype(BF)


def project(who, x, rank_column, gain, router, tables_k, tables_q, pieces):
    width, length = x.shape
    picks = tables_q[0].shape[1]
    blocks, height, part = pieces[0].shape
    kv = KVH * HD
    half = HD // 2
    return pl.pallas_call(
        project_body,
        grid_spec=pltpu.PrefetchScalarGridSpec(
        num_scalar_prefetch=1,
        grid=(blocks,),
        in_specs=[
            whole((width, length)),
            whole((length, 1)),
            whole((width, 1)),
            whole((width, 1)),
            whole((half, length)),
            whole((half, length)),
            whole((half, picks)),
            whole((half, picks)),
        ]
        + [pl.BlockSpec((1, height, part), lambda i, who: (i, 0, 0))] * len(pieces),
        out_specs=[
            whole((width, picks)),
            whole((1, picks)),
            whole((width, picks)),
            whole((kv, length)),
            whole((KVH, length, HD)),
            whole((kv, length)),
            whole((KVH, length, HD)),
            pl.BlockSpec((1, width, part), lambda i, who: (i ^ who[0], 0, 0)),
        ],
        scratch_shapes=[
            pltpu.VMEM((width, length), BF),
            pltpu.VMEM((width, picks), BF),
            pltpu.VMEM((width, picks), BF),
            pltpu.VMEM((2, kv, length), BF),
        ],
        ),
        out_shape=[
            struct((width, picks), BF),
            struct((1, picks), F32),
            struct((width, picks), BF),
            struct((kv, length), BF),
            struct((KVH, length, HD), BF),
            struct((kv, length), BF),
            struct((KVH, length, HD), BF),
            struct((blocks, width, part), BF),
        ],
        compiler_params=params(),
        cost_estimate=cost(
            2 * width * (length * picks + picks * width + length * 2 * kv),
            2 * (2 * blocks * width * part + 4 * x.size),
        ),
        name="project",
    )(who, x, rank_column, gain, router, *tables_k, *tables_q, *pieces)


def reach_of(block, length, picks):
    return max((block + 1) * QBLOCK + length - picks, length // 2)


def clear_of(block):
    return block * QBLOCK


def block_scores(q, k, limit, block, reach):
    scores = dot_nn(k[:reach], q)
    clear = clear_of(block)
    tail = scores[clear:] if clear else scores
    key = lax.broadcasted_iota(jnp.int32, tail.shape, 0) + clear
    tail = jnp.where(key <= limit, tail, NEG)
    return jnp.concatenate([scores[:clear], tail], axis=0) if clear else tail


def attend_body(q, k, vt, limit, out, total):
    length = k.shape[1]
    picks = q.shape[1]
    for block in range(picks // QBLOCK):
        at = block * QBLOCK
        reach = reach_of(block, length, picks)
        for head in range(GROUP):
            rows = slice(head * HD, (head + 1) * HD)
            scores = block_scores(
                q[rows, at : at + QBLOCK], k[0], limit[:, at : at + QBLOCK], block, reach
            )
            top = jnp.max(scores, axis=0, keepdims=True)
            weight = jnp.exp(scores - top)
            mass = jnp.sum(weight, axis=0, keepdims=True)
            mixed = dot_nn(vt[:, :reach], weight.astype(BF))
            out[rows, at : at + QBLOCK] = (mixed / mass).astype(BF)
            total[0, head : head + 1, at : at + QBLOCK] = top + jnp.log(mass)


def attend(q, k, vt, limit):
    width, picks = q.shape
    length = k.shape[1]
    part = GROUP * HD
    return pl.pallas_call(
        attend_body,
        grid=(KVH,),
        in_specs=[
            pl.BlockSpec((part, picks), lambda i: (i, 0)),
            pl.BlockSpec((1, length, HD), lambda i: (i, 0, 0)),
            pl.BlockSpec((HD, length), lambda i: (i, 0)),
            whole((1, picks)),
        ],
        out_specs=[
            pl.BlockSpec((part, picks), lambda i: (i, 0)),
            pl.BlockSpec((1, GROUP, picks), lambda i: (i, 0, 0)),
        ],
        out_shape=[struct((width, picks), BF), struct((KVH, GROUP, picks), F32)],
        compiler_params=params(),
        cost_estimate=cost(
            16 * width * length * picks, 4 * width * picks, H * length * picks
        ),
        name="attend",
    )(q, k, vt, limit)


def attend_back_body(
    q, k, kt, v, limit, total, grad, mixed, cos_k, sin_k, cos_q, sin_q,
    gq_out, gk_out, gv_out, gk, gv,
):
    length = k.shape[1]
    picks = q.shape[1]
    half = HD // 2
    gk[...] = jnp.zeros_like(gk)
    gv[...] = jnp.zeros_like(gv)
    for block in range(picks // QBLOCK):
        at = block * QBLOCK
        cols = slice(at, at + QBLOCK)
        reach = reach_of(block, length, picks)
        for head in range(GROUP):
            rows = slice(head * HD, (head + 1) * HD)
            q_part = q[rows, cols]
            g_part = grad[rows, cols]
            scores = block_scores(q_part, k[0], limit[:, cols], block, reach)
            weight = jnp.exp(scores - total[0, head : head + 1, cols])
            delta = jnp.sum(
                g_part.astype(F32) * mixed[rows, cols].astype(F32), axis=0, keepdims=True
            )
            pull = dot_nn(v[0, :reach], g_part)
            back = (weight * (pull - delta)).astype(BF)
            gq = dot_nn(kt[:, :reach], back) * HD ** (-0.5)
            a, b = turn(gq[:half], gq[half:], cos_q[:, cols], sin_q[:, cols], -1.0)
            gq_out[head * HD : head * HD + half, cols] = a.astype(BF)
            gq_out[head * HD + half : (head + 1) * HD, cols] = b.astype(BF)
            gk[:reach] += dot_nt(back, q_part)
            gv[:reach] += dot_nt(weight.astype(BF), g_part)
    turned = gk[...].T
    a, b = turn(turned[:half], turned[half:], cos_k[...], sin_k[...], -1.0)
    gk_out[:half] = a.astype(BF)
    gk_out[half:] = b.astype(BF)
    gv_out[...] = gv[...].T.astype(BF)


def attend_back(first, count, q, k, kt, v, limit, total, grad, mixed, tables_k, tables_q):
    picks = q.shape[1]
    length = k.shape[1]
    part = GROUP * HD
    half = HD // 2
    wide = pl.BlockSpec((part, picks), lambda i: (first + i, 0))
    tall = pl.BlockSpec((1, length, HD), lambda i: (first + i, 0, 0))
    flat = pl.BlockSpec((HD, length), lambda i: (first + i, 0))
    return pl.pallas_call(
        attend_back_body,
        grid=(count,),
        in_specs=[
            wide, tall, flat, tall, whole((1, picks)),
            pl.BlockSpec((1, GROUP, picks), lambda i: (first + i, 0, 0)),
            wide, wide,
            whole((half, length)), whole((half, length)),
            whole((half, picks)), whole((half, picks)),
        ],
        out_specs=[
            pl.BlockSpec((part, picks), lambda i: (i, 0)),
            pl.BlockSpec((HD, length), lambda i: (i, 0)),
            pl.BlockSpec((HD, length), lambda i: (i, 0)),
        ],
        out_shape=[
            struct((count * part, picks), BF),
            struct((count * HD, length), BF),
            struct((count * HD, length), BF),
        ],
        scratch_shapes=[pltpu.VMEM((length, HD), F32), pltpu.VMEM((length, HD), F32)],
        compiler_params=params(),
        cost_estimate=cost(
            40 * count * part * length * picks, 8 * count * part * picks, count * GROUP * length * picks
        ),
        name="attend_back",
    )(q, k, kt, v, limit, total, grad, mixed, *tables_k, *tables_q)


def merge_body(mixed, picked, gain, w, branch, inverse_out, normed, hidden, square):
    step = pl.program_id(0)
    width = mixed.shape[0]
    part = width // pl.num_programs(0)
    rows = pl.ds(pl.multiple_of(step * part, 8), part)

    @pl.when(step == 0)
    def _():
        square[...] = jnp.zeros_like(square)

    value = dot_tn(w[0, :, w.shape[2] - part :], mixed[...])
    branch[...] = value
    total = picked[rows, :].astype(F32) + value
    hidden[rows, :] = total
    square[...] += jnp.sum(total * total, axis=0, keepdims=True)

    @pl.when(step == pl.num_programs(0) - 1)
    def _():
        inverse = lax.rsqrt(square[...] / width + EPSILON)
        inverse_out[...] = inverse
        normed[...] = (hidden[...] * inverse * gain[...]).astype(BF)


def merge(mixed, picked, gain, w):
    width, picks = mixed.shape
    blocks, _, wide = w.shape
    part = width // blocks
    return pl.pallas_call(
        merge_body,
        grid=(blocks,),
        in_specs=[
            whole((width, picks)),
            whole((width, picks)),
            whole((width, 1)),
            pl.BlockSpec((1, width, wide), lambda i: (i, 0, 0)),
        ],
        out_specs=[
            pl.BlockSpec((part, picks), lambda i: (i, 0)),
            whole((1, picks)),
            whole((width, picks)),
        ],
        out_shape=[
            struct((width, picks), F32),
            struct((1, picks), F32),
            struct((width, picks), BF),
        ],
        scratch_shapes=[pltpu.VMEM((width, picks), F32), pltpu.VMEM((1, picks), F32)],
        compiler_params=params(),
        cost_estimate=cost(2 * width * width * picks, 14 * width * picks + 2 * w.size),
        name="merge",
    )(mixed, picked, gain, w)


def down_half(part):
    return -(-part // 32) * 16


def ffn_weights(who, first, blocks, sources, w_gate, w_up, w_down, done):
    step, steps = pl.program_id(0), pl.num_programs(0)
    slot = lax.rem(step, 2)
    width = w_gate.shape[1]

    def copies(step, at):
        turn = blocks - 1 - first - step
        block = turn ^ who[0]
        if len(sources) == 2:
            some = [
                (sources[0].at[0, block], w_gate.at[at]),
                (sources[0].at[1, block], w_up.at[at]),
                (sources[1].at[block], w_down.at[at]),
            ]
        else:
            (source,) = sources
            pairs, _, columns, _, _ = source.shape
            height, part = width // pairs, width // columns
            half = down_half(part)
            some = []
            for i in range(pairs):
                place = slice(i * height, (i + 1) * height)
                some.append((source.at[i, 0, turn, :height], w_gate.at[at, place]))
                some.append((source.at[i, 1, turn, :height], w_up.at[at, place]))
            for c in range(columns):
                begin = pl.multiple_of((c ^ who[0]) * part, 16)
                top = pl.ds(begin, half)
                some.append((source.at[block, 0, c, height : height + half], w_down.at[at, top]))
                end = pl.ds(pl.multiple_of(begin + half, 16), part - half)
                rest = slice(height + 2 * half - part, height + half)
                some.append((source.at[block, 1, c, rest], w_down.at[at, end]))
        return [
            pltpu.make_async_copy(source, target, done.at[at, i])
            for i, (source, target) in enumerate(some)
        ]

    @pl.when(step == 0)
    def _():
        for copy in copies(step, slot):
            copy.start()

    @pl.when(step + 1 < steps)
    def _():
        for copy in copies(step + 1, 1 - slot):
            copy.start()

    for copy in copies(step, slot):
        copy.wait()
    return slot


def ffn_scratch(width, sources):
    hidden = sources[0].shape[-1]
    count = 3
    if len(sources) == 1:
        count = 2 * (sources[0].shape[0] + sources[0].shape[2])
    return [pltpu.VMEM((2, width, hidden), BF)] * 3 + [pltpu.SemaphoreType.DMA((2, count))]


def ffn_body(many, who, normed, branch, prob, *refs):
    sources, refs = refs[:many], refs[many:]
    gate_out, up_out, active_out, delta, both_out, forward, *buffers = refs
    w_gate, w_up, w_down, _ = buffers
    slot = ffn_weights(who, 0, pl.num_programs(0), sources, *buffers)

    @pl.when(pl.program_id(0) == 0)
    def _():
        forward[...] = branch[...]

    tokens = normed[...]
    gate = dot_tn(w_gate[slot], tokens)
    up = dot_tn(w_up[slot], tokens)
    active = (gate * jax.nn.sigmoid(gate) * up).astype(BF)
    gate_out[0] = gate.astype(BF)
    up_out[0] = up.astype(BF)
    active_out[0] = active
    forward[...] += dot_nn(w_down[slot], active)

    @pl.when(pl.program_id(0) == pl.num_programs(0) - 1)
    def _():
        both = forward[...]
        delta[...] = (prob[...] * both).astype(BF)
        both_out[...] = both.astype(BF)


def ffn(who, normed, branch, prob, blocks, hidden, sources):
    width, picks = normed.shape
    full, row = whole((width, picks)), whole((1, picks))
    far = pl.BlockSpec(memory_space=pl.ANY)
    kept = pl.BlockSpec((1, hidden, picks), lambda i, who: (i, 0, 0))
    kept_shape = struct((blocks, hidden, picks), BF)
    low = struct((width, picks), BF)
    return pl.pallas_call(
        functools.partial(ffn_body, len(sources)),
        grid_spec=pltpu.PrefetchScalarGridSpec(
            num_scalar_prefetch=1,
            grid=(blocks,),
            in_specs=[full, full, row] + [far] * len(sources),
            out_specs=[kept] * 3 + [full, full],
            scratch_shapes=[pltpu.VMEM((width, picks), F32)] + ffn_scratch(width, sources),
        ),
        out_shape=[kept_shape] * 3 + [low, low],
        compiler_params=params(60),
        cost_estimate=cost(
            6 * width * hidden * blocks * picks, 6 * width * hidden * blocks + 8 * width * picks
        ),
        name="ffn",
    )(who, normed, branch, prob, *sources)


def down_grad_body(who, grad_ffn, active, keep, send):
    here, columns, half, lanes = keep.shape
    part = grad_ffn.shape[0] // columns
    even = who[2] == 0
    for c in range(columns):
        value = dot_nt(grad_ffn[c * part : (c + 1) * part], active[0])
        low, high = value[:half].astype(BF), value[part - half :].astype(BF)
        mine, other = jnp.where(even, low, high), jnp.where(even, high, low)
        for i in range(here):
            at = i ^ lax.rem(who[1], here) if here > 1 else 0
            keep[at, c ^ who[0]] = mine[:, i * lanes : (i + 1) * lanes]
            send[at, c ^ who[0]] = other[:, i * lanes : (i + 1) * lanes]


def down_grad(who, grad_ffn, active, pairs, columns):
    width, picks = grad_ffn.shape
    blocks, hidden, _ = active.shape
    here = pairs // blocks
    tile = (columns, down_half(width // columns), hidden // here)
    block = pl.BlockSpec(
        (here,) + tile, lambda i, who: ((blocks - 1 - i) ^ who[0] ^ lax.div(who[1], here), 0, 0, 0)
    )
    return pl.pallas_call(
        down_grad_body,
        grid_spec=pltpu.PrefetchScalarGridSpec(
            num_scalar_prefetch=1,
            grid=(blocks,),
            in_specs=[
                whole((width, picks)),
                pl.BlockSpec((1, hidden, picks), lambda i, who: (i, 0, 0)),
            ],
            out_specs=[block, block],
        ),
        out_shape=[struct((pairs,) + tile, BF)] * 2,
        compiler_params=params(),
        cost_estimate=cost(2 * blocks * hidden * width * picks, 6 * blocks * hidden * width),
        name="down_grad",
    )(who, grad_ffn, active)


def ffn_back_body(first, blocks, last, many, who, normed, grad_ffn, gate_in, up_in, *refs):
    sources, refs = refs[:many], refs[many:]
    if first:
        carried, refs = refs[0], refs[1:]
    if last:
        (branch, both_in, picked, cot, prob, inverse, gain, router), refs = refs[:8], refs[8:]
    keep_pair, send_pair, refs = refs[0], refs[1], refs[2:]
    outs, backward, buffers = refs[:-5], refs[-5], refs[-4:]
    w_gate, w_up, w_down, _ = buffers
    slot = ffn_weights(who, first, blocks, sources, *buffers)
    width = normed.shape[0]
    even = who[2] == 0

    @pl.when(pl.program_id(0) == 0)
    def _():
        backward[...] = carried[...] if first else jnp.zeros_like(backward)

    pull = dot_tn(w_down[slot], grad_ffn[...])
    gate = gate_in[0].astype(F32)
    sigmoid = jax.nn.sigmoid(gate)
    silu = gate * sigmoid
    grad_gate = (pull * up_in[0].astype(F32) * (sigmoid + silu * (1.0 - sigmoid))).astype(BF)
    grad_up = (pull * silu).astype(BF)
    backward[...] += dot_nn(w_gate[slot], grad_gate) + dot_nn(w_up[slot], grad_up)
    tokens = normed[...]
    for_gate = dot_nt(tokens, grad_gate).astype(BF)
    for_up = dot_nt(tokens, grad_up).astype(BF)
    pieces, _, height, _ = keep_pair.shape
    for i in range(pieces):
        place = slice(i * height, (i + 1) * height)
        at = i ^ who[1] if pieces > 1 else 0
        keep_pair[at, 0] = jnp.where(even, for_gate[place], for_up[place])
        send_pair[at, 0] = jnp.where(even, for_up[place], for_gate[place])

    @pl.when(pl.program_id(0) == pl.num_programs(0) - 1)
    def _():
        if not last:
            outs[0][...] = backward[...]
            return
        grad_attn, rest_out, gain_out, router_out = outs
        share = prob[...]
        cot_full = cot[...].astype(F32)
        slope = share * (1.0 - share) * jnp.sum(
            cot_full * both_in[...].astype(F32), axis=0, keepdims=True
        )
        token = picked[...].astype(F32)
        router_out[...] = jnp.sum(slope * token, axis=1, keepdims=True)
        hidden = token + branch[...]
        inv = inverse[...]
        grad_norm = backward[...]
        gain_out[...] = jnp.sum(grad_norm * hidden * inv, axis=1, keepdims=True)
        unit = grad_norm * gain[...]
        along = jnp.sum(unit * hidden, axis=0, keepdims=True) / width
        grad_hidden = inv * unit - hidden * (inv * inv * inv * along)
        grad_attn[...] = (grad_hidden + share * cot_full).astype(BF)
        rest_out[...] = (grad_hidden + slope * router[...]).astype(BF)


def ffn_back(who, first, count, last, pieces, normed, grad_ffn, gate, up, sources, carried, tail):
    width, picks = normed.shape
    hidden = gate.shape[1]
    height = width // pieces
    full, row, column = whole((width, picks)), whole((1, picks)), whole((width, 1))
    far = pl.BlockSpec(memory_space=pl.ANY)
    kept = pl.BlockSpec((1, hidden, picks), lambda i, who: (i + first, 0, 0))
    tall = pl.BlockSpec((pieces, 1, height, hidden), lambda i, who: (0, i, 0, 0))
    tall_shape = struct((pieces, count, height, hidden), BF)
    low, thin = struct((width, picks), BF), struct((width, 1), F32)
    extra = ([carried] if first else []) + (list(tail) if last else [])
    extra_specs = ([full] if first else []) + ([full] * 4 + [row] * 2 + [column] * 2 if last else [])
    return pl.pallas_call(
        functools.partial(ffn_back_body, first, gate.shape[0], last, len(sources)),
        grid_spec=pltpu.PrefetchScalarGridSpec(
            num_scalar_prefetch=1,
            grid=(count,),
            in_specs=[full, full, kept, kept] + [far] * len(sources) + extra_specs,
            out_specs=[tall, tall] + ([full, full, column, column] if last else [full]),
            scratch_shapes=[pltpu.VMEM((width, picks), F32)] + ffn_scratch(width, sources),
        ),
        out_shape=[tall_shape, tall_shape]
        + ([low, low, thin, thin] if last else [struct((width, picks), F32)]),
        compiler_params=params(60),
        cost_estimate=cost(
            10 * width * hidden * count * picks, 10 * width * hidden * count + 12 * width * picks
        ),
        name="ffn_back",
    )(who, normed, grad_ffn, gate, up, *sources, *extra)


def merge_back_body(mixed, grad, w, gw, grad_mixed, total):
    step = pl.program_id(0)
    part = gw.shape[2]
    rows = pl.ds(pl.multiple_of(step * part, 8), part)
    piece = grad[rows, :]
    gw[0] = dot_nt(mixed[...], piece).astype(BF)
    value = dot_nn(w[0, :, w.shape[2] - part :], piece)

    @pl.when(step == 0)
    def _():
        total[...] = value

    @pl.when(step > 0)
    def _():
        total[...] += value

    @pl.when(step == pl.num_programs(0) - 1)
    def _():
        grad_mixed[...] = total[...].astype(BF)


def merge_back(mixed, grad, w):
    width, picks = mixed.shape
    blocks, _, wide = w.shape
    part = width // blocks
    block = pl.BlockSpec((1, width, part), lambda i: (i, 0, 0))
    wide_block = pl.BlockSpec((1, width, wide), lambda i: (i, 0, 0))
    return pl.pallas_call(
        merge_back_body,
        grid=(blocks,),
        in_specs=[whole((width, picks)), whole((width, picks)), wide_block],
        out_specs=[block, whole((width, picks))],
        out_shape=[struct((blocks, width, part), BF), struct((width, picks), BF)],
        scratch_shapes=[pltpu.VMEM((width, picks), F32)],
        compiler_params=params(),
        cost_estimate=cost(4 * width * width * picks, 6 * width * picks + 4 * w.size),
        name="merge_back",
    )(mixed, grad, w)


def project_back_body(x, rank, gain, *refs):
    gq, gk, gv, refs = refs[:2], refs[2:4], refs[4:6], refs[6:]
    rest, w, out, grads_out, gain_out, gq_full, gkv_full, total = refs
    step = pl.program_id(0)
    width = x.shape[0]
    q_part = width // pl.num_programs(0)
    kv_part = KVH * HD // pl.num_programs(0)

    @pl.when(step == 0)
    def _():
        chosen = pick_rows(rank[...], gq[0].shape[1])
        at = 0
        for piece in gq:
            gq_full[at : at + piece.shape[0]] = dot_nn(piece[...], chosen).astype(BF)
            at += piece.shape[0]
        for i, pieces in enumerate((gk, gv)):
            at = 0
            for piece in pieces:
                gkv_full[i, at : at + piece.shape[0]] = piece[...]
                at += piece.shape[0]
        total[...] = jnp.zeros_like(total)

    q_rows = pl.ds(pl.multiple_of(step * q_part, 8), q_part)
    kv_rows = pl.ds(pl.multiple_of(step * kv_part, 8), kv_part)
    grads = jnp.concatenate(
        [gq_full[q_rows, :], gkv_full[0, kv_rows, :], gkv_full[1, kv_rows, :]], axis=0
    )
    grads_out[0] = grads
    total[...] += dot_nn(w[0, :, : grads.shape[0]], grads)

    @pl.when(step == pl.num_programs(0) - 1)
    def _():
        full = x[...].astype(F32)
        inv = lax.rsqrt(jnp.sum(full * full, axis=0, keepdims=True) / width + EPSILON)
        grad_norm = total[...]
        gain_out[...] = jnp.sum(grad_norm * full * inv, axis=1, keepdims=True)
        unit = grad_norm * gain[...]
        along = jnp.sum(unit * full, axis=0, keepdims=True) / width
        chosen = pick_rows(rank[...], rest.shape[1])
        out[...] = (
            inv * unit - full * (inv * inv * inv * along) + dot_nn(rest[...], chosen)
        ).astype(BF)


def project_back(x, rank_row, gain, gq, gk, gv, rest, w):
    width, length = x.shape
    picks = rest.shape[1]
    blocks = w.shape[0]
    kv = KVH * HD
    part = (width + 2 * kv) // blocks
    return pl.pallas_call(
        project_back_body,
        grid=(blocks,),
        in_specs=[
            whole((width, length)),
            whole((1, length)),
            whole((width, 1)),
            *(whole(piece.shape) for piece in (*gq, *gk, *gv)),
            whole((width, picks)),
            pl.BlockSpec((1,) + w.shape[1:], lambda i: (i, 0, 0)),
        ],
        out_specs=[
            whole((width, length)),
            pl.BlockSpec((1, part, length), lambda i: (i, 0, 0)),
            whole((width, 1)),
        ],
        out_shape=[
            struct((width, length), BF),
            struct((blocks, part, length), BF),
            struct((width, 1), F32),
        ],
        scratch_shapes=[
            pltpu.VMEM((width, length), BF),
            pltpu.VMEM((2, kv, length), BF),
            pltpu.VMEM((width, length), F32),
        ],
        compiler_params=params(),
        cost_estimate=cost(
            2 * width * length * (2 * picks + blocks * part), 10 * x.size + 2 * w.size
        ),
        name="project_back",
    )(x, rank_row, gain, *gq, *gk, *gv, rest, w)


def mixing_grad_body(who, x, gain, grads, gw_out, keep, send, normed):
    width = x.shape[0]
    even = who[2] == 0

    @pl.when(pl.program_id(0) == 0)
    def _():
        full = x[...].astype(F32)
        inverse = lax.rsqrt(jnp.sum(full * full, axis=0, keepdims=True) / width + EPSILON)
        normed[...] = (full * inverse * gain[...]).astype(BF)

    value = dot_nt(normed[...], grads[0])
    value = jnp.concatenate([value, gw_out[0].astype(F32)], axis=1)
    pairs = keep.shape[0]
    rows = width // (2 * pairs)
    for pair in range(pairs):
        low = value[2 * pair * rows : (2 * pair + 1) * rows]
        high = value[(2 * pair + 1) * rows : (2 * pair + 2) * rows]
        keep[pair ^ who[1], 0, :rows] = jnp.where(even, low, high).astype(BF)
        send[pair ^ who[1], 0, :rows] = jnp.where(even, high, low).astype(BF)


def mixing_grad(who, x, gain, grads, gw_out, pairs):
    width, length = x.shape
    blocks, part, _ = grads.shape
    out_part = gw_out.shape[2]
    rows = width // (2 * pairs) + VECTOR_ROWS
    split = pl.BlockSpec((pairs, 1, rows, part + out_part), lambda i, who: (0, i ^ who[0], 0, 0))
    split_shape = struct((pairs, blocks, rows, part + out_part), BF)
    return pl.pallas_call(
        mixing_grad_body,
        grid_spec=pltpu.PrefetchScalarGridSpec(
            num_scalar_prefetch=1,
            grid=(blocks,),
            in_specs=[
                whole((width, length)),
                whole((width, 1)),
                pl.BlockSpec((1, part, length), lambda i, who: (i, 0, 0)),
                pl.BlockSpec((1, width, out_part), lambda i, who: (i, 0, 0)),
            ],
            out_specs=[split, split],
            scratch_shapes=[pltpu.VMEM((width, length), BF)],
        ),
        out_shape=[split_shape, split_shape],
        compiler_params=params(),
        cost_estimate=cost(2 * width * length * blocks * part, 10 * x.size),
        name="mixing_grad",
    )(who, x, gain, grads, gw_out)


def hold(*values):
    return lax.optimization_barrier(values)


def swap(value):
    count = lax.axis_size("row")
    return lax.ppermute(value, "row", [(i, i ^ 1) for i in range(count)])


def partner(value, axis, k):
    count = lax.axis_size(axis)
    far = k if axis == "col" else 2 * k
    return lax.ppermute(value, axis, [(i, i ^ far) for i in range(count)])


def collect(value, axis, partners):
    return [partner(value, axis, k) if k else value for k in partners]


def spread(values, axis):
    return [values[0]] + [partner(value, axis, k) for k, value in enumerate(values) if k]


def add_up(values):
    return sum(value.astype(F32) for value in values)


def pack(first, second):
    if first.shape[1] == second.shape[1]:
        return [jnp.concatenate([first, second], axis=0)]
    return [first, second]


def unpack(values, rows):
    return (values[0][:rows], values[0][rows:]) if len(values) == 1 else tuple(values)


def pair_up(keep, got):
    return [add_up((a, b)).astype(BF) for a, b in zip(keep, got)]


def to_owner(value):
    copies = lax.axis_size("col") // value.shape[0]
    if copies > 1:
        value = jnp.concatenate([value] * copies, axis=0)
    moved = lax.all_to_all(value, "col", split_axis=0, concat_axis=1, tiled=True)
    return moved[0]


def from_owner(value, sequences):
    count = lax.axis_size("col")
    value = value.reshape(count, value.shape[0] // count, value.shape[1])
    moved = lax.all_to_all(value, "col", split_axis=0, concat_axis=0, tiled=True)
    return moved[:sequences]


def rope_tables(positions):
    half = HD // 2
    frequency = jnp.exp(jnp.arange(half, dtype=F32) * (-2.0 * math.log(ROPE_BASE) / HD))
    angles = frequency[:, None] * positions.astype(F32)[None, :]
    return jnp.cos(angles), jnp.sin(angles)


def on_device(
    resid, cotangent, prefix, slot, chosen, norm1_gain, norm2_gain, router,
    w_query, w_key, w_value, w_out, w_gate, w_up, w_down,
):
    col_count, row_count = lax.axis_size("col"), lax.axis_size("row")
    column = lax.axis_index("col")
    sequences, part, length = resid.shape
    width = part * col_count
    picks = chosen.shape[2]
    copies = col_count // sequences
    own = lax.rem(column, sequences)
    rows, hidden = w_gate.shape
    down_rows = w_down.shape[0]
    pairs = row_count // 2
    mixing_part = part + 2 * w_key.shape[1] + part

    own_pair_index = lax.axis_index("row") >> 1
    core = lax.axis_index("row") & 1
    even = core == 0
    who = jnp.stack([column, own_pair_index, core]).astype(jnp.int32)
    aligned = 2 * rows % 16 == 0

    half = col_count // 2

    mine = jnp.where(even, w_gate, w_up)
    other = swap(jnp.where(even, w_up, w_gate))
    pair = jnp.concatenate([jnp.where(even, mine, other), jnp.where(even, other, mine)], axis=0)
    down_rows_kept = down_half(part)
    turned = w_down.T
    low, high = turned[:down_rows_kept], turned[part - down_rows_kept :]
    mine, other = jnp.where(even, low, high), swap(jnp.where(even, high, low))
    down = jnp.concatenate([jnp.where(even, mine, other), jnp.where(even, other, mine)], axis=1)
    mixing = jnp.concatenate([w_query, w_key, w_value, w_out], axis=1)
    mixing, pair, down = hold(collect(mixing, "col", range(col_count)), pair, down)
    mixing, x = jnp.stack(mixing), resid.astype(BF)
    if aligned:
        sources = jnp.concatenate([pair, down], axis=0)
        sources, mixing, x = hold(
            collect(sources, "col", range(col_count)), collect(mixing, "row", range(pairs)), x
        )
        sources = lax.all_gather(jnp.stack(sources), "row", axis=0)
        sources = (sources.reshape((pairs, 2) + sources.shape[1:]),)
    else:
        mixing, x = hold(collect(mixing, "row", range(pairs)), x)
        pair_all = lax.all_gather(pair, ("row", "col"), axis=0)
        pair_all = pair_all.reshape(pairs, 2, col_count, 2 * rows, hidden).transpose(1, 2, 0, 3, 4)
        down_all = lax.all_gather(down, ("row", "col"), axis=0)
        down_all = down_all.reshape((col_count, pairs // col_count, 2, col_count) + down.shape)
        down_all = jnp.concatenate(
            [down_all[:, :, 0], down_all[:, :, 1, :, 2 * down_rows_kept - part :]], axis=3
        )
        sources = (
            pair_all.reshape(2, col_count, width, hidden),
            down_all.transpose(0, 2, 3, 1, 4).reshape(col_count, width, hidden),
        )
    every = jnp.arange(length, dtype=jnp.int32)
    chosen_of = chosen[:, 0][slot]
    selected = jnp.any(every[None, :, None] == chosen_of[:, None, :], axis=2)
    before = (every[:, None] < every[None, :]).astype(BF)
    places = jnp.dot(selected.astype(BF), before, preferred_element_type=F32)
    ranks = jnp.where(selected, places.astype(jnp.int32), -1)
    rank = lax.dynamic_index_in_dim(ranks, own, 0, keepdims=False)
    prefix_len = lax.dynamic_index_in_dim(prefix, own, 0, keepdims=False)
    place = jnp.arange(picks, dtype=jnp.int32)
    spot = jnp.sum(jnp.where(rank[None, :] == place[:, None], every[None, :], 0), axis=1)
    limit = jnp.maximum(spot, prefix_len - 1)[None, :]
    tables_k = rope_tables(every)
    tables_q = rope_tables(spot)
    gain_one, gain_two, router = norm1_gain[:, None], norm2_gain[:, None], router[:, None]
    cot = gather_tokens(cotangent, ranks[:, :, None], picks)

    x, mixing_other, mixing, cot, limit, tables_k, tables_q = hold(
        to_owner(x), [swap(piece) for piece in mixing], mixing, cot, limit, tables_k, tables_q
    )
    cot = to_owner(cot)
    if aligned:
        mixing = mixing + mixing_other
    else:
        order = jnp.arange(pairs) ^ own_pair_index
        mixing = jnp.stack([jnp.stack(mixing), jnp.stack(mixing_other)])[jnp.stack([core, 1 - core])]
        mixing = [mixing[:, order].transpose(2, 1, 0, 3, 4).reshape(col_count, width, mixing_part)]
    picked, prob, q, kt, k, vt, v, mixing = project(
        who, x, rank[:, None], gain_one, router, tables_k, tables_q, mixing
    )
    mixed, mass = attend(q, k, vt, limit)
    (branch, inverse, normed), cot = hold(merge(mixed, picked, gain_two, mixing), cot)
    gate, up, active, delta, both = ffn(who, normed, branch, prob, col_count, hidden, sources)
    grad_ffn = (prob * cot.astype(F32)).astype(BF)
    (keep_down, send_down), delta, gate = hold(
        down_grad(who, grad_ffn, active, pairs, col_count), delta, gate
    )
    delta = from_owner(delta, sequences)
    pieces = pairs if aligned else 1
    back_args = (pieces, normed, grad_ffn, gate, up, sources)
    tail = (branch, both, picked, cot, prob, inverse, gain_two, router)

    def by_pairs(value):
        if aligned:
            return value
        value = value[0].reshape(half, pairs, 2 * rows, hidden).transpose(1, 0, 2, 3)
        return value[jnp.arange(pairs) ^ own_pair_index]

    got_down, (keep_low, send_low, carried), keep_down = hold(
        swap(send_down), ffn_back(who, 0, half, False, *back_args, None, None), keep_down
    )
    sum_down = pair_up(keep_down, got_down)
    sum_down, send_low, keep_low, carried = hold(sum_down, send_low, keep_low, carried)
    (
        got_low, sum_down,
        (keep_high, send_high, grad_attn, rest, gain_two_grad, router_grad), keep_low,
    ) = hold(
        swap(send_low),
        spread(sum_down, "row"),
        ffn_back(who, half, half, True, *back_args, carried, tail),
        keep_low,
    )
    sum_low = pair_up(by_pairs(keep_low), by_pairs(got_low))
    sum_down = list(add_up(sum_down).astype(BF))
    sum_low, sum_down, send_high, keep_high, grad_attn = hold(
        sum_low, sum_down, send_high, keep_high, grad_attn
    )
    sum_low = spread(sum_low, "row")
    got_high, (gw_out, grad_mixed), keep_high = hold(
        swap(send_high), merge_back(mixed, grad_attn, mixing), keep_high
    )
    sum_high = pair_up(by_pairs(keep_high), by_pairs(got_high))
    sum_high, grad_mixed = hold(sum_high, grad_mixed)
    heads = (q, k, kt, v, limit, mass, grad_mixed, mixed, tables_k, tables_q)
    most = (KVH + 1) // 2
    sum_low, delta, one, sum_high = hold(
        sum_low, delta, attend_back(0, most, *heads), sum_high
    )
    far = [
        pack(value, sum_down[-1 - i])
        for i, value in enumerate(add_up(sum_low).astype(BF))
    ]
    far, one, grad_mixed = hold(far, one, grad_mixed)
    far = [
        [partner(value, "col", col_count - 1 - i) for value in values]
        for i, values in enumerate(far)
    ]
    heads = heads[:6] + (grad_mixed,) + heads[7:]
    sum_high = spread(sum_high, "row")
    (two,) = hold(attend_back(most, KVH - most, *heads))
    gq, gk, gv = zip(one, two)
    far, sum_high, (back, grads, gain_one_grad) = hold(
        far,
        sum_high,
        project_back(x, rank[None, :], gain_one, gq, gk, gv, rest, mixing),
    )
    *near, sum_pair = add_up(sum_high).astype(BF)
    near = [pack(value, sum_down[half - 1 - i]) for i, value in enumerate(near)]
    vectors = jnp.concatenate([gain_one_grad, gain_two_grad, router_grad], axis=1).T.astype(BF)
    vectors = vectors.reshape(3, col_count, part).transpose(1, 0, 2)
    vectors = vectors[jnp.arange(col_count) ^ column]
    vectors = jnp.pad(vectors, ((0, 0), (0, VECTOR_ROWS - 3), (0, mixing_part - part)))
    vectors = jnp.broadcast_to(vectors[None], (pairs,) + vectors.shape)
    near, back, grads, vectors = hold(near, back, grads, vectors)
    back = from_owner(back, sequences)
    near, gw_mixing = hold(
        [
            [partner(value, "col", half - 1 - i) for value in values]
            for i, values in enumerate(near)
        ],
        mixing_grad(who, x, gain_one, grads, gw_out, pairs),
    )
    keep_mixing, send_mixing = (
        lax.dynamic_update_slice(value, vectors, (0, 0, rows, 0)) for value in gw_mixing
    )
    got_mixing, block_out, keep_mixing = hold(
        swap(send_mixing), scatter_tokens(resid, delta, ranks[:, None, :]), keep_mixing
    )
    sum_mixing = add_up(spread(pair_up(keep_mixing, got_mixing), "row")).astype(BF)
    parts = [unpack(values, 2 * rows) for values in near + far]
    sum_pair = add_up([sum_pair] + [first for first, _ in parts])
    sum_down = add_up([sum_down[0]] + [second for _, second in parts])

    lanes = sum_down.shape[1] // 2
    first, second = sum_down[:, :lanes], sum_down[:, lanes:]
    mine, other = jnp.where(even, first, second), jnp.where(even, second, first)
    other = swap(other.astype(BF)).astype(F32)
    top, end = jnp.where(even, mine, other), jnp.where(even, other, mine)
    gw_down = jnp.concatenate([top, end[2 * down_rows_kept - part :]], axis=0).T

    gw_mixing = add_up(spread(list(sum_mixing), "col"))

    sum_pair = sum_pair.reshape(2, rows, hidden)
    mine = jnp.where(even, sum_pair[0], sum_pair[1])
    other = jnp.where(even, sum_pair[1], sum_pair[0]).astype(BF)
    other = swap(other).astype(F32)
    gw_gate, gw_up = jnp.where(even, mine, other), jnp.where(even, other, mine)
    if copies > 1:
        gw_gate, gw_up, gw_down, gw_mixing = (
            a / copies for a in (gw_gate, gw_up, gw_down, gw_mixing)
        )

    resid_grad = cotangent + back.astype(F32)
    kv_part = w_key.shape[1]
    ends = (part, part + kv_part, part + 2 * kv_part)
    return (
        block_out, resid_grad,
        gw_mixing[rows, :part], gw_mixing[rows + 1, :part], gw_mixing[rows + 2, :part],
        gw_mixing[:rows, : ends[0]], gw_mixing[:rows, ends[0] : ends[1]],
        gw_mixing[:rows, ends[1] : ends[2]], gw_mixing[:rows, ends[2] :],
        gw_gate, gw_up, gw_down,
    )


def solution(mesh):
    block = P("row", "col")
    placed = (
        P("row", "col", None), P("row", "col", None), P("row"), P("row"), P(None, "row", None),
        P(), P(), P(),
        block, block, block, block, block, block, block,
    )
    given = (
        P("row", "col", None), P("row", "col", None), P("col"), P("col"), P("col"),
        block, block, block, block, block, block, block,
    )
    return jax.shard_map(
        on_device, mesh=mesh, in_specs=placed, out_specs=given, check_vma=False
    )
```

```python
import functools
import math

import jax
import jax.numpy as jnp
from jax import lax
from jax.experimental import pallas as pl
from jax.experimental.pallas import tpu as pltpu
from jax.sharding import PartitionSpec as P

H = 15
KVH = 5
HD = 64
GROUP = H // KVH
QBLOCK = 256

EPSILON = 1e-05
ROPE_BASE = 10000.0
NEG = -1e30
VECTOR_ROWS = 8

BF = jnp.bfloat16
F32 = jnp.float32
MIB = 1 << 20


def dot_nn(a, b):
    return lax.dot_general(a, b, (((1,), (0,)), ((), ())), preferred_element_type=F32)


def dot_tn(a, b):
    return lax.dot_general(a, b, (((0,), (0,)), ((), ())), preferred_element_type=F32)


def dot_nt(a, b):
    return lax.dot_general(a, b, (((1,), (1,)), ((), ())), preferred_element_type=F32)


def params(limit=56):
    return pltpu.CompilerParams(
        dimension_semantics=("arbitrary",), vmem_limit_bytes=limit * MIB
    )


def cost(flops, nbytes, exps=0):
    return pl.CostEstimate(
        flops=int(flops) // 32,
        bytes_accessed=int(nbytes) // 32,
        transcendentals=int(exps) // 32,
    )


def struct(shape, dtype):
    return jax.ShapeDtypeStruct(shape, dtype)


def whole(shape):
    return pl.BlockSpec(shape, lambda i, *_: (0,) * len(shape))


def pick_columns(rank_column, picks):
    place = lax.broadcasted_iota(jnp.int32, (rank_column.shape[0], picks), 1)
    return jnp.where(rank_column == place, 1.0, 0.0).astype(BF)


def pick_rows(rank_row, picks):
    place = lax.broadcasted_iota(jnp.int32, (picks, rank_row.shape[1]), 0)
    return jnp.where(rank_row == place, 1.0, 0.0).astype(BF)


def turn(first, second, cosine, sine, direction):
    signed = sine * direction
    return first * cosine - second * signed, second * cosine + first * signed


def gather_body(values, rank, out):
    chosen = pick_columns(rank[0], out.shape[2])
    out[0] = dot_nn(values[0].astype(BF), chosen).astype(BF)


def gather_tokens(values, rank_column, picks):
    count, width, length = values.shape
    return pl.pallas_call(
        gather_body,
        grid=(count,),
        in_specs=[
            pl.BlockSpec((1, width, length), lambda i: (i, 0, 0)),
            pl.BlockSpec((1, length, 1), lambda i: (i, 0, 0)),
        ],
        out_specs=pl.BlockSpec((1, width, picks), lambda i: (i, 0, 0)),
        out_shape=struct((count, width, picks), BF),
        compiler_params=params(),
        cost_estimate=cost(2 * count * width * length * picks, 6 * values.size),
        name="gather_tokens",
    )(values, rank_column)


def scatter_body(base, values, rank, out):
    chosen = pick_rows(rank[0], values.shape[2])
    out[0] = base[0] + dot_nn(values[0], chosen)


def scatter_tokens(base, values, rank_row):
    count, width, length = base.shape
    picks = values.shape[2]
    return pl.pallas_call(
        scatter_body,
        grid=(count,),
        in_specs=[
            pl.BlockSpec((1, width, length), lambda i: (i, 0, 0)),
            pl.BlockSpec((1, width, picks), lambda i: (i, 0, 0)),
            pl.BlockSpec((1, 1, length), lambda i: (i, 0, 0)),
        ],
        out_specs=pl.BlockSpec((1, width, length), lambda i: (i, 0, 0)),
        out_shape=struct(base.shape, F32),
        compiler_params=params(),
        cost_estimate=cost(2 * count * width * length * picks, 10 * base.size),
        name="scatter_tokens",
    )(base, values, rank_row)


def project_body(who, x, rank, gain, router, cos_k, sin_k, cos_q, sin_q, *refs):
    pieces = refs[:-12]
    (
        picked, prob, q_out, kt_out, k_out, vt_out, v_out, w,
        normed, normed_picked, q_raw, kv_raw,
    ) = refs[-12:]
    step = pl.program_id(0)
    block = step ^ who[0]
    width = x.shape[0]
    q_part = width // pl.num_programs(0)
    kv_part = KVH * HD // pl.num_programs(0)
    if len(pieces) == 1:
        w[0] = pieces[0][0]
    else:
        even = who[2] == 0
        count = len(pieces) // 2
        for k, (own, other) in enumerate(zip(pieces[:count], pieces[count:])):
            first, second = own[0].astype(F32), other[0].astype(F32)
            both = [jnp.where(even, first, second), jnp.where(even, second, first)]
            height = 2 * first.shape[0]
            place = pl.ds(pl.multiple_of((who[1] ^ k) * height, 16), height)
            w[0, place] = jnp.concatenate(both, axis=0).astype(BF)

    @pl.when(step == 0)
    def _():
        full = x[...].astype(F32)
        inverse = lax.rsqrt(jnp.sum(full * full, axis=0, keepdims=True) / width + EPSILON)
        normed[...] = (full * inverse * gain[...]).astype(BF)
        chosen = pick_columns(rank[...], picked.shape[1])
        part = dot_nn(x[...], chosen)
        picked[...] = part.astype(BF)
        inverse = lax.rsqrt(jnp.sum(part * part, axis=0, keepdims=True) / width + EPSILON)
        normed_picked[...] = (part * inverse * gain[...]).astype(BF)
        logit = jnp.sum(part * router[...], axis=0, keepdims=True)
        prob[...] = jax.nn.sigmoid(logit)

    q_raw[pl.ds(pl.multiple_of(block * q_part, 8), q_part)] = dot_tn(
        w[0, :, :q_part], normed_picked[...]
    ).astype(BF)
    kv = dot_tn(w[0, :, q_part : q_part + 2 * kv_part], normed[...]).astype(BF)
    kv_raw[0, pl.ds(pl.multiple_of(block * kv_part, 8), kv_part)] = kv[:kv_part]
    kv_raw[1, pl.ds(pl.multiple_of(block * kv_part, 8), kv_part)] = kv[kv_part:]

    @pl.when(step == pl.num_programs(0) - 1)
    def _():
        half = HD // 2
        for head in range(H):
            at = head * HD
            a, b = turn(
                q_raw[at : at + half].astype(F32),
                q_raw[at + half : at + HD].astype(F32),
                cos_q[...], sin_q[...], 1.0,
            )
            scale = HD ** (-0.5)
            q_out[at : at + half] = (a.astype(BF).astype(F32) * scale).astype(BF)
            q_out[at + half : at + HD] = (b.astype(BF).astype(F32) * scale).astype(BF)
        for head in range(KVH):
            at = head * HD
            a, b = turn(
                kv_raw[0, at : at + half].astype(F32),
                kv_raw[0, at + half : at + HD].astype(F32),
                cos_k[...], sin_k[...], 1.0,
            )
            turned = jnp.concatenate([a, b], axis=0)
            kt_out[at : at + HD] = turned.astype(BF)
            k_out[head] = turned.T.astype(BF)
            value = kv_raw[1, at : at + HD]
            vt_out[at : at + HD] = value
            v_out[head] = value.astype(F32).T.astype(BF)


def project(who, x, rank_column, gain, router, tables_k, tables_q, pieces):
    width, length = x.shape
    picks = tables_q[0].shape[1]
    blocks, height, part = pieces[0].shape
    kv = KVH * HD
    half = HD // 2
    return pl.pallas_call(
        project_body,
        grid_spec=pltpu.PrefetchScalarGridSpec(
        num_scalar_prefetch=1,
        grid=(blocks,),
        in_specs=[
            whole((width, length)),
            whole((length, 1)),
            whole((width, 1)),
            whole((width, 1)),
            whole((half, length)),
            whole((half, length)),
            whole((half, picks)),
            whole((half, picks)),
        ]
        + [pl.BlockSpec((1, height, part), lambda i, who: (i, 0, 0))] * len(pieces),
        out_specs=[
            whole((width, picks)),
            whole((1, picks)),
            whole((width, picks)),
            whole((kv, length)),
            whole((KVH, length, HD)),
            whole((kv, length)),
            whole((KVH, length, HD)),
            pl.BlockSpec((1, width, part), lambda i, who: (i ^ who[0], 0, 0)),
        ],
        scratch_shapes=[
            pltpu.VMEM((width, length), BF),
            pltpu.VMEM((width, picks), BF),
            pltpu.VMEM((width, picks), BF),
            pltpu.VMEM((2, kv, length), BF),
        ],
        ),
        out_shape=[
            struct((width, picks), BF),
            struct((1, picks), F32),
            struct((width, picks), BF),
            struct((kv, length), BF),
            struct((KVH, length, HD), BF),
            struct((kv, length), BF),
            struct((KVH, length, HD), BF),
            struct((blocks, width, part), BF),
        ],
        compiler_params=params(),
        cost_estimate=cost(
            2 * width * (length * picks + picks * width + length * 2 * kv),
            2 * (2 * blocks * width * part + 4 * x.size),
        ),
        name="project",
    )(who, x, rank_column, gain, router, *tables_k, *tables_q, *pieces)


def reach_of(block, length, picks):
    return max((block + 1) * QBLOCK + length - picks, length // 2)


def clear_of(block):
    return block * QBLOCK


def block_scores(q, k, limit, block, reach):
    scores = dot_nn(k[:reach], q)
    clear = clear_of(block)
    tail = scores[clear:] if clear else scores
    key = lax.broadcasted_iota(jnp.int32, tail.shape, 0) + clear
    tail = jnp.where(key <= limit, tail, NEG)
    return jnp.concatenate([scores[:clear], tail], axis=0) if clear else tail


def side_by_side(value, cols):
    return jnp.concatenate(
        [value[head * HD : (head + 1) * HD, cols] for head in range(GROUP)], axis=1
    )


def attend_body(q, k, vt, limit, out, total):
    length = k.shape[1]
    picks = q.shape[1]
    for block in range(picks // QBLOCK):
        cols = slice(block * QBLOCK, (block + 1) * QBLOCK)
        reach = reach_of(block, length, picks)
        limits = jnp.concatenate([limit[:, cols]] * GROUP, axis=1)
        scores = block_scores(side_by_side(q, cols), k[0], limits, block, reach)
        top = jnp.max(scores, axis=0, keepdims=True)
        weight = jnp.exp(scores - top)
        mass = jnp.sum(weight, axis=0, keepdims=True)
        mixed = (dot_nn(vt[:, :reach], weight.astype(BF)) / mass).astype(BF)
        logs = top + jnp.log(mass)
        for head in range(GROUP):
            part = slice(head * QBLOCK, (head + 1) * QBLOCK)
            out[head * HD : (head + 1) * HD, cols] = mixed[:, part]
            total[0, head : head + 1, cols] = logs[:, part]


def attend(q, k, vt, limit):
    width, picks = q.shape
    length = k.shape[1]
    part = GROUP * HD
    return pl.pallas_call(
        attend_body,
        grid=(KVH,),
        in_specs=[
            pl.BlockSpec((part, picks), lambda i: (i, 0)),
            pl.BlockSpec((1, length, HD), lambda i: (i, 0, 0)),
            pl.BlockSpec((HD, length), lambda i: (i, 0)),
            whole((1, picks)),
        ],
        out_specs=[
            pl.BlockSpec((part, picks), lambda i: (i, 0)),
            pl.BlockSpec((1, GROUP, picks), lambda i: (i, 0, 0)),
        ],
        out_shape=[struct((width, picks), BF), struct((KVH, GROUP, picks), F32)],
        compiler_params=params(),
        cost_estimate=cost(
            16 * width * length * picks, 4 * width * picks, H * length * picks
        ),
        name="attend",
    )(q, k, vt, limit)


def attend_back_body(
    q, k, kt, v, limit, total, grad, mixed, cos_k, sin_k, cos_q, sin_q,
    gq_out, gk_out, gv_out, gk, gv,
):
    length = k.shape[1]
    picks = q.shape[1]
    half = HD // 2
    gk[...] = jnp.zeros_like(gk)
    gv[...] = jnp.zeros_like(gv)
    for block in range(picks // QBLOCK):
        cols = slice(block * QBLOCK, (block + 1) * QBLOCK)
        reach = reach_of(block, length, picks)
        limits = jnp.concatenate([limit[:, cols]] * GROUP, axis=1)
        q_part, g_part = side_by_side(q, cols), side_by_side(grad, cols)
        scores = block_scores(q_part, k[0], limits, block, reach)
        logs = jnp.concatenate([total[0, head : head + 1, cols] for head in range(GROUP)], axis=1)
        weight = jnp.exp(scores - logs)
        delta = jnp.sum(
            g_part.astype(F32) * side_by_side(mixed, cols).astype(F32), axis=0, keepdims=True
        )
        pull = dot_nn(v[0, :reach], g_part)
        back = (weight * (pull - delta)).astype(BF)
        gq = dot_nn(kt[:, :reach], back) * HD ** (-0.5)
        gk[:reach] += dot_nt(back, q_part)
        gv[:reach] += dot_nt(weight.astype(BF), g_part)
        for head in range(GROUP):
            part = slice(head * QBLOCK, (head + 1) * QBLOCK)
            a, b = turn(gq[:half, part], gq[half:, part], cos_q[:, cols], sin_q[:, cols], -1.0)
            gq_out[head * HD : head * HD + half, cols] = a.astype(BF)
            gq_out[head * HD + half : (head + 1) * HD, cols] = b.astype(BF)
    turned = gk[...].T
    a, b = turn(turned[:half], turned[half:], cos_k[...], sin_k[...], -1.0)
    gk_out[:half] = a.astype(BF)
    gk_out[half:] = b.astype(BF)
    gv_out[...] = gv[...].T.astype(BF)


def attend_back(first, count, q, k, kt, v, limit, total, grad, mixed, tables_k, tables_q):
    picks = q.shape[1]
    length = k.shape[1]
    part = GROUP * HD
    half = HD // 2
    wide = pl.BlockSpec((part, picks), lambda i: (first + i, 0))
    tall = pl.BlockSpec((1, length, HD), lambda i: (first + i, 0, 0))
    flat = pl.BlockSpec((HD, length), lambda i: (first + i, 0))
    return pl.pallas_call(
        attend_back_body,
        grid=(count,),
        in_specs=[
            wide, tall, flat, tall, whole((1, picks)),
            pl.BlockSpec((1, GROUP, picks), lambda i: (first + i, 0, 0)),
            wide, wide,
            whole((half, length)), whole((half, length)),
            whole((half, picks)), whole((half, picks)),
        ],
        out_specs=[
            pl.BlockSpec((part, picks), lambda i: (i, 0)),
            pl.BlockSpec((HD, length), lambda i: (i, 0)),
            pl.BlockSpec((HD, length), lambda i: (i, 0)),
        ],
        out_shape=[
            struct((count * part, picks), BF),
            struct((count * HD, length), BF),
            struct((count * HD, length), BF),
        ],
        scratch_shapes=[pltpu.VMEM((length, HD), F32), pltpu.VMEM((length, HD), F32)],
        compiler_params=params(),
        cost_estimate=cost(
            40 * count * part * length * picks, 8 * count * part * picks, count * GROUP * length * picks
        ),
        name="attend_back",
    )(q, k, kt, v, limit, total, grad, mixed, *tables_k, *tables_q)


def merge_body(mixed, picked, gain, w, branch, inverse_out, normed, hidden, square):
    step = pl.program_id(0)
    width = mixed.shape[0]
    part = width // pl.num_programs(0)
    rows = pl.ds(pl.multiple_of(step * part, 8), part)

    @pl.when(step == 0)
    def _():
        square[...] = jnp.zeros_like(square)

    value = dot_tn(w[0, :, w.shape[2] - part :], mixed[...])
    branch[...] = value
    total = picked[rows, :].astype(F32) + value
    hidden[rows, :] = total
    square[...] += jnp.sum(total * total, axis=0, keepdims=True)

    @pl.when(step == pl.num_programs(0) - 1)
    def _():
        inverse = lax.rsqrt(square[...] / width + EPSILON)
        inverse_out[...] = inverse
        normed[...] = (hidden[...] * inverse * gain[...]).astype(BF)


def merge(mixed, picked, gain, w):
    width, picks = mixed.shape
    blocks, _, wide = w.shape
    part = width // blocks
    return pl.pallas_call(
        merge_body,
        grid=(blocks,),
        in_specs=[
            whole((width, picks)),
            whole((width, picks)),
            whole((width, 1)),
            pl.BlockSpec((1, width, wide), lambda i: (i, 0, 0)),
        ],
        out_specs=[
            pl.BlockSpec((part, picks), lambda i: (i, 0)),
            whole((1, picks)),
            whole((width, picks)),
        ],
        out_shape=[
            struct((width, picks), F32),
            struct((1, picks), F32),
            struct((width, picks), BF),
        ],
        scratch_shapes=[pltpu.VMEM((width, picks), F32), pltpu.VMEM((1, picks), F32)],
        compiler_params=params(),
        cost_estimate=cost(2 * width * width * picks, 14 * width * picks + 2 * w.size),
        name="merge",
    )(mixed, picked, gain, w)


def down_half(part):
    return -(-part // 32) * 16


def ffn_weights(who, first, blocks, sources, w_pair, w_down, done):
    step, steps = pl.program_id(0), pl.num_programs(0)
    slot = lax.rem(step, 2)
    width, hidden = w_pair.shape[1], w_down.shape[2]
    gates, ups = slice(0, hidden), slice(hidden, 2 * hidden)

    def copies(step, at):
        turn = blocks - 1 - first - step
        block = turn ^ who[0]
        if len(sources) == 2:
            some = [
                (sources[0].at[block], w_pair.at[at]),
                (sources[1].at[block], w_down.at[at]),
            ]
        else:
            (source,) = sources
            pairs, _, columns, _, _ = source.shape
            height, part = width // pairs, width // columns
            half = down_half(part)
            some = []
            for i in range(pairs):
                place = slice(i * height, (i + 1) * height)
                some.append((source.at[i, 0, turn, :height], w_pair.at[at, place, gates]))
                some.append((source.at[i, 1, turn, :height], w_pair.at[at, place, ups]))
            for c in range(columns):
                begin = pl.multiple_of((c ^ who[0]) * part, 16)
                top = pl.ds(begin, half)
                some.append((source.at[block, 0, c, height : height + half], w_down.at[at, top]))
                end = pl.ds(pl.multiple_of(begin + half, 16), part - half)
                rest = slice(height + 2 * half - part, height + half)
                some.append((source.at[block, 1, c, rest], w_down.at[at, end]))
        return [
            pltpu.make_async_copy(source, target, done.at[at, i])
            for i, (source, target) in enumerate(some)
        ]

    @pl.when(step == 0)
    def _():
        for copy in copies(step, slot):
            copy.start()

    @pl.when(step + 1 < steps)
    def _():
        for copy in copies(step + 1, 1 - slot):
            copy.start()

    for copy in copies(step, slot):
        copy.wait()
    return slot


def ffn_scratch(width, sources):
    hidden = sources[-1].shape[-1]
    count = 2
    if len(sources) == 1:
        count = 2 * (sources[0].shape[0] + sources[0].shape[2])
    return [
        pltpu.VMEM((2, width, 2 * hidden), BF),
        pltpu.VMEM((2, width, hidden), BF),
        pltpu.SemaphoreType.DMA((2, count)),
    ]


def ffn_body(many, who, normed, branch, prob, *refs):
    sources, refs = refs[:many], refs[many:]
    gate_out, up_out, active_out, delta, both_out, forward, *buffers = refs
    w_pair, w_down, _ = buffers
    hidden = w_down.shape[2]
    slot = ffn_weights(who, 0, pl.num_programs(0), sources, *buffers)

    @pl.when(pl.program_id(0) == 0)
    def _():
        forward[...] = branch[...]

    tokens = normed[...]
    pair = dot_tn(w_pair[slot], tokens)
    gate, up = pair[:hidden], pair[hidden:]
    active = (gate * jax.nn.sigmoid(gate) * up).astype(BF)
    gate_out[0] = gate.astype(BF)
    up_out[0] = up.astype(BF)
    active_out[0] = active
    forward[...] += dot_nn(w_down[slot], active)

    @pl.when(pl.program_id(0) == pl.num_programs(0) - 1)
    def _():
        both = forward[...]
        delta[...] = (prob[...] * both).astype(BF)
        both_out[...] = both.astype(BF)


def ffn(who, normed, branch, prob, blocks, hidden, sources):
    width, picks = normed.shape
    full, row = whole((width, picks)), whole((1, picks))
    far = pl.BlockSpec(memory_space=pl.ANY)
    kept = pl.BlockSpec((1, hidden, picks), lambda i, who: (i, 0, 0))
    kept_shape = struct((blocks, hidden, picks), BF)
    low = struct((width, picks), BF)
    return pl.pallas_call(
        functools.partial(ffn_body, len(sources)),
        grid_spec=pltpu.PrefetchScalarGridSpec(
            num_scalar_prefetch=1,
            grid=(blocks,),
            in_specs=[full, full, row] + [far] * len(sources),
            out_specs=[kept] * 3 + [full, full],
            scratch_shapes=[pltpu.VMEM((width, picks), F32)] + ffn_scratch(width, sources),
        ),
        out_shape=[kept_shape] * 3 + [low, low],
        compiler_params=params(60),
        cost_estimate=cost(
            6 * width * hidden * blocks * picks, 6 * width * hidden * blocks + 8 * width * picks
        ),
        name="ffn",
    )(who, normed, branch, prob, *sources)


def down_grad_body(who, grad_ffn, active, keep, send):
    here, columns, half, lanes = keep.shape
    part = grad_ffn.shape[0] // columns
    even = who[2] == 0
    for c in range(columns):
        value = dot_nt(grad_ffn[c * part : (c + 1) * part], active[0])
        low, high = value[:half].astype(BF), value[part - half :].astype(BF)
        mine, other = jnp.where(even, low, high), jnp.where(even, high, low)
        for i in range(here):
            at = i ^ lax.rem(who[1], here) if here > 1 else 0
            keep[at, c ^ who[0]] = mine[:, i * lanes : (i + 1) * lanes]
            send[at, c ^ who[0]] = other[:, i * lanes : (i + 1) * lanes]


def down_grad(who, grad_ffn, active, pairs, columns):
    width, picks = grad_ffn.shape
    blocks, hidden, _ = active.shape
    here = pairs // blocks
    tile = (columns, down_half(width // columns), hidden // here)
    block = pl.BlockSpec(
        (here,) + tile, lambda i, who: ((blocks - 1 - i) ^ who[0] ^ lax.div(who[1], here), 0, 0, 0)
    )
    return pl.pallas_call(
        down_grad_body,
        grid_spec=pltpu.PrefetchScalarGridSpec(
            num_scalar_prefetch=1,
            grid=(blocks,),
            in_specs=[
                whole((width, picks)),
                pl.BlockSpec((1, hidden, picks), lambda i, who: (i, 0, 0)),
            ],
            out_specs=[block, block],
        ),
        out_shape=[struct((pairs,) + tile, BF)] * 2,
        compiler_params=params(),
        cost_estimate=cost(2 * blocks * hidden * width * picks, 6 * blocks * hidden * width),
        name="down_grad",
    )(who, grad_ffn, active)


def ffn_back_body(first, blocks, last, many, who, normed, grad_ffn, gate_in, up_in, *refs):
    sources, refs = refs[:many], refs[many:]
    if first:
        carried, refs = refs[0], refs[1:]
    if last:
        (branch, both_in, picked, cot, prob, inverse, gain, router), refs = refs[:8], refs[8:]
    keep_pair, send_pair, refs = refs[0], refs[1], refs[2:]
    outs, backward, buffers = refs[:-4], refs[-4], refs[-3:]
    w_pair, w_down, _ = buffers
    hidden = w_down.shape[2]
    slot = ffn_weights(who, first, blocks, sources, *buffers)
    width = normed.shape[0]
    even = who[2] == 0

    @pl.when(pl.program_id(0) == 0)
    def _():
        backward[...] = carried[...] if first else jnp.zeros_like(backward)

    pull = dot_tn(w_down[slot], grad_ffn[...])
    gate = gate_in[0].astype(F32)
    sigmoid = jax.nn.sigmoid(gate)
    silu = gate * sigmoid
    grad_gate = (pull * up_in[0].astype(F32) * (sigmoid + silu * (1.0 - sigmoid))).astype(BF)
    grad_up = (pull * silu).astype(BF)
    tokens = normed[...]
    grads = jnp.concatenate([grad_gate, grad_up], axis=0)
    backward[...] += dot_nn(w_pair[slot], grads)
    for_pair = dot_nt(tokens, grads).astype(BF)
    for_gate, for_up = for_pair[:, :hidden], for_pair[:, hidden:]
    pieces, _, height, _ = keep_pair.shape
    for i in range(pieces):
        place = slice(i * height, (i + 1) * height)
        at = i ^ who[1] if pieces > 1 else 0
        keep_pair[at, 0] = jnp.where(even, for_gate[place], for_up[place])
        send_pair[at, 0] = jnp.where(even, for_up[place], for_gate[place])

    @pl.when(pl.program_id(0) == pl.num_programs(0) - 1)
    def _():
        if not last:
            outs[0][...] = backward[...]
            return
        grad_attn, rest_out, gain_out, router_out = outs
        share = prob[...]
        cot_full = cot[...].astype(F32)
        slope = share * (1.0 - share) * jnp.sum(
            cot_full * both_in[...].astype(F32), axis=0, keepdims=True
        )
        token = picked[...].astype(F32)
        router_out[...] = jnp.sum(slope * token, axis=1, keepdims=True)
        merged = token + branch[...]
        inv = inverse[...]
        grad_norm = backward[...]
        gain_out[...] = jnp.sum(grad_norm * merged * inv, axis=1, keepdims=True)
        unit = grad_norm * gain[...]
        along = jnp.sum(unit * merged, axis=0, keepdims=True) / width
        grad_hidden = inv * unit - merged * (inv * inv * inv * along)
        grad_attn[...] = (grad_hidden + share * cot_full).astype(BF)
        rest_out[...] = (grad_hidden + slope * router[...]).astype(BF)


def ffn_back(who, first, count, last, pieces, normed, grad_ffn, gate, up, sources, carried, tail):
    width, picks = normed.shape
    hidden = gate.shape[1]
    height = width // pieces
    full, row, column = whole((width, picks)), whole((1, picks)), whole((width, 1))
    far = pl.BlockSpec(memory_space=pl.ANY)
    kept = pl.BlockSpec((1, hidden, picks), lambda i, who: (i + first, 0, 0))
    tall = pl.BlockSpec((pieces, 1, height, hidden), lambda i, who: (0, i, 0, 0))
    tall_shape = struct((pieces, count, height, hidden), BF)
    low, thin = struct((width, picks), BF), struct((width, 1), F32)
    extra = ([carried] if first else []) + (list(tail) if last else [])
    extra_specs = ([full] if first else []) + ([full] * 4 + [row] * 2 + [column] * 2 if last else [])
    return pl.pallas_call(
        functools.partial(ffn_back_body, first, gate.shape[0], last, len(sources)),
        grid_spec=pltpu.PrefetchScalarGridSpec(
            num_scalar_prefetch=1,
            grid=(count,),
            in_specs=[full, full, kept, kept] + [far] * len(sources) + extra_specs,
            out_specs=[tall, tall] + ([full, full, column, column] if last else [full]),
            scratch_shapes=[pltpu.VMEM((width, picks), F32)] + ffn_scratch(width, sources),
        ),
        out_shape=[tall_shape, tall_shape]
        + ([low, low, thin, thin] if last else [struct((width, picks), F32)]),
        compiler_params=params(60),
        cost_estimate=cost(
            10 * width * hidden * count * picks, 10 * width * hidden * count + 12 * width * picks
        ),
        name="ffn_back",
    )(who, normed, grad_ffn, gate, up, *sources, *extra)


def merge_back_body(mixed, grad, w, gw, grad_mixed, total):
    step = pl.program_id(0)
    part = gw.shape[2]
    rows = pl.ds(pl.multiple_of(step * part, 8), part)
    piece = grad[rows, :]
    gw[0] = dot_nt(mixed[...], piece).astype(BF)
    value = dot_nn(w[0, :, w.shape[2] - part :], piece)

    @pl.when(step == 0)
    def _():
        total[...] = value

    @pl.when(step > 0)
    def _():
        total[...] += value

    @pl.when(step == pl.num_programs(0) - 1)
    def _():
        grad_mixed[...] = total[...].astype(BF)


def merge_back(mixed, grad, w):
    width, picks = mixed.shape
    blocks, _, wide = w.shape
    part = width // blocks
    block = pl.BlockSpec((1, width, part), lambda i: (i, 0, 0))
    wide_block = pl.BlockSpec((1, width, wide), lambda i: (i, 0, 0))
    return pl.pallas_call(
        merge_back_body,
        grid=(blocks,),
        in_specs=[whole((width, picks)), whole((width, picks)), wide_block],
        out_specs=[block, whole((width, picks))],
        out_shape=[struct((blocks, width, part), BF), struct((width, picks), BF)],
        scratch_shapes=[pltpu.VMEM((width, picks), F32)],
        compiler_params=params(),
        cost_estimate=cost(4 * width * width * picks, 6 * width * picks + 4 * w.size),
        name="merge_back",
    )(mixed, grad, w)


def project_back_body(x, rank, gain, *refs):
    gq, gk, gv, refs = refs[:2], refs[2:4], refs[4:6], refs[6:]
    rest, w, out, grads_out, gain_out, gq_full, gkv_full, total = refs
    step = pl.program_id(0)
    width = x.shape[0]
    q_part = width // pl.num_programs(0)
    kv_part = KVH * HD // pl.num_programs(0)

    @pl.when(step == 0)
    def _():
        chosen = pick_rows(rank[...], gq[0].shape[1])
        at = 0
        for piece in gq:
            gq_full[at : at + piece.shape[0]] = dot_nn(piece[...], chosen).astype(BF)
            at += piece.shape[0]
        for i, pieces in enumerate((gk, gv)):
            at = 0
            for piece in pieces:
                gkv_full[i, at : at + piece.shape[0]] = piece[...]
                at += piece.shape[0]
        total[...] = jnp.zeros_like(total)

    q_rows = pl.ds(pl.multiple_of(step * q_part, 8), q_part)
    kv_rows = pl.ds(pl.multiple_of(step * kv_part, 8), kv_part)
    grads = jnp.concatenate(
        [gq_full[q_rows, :], gkv_full[0, kv_rows, :], gkv_full[1, kv_rows, :]], axis=0
    )
    grads_out[0] = grads
    total[...] += dot_nn(w[0, :, : grads.shape[0]], grads)

    @pl.when(step == pl.num_programs(0) - 1)
    def _():
        full = x[...].astype(F32)
        inv = lax.rsqrt(jnp.sum(full * full, axis=0, keepdims=True) / width + EPSILON)
        grad_norm = total[...]
        gain_out[...] = jnp.sum(grad_norm * full * inv, axis=1, keepdims=True)
        unit = grad_norm * gain[...]
        along = jnp.sum(unit * full, axis=0, keepdims=True) / width
        chosen = pick_rows(rank[...], rest.shape[1])
        out[...] = (
            inv * unit - full * (inv * inv * inv * along) + dot_nn(rest[...], chosen)
        ).astype(BF)


def project_back(x, rank_row, gain, gq, gk, gv, rest, w):
    width, length = x.shape
    picks = rest.shape[1]
    blocks = w.shape[0]
    kv = KVH * HD
    part = (width + 2 * kv) // blocks
    return pl.pallas_call(
        project_back_body,
        grid=(blocks,),
        in_specs=[
            whole((width, length)),
            whole((1, length)),
            whole((width, 1)),
            *(whole(piece.shape) for piece in (*gq, *gk, *gv)),
            whole((width, picks)),
            pl.BlockSpec((1,) + w.shape[1:], lambda i: (i, 0, 0)),
        ],
        out_specs=[
            whole((width, length)),
            pl.BlockSpec((1, part, length), lambda i: (i, 0, 0)),
            whole((width, 1)),
        ],
        out_shape=[
            struct((width, length), BF),
            struct((blocks, part, length), BF),
            struct((width, 1), F32),
        ],
        scratch_shapes=[
            pltpu.VMEM((width, length), BF),
            pltpu.VMEM((2, kv, length), BF),
            pltpu.VMEM((width, length), F32),
        ],
        compiler_params=params(),
        cost_estimate=cost(
            2 * width * length * (2 * picks + blocks * part), 10 * x.size + 2 * w.size
        ),
        name="project_back",
    )(x, rank_row, gain, *gq, *gk, *gv, rest, w)


def mixing_grad_body(who, x, gain, grads, gw_out, keep, send, normed):
    width = x.shape[0]
    even = who[2] == 0

    @pl.when(pl.program_id(0) == 0)
    def _():
        full = x[...].astype(F32)
        inverse = lax.rsqrt(jnp.sum(full * full, axis=0, keepdims=True) / width + EPSILON)
        normed[...] = (full * inverse * gain[...]).astype(BF)

    value = dot_nt(normed[...], grads[0])
    value = jnp.concatenate([value, gw_out[0].astype(F32)], axis=1)
    pairs = keep.shape[0]
    rows = width // (2 * pairs)
    for pair in range(pairs):
        low = value[2 * pair * rows : (2 * pair + 1) * rows]
        high = value[(2 * pair + 1) * rows : (2 * pair + 2) * rows]
        keep[pair ^ who[1], 0, :rows] = jnp.where(even, low, high).astype(BF)
        send[pair ^ who[1], 0, :rows] = jnp.where(even, high, low).astype(BF)


def mixing_grad(who, x, gain, grads, gw_out, pairs):
    width, length = x.shape
    blocks, part, _ = grads.shape
    out_part = gw_out.shape[2]
    rows = width // (2 * pairs) + VECTOR_ROWS
    split = pl.BlockSpec((pairs, 1, rows, part + out_part), lambda i, who: (0, i ^ who[0], 0, 0))
    split_shape = struct((pairs, blocks, rows, part + out_part), BF)
    return pl.pallas_call(
        mixing_grad_body,
        grid_spec=pltpu.PrefetchScalarGridSpec(
            num_scalar_prefetch=1,
            grid=(blocks,),
            in_specs=[
                whole((width, length)),
                whole((width, 1)),
                pl.BlockSpec((1, part, length), lambda i, who: (i, 0, 0)),
                pl.BlockSpec((1, width, out_part), lambda i, who: (i, 0, 0)),
            ],
            out_specs=[split, split],
            scratch_shapes=[pltpu.VMEM((width, length), BF)],
        ),
        out_shape=[split_shape, split_shape],
        compiler_params=params(),
        cost_estimate=cost(2 * width * length * blocks * part, 10 * x.size),
        name="mixing_grad",
    )(who, x, gain, grads, gw_out)


def hold(*values):
    return lax.optimization_barrier(values)


def swap(value):
    count = lax.axis_size("row")
    return lax.ppermute(value, "row", [(i, i ^ 1) for i in range(count)])


def partner(value, axis, k):
    count = lax.axis_size(axis)
    far = k if axis == "col" else 2 * k
    return lax.ppermute(value, axis, [(i, i ^ far) for i in range(count)])


def collect(value, axis, partners):
    return [partner(value, axis, k) if k else value for k in partners]


def spread(values, axis):
    return [values[0]] + [partner(value, axis, k) for k, value in enumerate(values) if k]


def add_up(values):
    return sum(value.astype(F32) for value in values)


def pack(first, second):
    if first.shape[1] == second.shape[1]:
        return [jnp.concatenate([first, second], axis=0)]
    return [first, second]


def unpack(values, rows):
    return (values[0][:rows], values[0][rows:]) if len(values) == 1 else tuple(values)


def pair_up(keep, got):
    return [add_up((a, b)).astype(BF) for a, b in zip(keep, got)]


def to_owner(value):
    copies = lax.axis_size("col") // value.shape[0]
    if copies > 1:
        value = jnp.concatenate([value] * copies, axis=0)
    moved = lax.all_to_all(value, "col", split_axis=0, concat_axis=1, tiled=True)
    return moved[0]


def from_owner(value, sequences):
    count = lax.axis_size("col")
    value = value.reshape(count, value.shape[0] // count, value.shape[1])
    moved = lax.all_to_all(value, "col", split_axis=0, concat_axis=0, tiled=True)
    return moved[:sequences]


def rope_tables(positions):
    half = HD // 2
    frequency = jnp.exp(jnp.arange(half, dtype=F32) * (-2.0 * math.log(ROPE_BASE) / HD))
    angles = frequency[:, None] * positions.astype(F32)[None, :]
    return jnp.cos(angles), jnp.sin(angles)


def on_device(
    resid, cotangent, prefix, slot, chosen, norm1_gain, norm2_gain, router,
    w_query, w_key, w_value, w_out, w_gate, w_up, w_down,
):
    col_count, row_count = lax.axis_size("col"), lax.axis_size("row")
    column = lax.axis_index("col")
    sequences, part, length = resid.shape
    width = part * col_count
    picks = chosen.shape[2]
    copies = col_count // sequences
    own = lax.rem(column, sequences)
    rows, hidden = w_gate.shape
    down_rows = w_down.shape[0]
    pairs = row_count // 2
    mixing_part = part + 2 * w_key.shape[1] + part

    own_pair_index = lax.axis_index("row") >> 1
    core = lax.axis_index("row") & 1
    even = core == 0
    who = jnp.stack([column, own_pair_index, core]).astype(jnp.int32)
    aligned = 2 * rows % 16 == 0 and hidden % 128 == 0

    half = col_count // 2

    mine = jnp.where(even, w_gate, w_up)
    other = swap(jnp.where(even, w_up, w_gate))
    pair = jnp.concatenate([jnp.where(even, mine, other), jnp.where(even, other, mine)], axis=0)
    down_rows_kept = down_half(part)
    turned = w_down.T
    low, high = turned[:down_rows_kept], turned[part - down_rows_kept :]
    mine, other = jnp.where(even, low, high), swap(jnp.where(even, high, low))
    down = jnp.concatenate([jnp.where(even, mine, other), jnp.where(even, other, mine)], axis=1)
    mixing = jnp.concatenate([w_query, w_key, w_value, w_out], axis=1)
    mixing, pair, down = hold(collect(mixing, "col", range(col_count)), pair, down)
    mixing, x = jnp.stack(mixing), resid.astype(BF)
    if aligned:
        sources = jnp.concatenate([pair, down], axis=0)
        sources, mixing, x = hold(
            collect(sources, "col", range(col_count)), collect(mixing, "row", range(pairs)), x
        )
        sources = lax.all_gather(jnp.stack(sources), "row", axis=0)
        sources = (sources.reshape((pairs, 2) + sources.shape[1:]),)
    else:
        mixing, x = hold(collect(mixing, "row", range(pairs)), x)
        pair_all = lax.all_gather(pair, ("row", "col"), axis=0)
        pair_all = pair_all.reshape(pairs, 2, col_count, 2 * rows, hidden).transpose(2, 0, 3, 1, 4)
        down_all = lax.all_gather(down, ("row", "col"), axis=0)
        down_all = down_all.reshape((col_count, pairs // col_count, 2, col_count) + down.shape)
        down_all = jnp.concatenate(
            [down_all[:, :, 0], down_all[:, :, 1, :, 2 * down_rows_kept - part :]], axis=3
        )
        sources = (
            pair_all.reshape(col_count, width, 2 * hidden),
            down_all.transpose(0, 2, 3, 1, 4).reshape(col_count, width, hidden),
        )
    every = jnp.arange(length, dtype=jnp.int32)
    chosen_of = chosen[:, 0][slot]
    selected = jnp.any(every[None, :, None] == chosen_of[:, None, :], axis=2)
    before = (every[:, None] < every[None, :]).astype(BF)
    places = jnp.dot(selected.astype(BF), before, preferred_element_type=F32)
    ranks = jnp.where(selected, places.astype(jnp.int32), -1)
    rank = lax.dynamic_index_in_dim(ranks, own, 0, keepdims=False)
    prefix_len = lax.dynamic_index_in_dim(prefix, own, 0, keepdims=False)
    place = jnp.arange(picks, dtype=jnp.int32)
    spot = jnp.sum(jnp.where(rank[None, :] == place[:, None], every[None, :], 0), axis=1)
    limit = jnp.maximum(spot, prefix_len - 1)[None, :]
    tables_k = rope_tables(every)
    tables_q = rope_tables(spot)
    gain_one, gain_two, router = norm1_gain[:, None], norm2_gain[:, None], router[:, None]
    cot = gather_tokens(cotangent, ranks[:, :, None], picks)

    x, mixing_other, mixing, cot, limit, tables_k, tables_q = hold(
        to_owner(x), [swap(piece) for piece in mixing], mixing, cot, limit, tables_k, tables_q
    )
    cot = to_owner(cot)
    if aligned:
        mixing = mixing + mixing_other
    else:
        order = jnp.arange(pairs) ^ own_pair_index
        mixing = jnp.stack([jnp.stack(mixing), jnp.stack(mixing_other)])[jnp.stack([core, 1 - core])]
        mixing = [mixing[:, order].transpose(2, 1, 0, 3, 4).reshape(col_count, width, mixing_part)]
    picked, prob, q, kt, k, vt, v, mixing = project(
        who, x, rank[:, None], gain_one, router, tables_k, tables_q, mixing
    )
    mixed, mass = attend(q, k, vt, limit)
    (branch, inverse, normed), cot = hold(merge(mixed, picked, gain_two, mixing), cot)
    gate, up, active, delta, both = ffn(who, normed, branch, prob, col_count, hidden, sources)
    grad_ffn = (prob * cot.astype(F32)).astype(BF)
    (keep_down, send_down), delta, gate = hold(
        down_grad(who, grad_ffn, active, pairs, col_count), delta, gate
    )
    delta = from_owner(delta, sequences)
    pieces = pairs if aligned else 1
    back_args = (pieces, normed, grad_ffn, gate, up, sources)
    tail = (branch, both, picked, cot, prob, inverse, gain_two, router)

    def by_pairs(value):
        if aligned:
            return value
        value = value[0].reshape(half, pairs, 2 * rows, hidden).transpose(1, 0, 2, 3)
        return value[jnp.arange(pairs) ^ own_pair_index]

    got_down, (keep_low, send_low, carried), keep_down = hold(
        swap(send_down), ffn_back(who, 0, half, False, *back_args, None, None), keep_down
    )
    sum_down = pair_up(keep_down, got_down)
    sum_down, send_low, keep_low, carried = hold(sum_down, send_low, keep_low, carried)
    (
        got_low, sum_down,
        (keep_high, send_high, grad_attn, rest, gain_two_grad, router_grad), keep_low,
    ) = hold(
        swap(send_low),
        spread(sum_down, "row"),
        ffn_back(who, half, half, True, *back_args, carried, tail),
        keep_low,
    )
    sum_low = pair_up(by_pairs(keep_low), by_pairs(got_low))
    sum_down = list(add_up(sum_down).astype(BF))
    sum_low, sum_down, send_high, keep_high, grad_attn = hold(
        sum_low, sum_down, send_high, keep_high, grad_attn
    )
    sum_low = spread(sum_low, "row")
    got_high, (gw_out, grad_mixed), keep_high = hold(
        swap(send_high), merge_back(mixed, grad_attn, mixing), keep_high
    )
    sum_high = pair_up(by_pairs(keep_high), by_pairs(got_high))
    sum_high, grad_mixed = hold(sum_high, grad_mixed)
    heads = (q, k, kt, v, limit, mass, grad_mixed, mixed, tables_k, tables_q)
    most = (KVH + 1) // 2
    sum_low, delta, one, sum_high = hold(
        sum_low, delta, attend_back(0, most, *heads), sum_high
    )
    far = [
        pack(value, sum_down[-1 - i])
        for i, value in enumerate(add_up(sum_low).astype(BF))
    ]
    far, one, grad_mixed = hold(far, one, grad_mixed)
    far = [
        [partner(value, "col", col_count - 1 - i) for value in values]
        for i, values in enumerate(far)
    ]
    heads = heads[:6] + (grad_mixed,) + heads[7:]
    sum_high = spread(sum_high, "row")
    (two,) = hold(attend_back(most, KVH - most, *heads))
    gq, gk, gv = zip(one, two)
    far, sum_high, (back, grads, gain_one_grad) = hold(
        far,
        sum_high,
        project_back(x, rank[None, :], gain_one, gq, gk, gv, rest, mixing),
    )
    *near, sum_pair = add_up(sum_high).astype(BF)
    near = [pack(value, sum_down[half - 1 - i]) for i, value in enumerate(near)]
    vectors = jnp.concatenate([gain_one_grad, gain_two_grad, router_grad], axis=1).T.astype(BF)
    vectors = vectors.reshape(3, col_count, part).transpose(1, 0, 2)
    vectors = vectors[jnp.arange(col_count) ^ column]
    vectors = jnp.pad(vectors, ((0, 0), (0, VECTOR_ROWS - 3), (0, mixing_part - part)))
    vectors = jnp.broadcast_to(vectors[None], (pairs,) + vectors.shape)
    near, back, grads, vectors = hold(near, back, grads, vectors)
    back = from_owner(back, sequences)
    near, gw_mixing = hold(
        [
            [partner(value, "col", half - 1 - i) for value in values]
            for i, values in enumerate(near)
        ],
        mixing_grad(who, x, gain_one, grads, gw_out, pairs),
    )
    keep_mixing, send_mixing = (
        lax.dynamic_update_slice(value, vectors, (0, 0, rows, 0)) for value in gw_mixing
    )
    got_mixing, block_out, keep_mixing = hold(
        swap(send_mixing), scatter_tokens(resid, delta, ranks[:, None, :]), keep_mixing
    )
    sum_mixing = add_up(spread(pair_up(keep_mixing, got_mixing), "row")).astype(BF)
    parts = [unpack(values, 2 * rows) for values in near + far]
    sum_pair = add_up([sum_pair] + [first for first, _ in parts])
    sum_down = add_up([sum_down[0]] + [second for _, second in parts])

    lanes = sum_down.shape[1] // 2
    first, second = sum_down[:, :lanes], sum_down[:, lanes:]
    mine, other = jnp.where(even, first, second), jnp.where(even, second, first)
    other = swap(other.astype(BF)).astype(F32)
    top, end = jnp.where(even, mine, other), jnp.where(even, other, mine)
    gw_down = jnp.concatenate([top, end[2 * down_rows_kept - part :]], axis=0).T

    gw_mixing = add_up(spread(list(sum_mixing), "col"))

    sum_pair = sum_pair.reshape(2, rows, hidden)
    mine = jnp.where(even, sum_pair[0], sum_pair[1])
    other = jnp.where(even, sum_pair[1], sum_pair[0]).astype(BF)
    other = swap(other).astype(F32)
    gw_gate, gw_up = jnp.where(even, mine, other), jnp.where(even, other, mine)
    if copies > 1:
        gw_gate, gw_up, gw_down, gw_mixing = (
            a / copies for a in (gw_gate, gw_up, gw_down, gw_mixing)
        )

    resid_grad = cotangent + back.astype(F32)
    kv_part = w_key.shape[1]
    ends = (part, part + kv_part, part + 2 * kv_part)
    return (
        block_out, resid_grad,
        gw_mixing[rows, :part], gw_mixing[rows + 1, :part], gw_mixing[rows + 2, :part],
        gw_mixing[:rows, : ends[0]], gw_mixing[:rows, ends[0] : ends[1]],
        gw_mixing[:rows, ends[1] : ends[2]], gw_mixing[:rows, ends[2] :],
        gw_gate, gw_up, gw_down,
    )


def solution(mesh):
    block = P("row", "col")
    placed = (
        P("row", "col", None), P("row", "col", None), P("row"), P("row"), P(None, "row", None),
        P(), P(), P(),
        block, block, block, block, block, block, block,
    )
    given = (
        P("row", "col", None), P("row", "col", None), P("col"), P("col"), P("col"),
        block, block, block, block, block, block, block,
    )
    return jax.shard_map(
        on_device, mesh=mesh, in_specs=placed, out_specs=given, check_vma=False
    )
```

```python
import functools
import math

import jax
import jax.numpy as jnp
from jax import lax
from jax.experimental import pallas as pl
from jax.experimental.pallas import tpu as pltpu
from jax.sharding import PartitionSpec as P

H = 15
KVH = 5
HD = 64
GROUP = H // KVH
QBLOCK = 256

EPSILON = 1e-05
ROPE_BASE = 10000.0
NEG = -1e30
VECTOR_ROWS = 8
LANES = 128

BF = jnp.bfloat16
F32 = jnp.float32
MIB = 1 << 20


def dot_nn(a, b):
    return lax.dot_general(a, b, (((1,), (0,)), ((), ())), preferred_element_type=F32)


def dot_tn(a, b):
    return lax.dot_general(a, b, (((0,), (0,)), ((), ())), preferred_element_type=F32)


def dot_nt(a, b):
    return lax.dot_general(a, b, (((1,), (1,)), ((), ())), preferred_element_type=F32)


def params(limit=56):
    return pltpu.CompilerParams(
        dimension_semantics=("arbitrary",), vmem_limit_bytes=limit * MIB
    )


def cost(flops, nbytes, exps=0):
    return pl.CostEstimate(
        flops=int(flops) // 32,
        bytes_accessed=int(nbytes) // 32,
        transcendentals=int(exps) // 32,
    )


def struct(shape, dtype):
    return jax.ShapeDtypeStruct(shape, dtype)


def whole(shape):
    return pl.BlockSpec(shape, lambda i, *_: (0,) * len(shape))


def pick_columns(rank_column, picks):
    place = lax.broadcasted_iota(jnp.int32, (rank_column.shape[0], picks), 1)
    return jnp.where(rank_column == place, 1.0, 0.0).astype(BF)


def pick_rows(rank_row, picks):
    place = lax.broadcasted_iota(jnp.int32, (picks, rank_row.shape[1]), 0)
    return jnp.where(rank_row == place, 1.0, 0.0).astype(BF)


def turn(first, second, cosine, sine, direction):
    signed = sine * direction
    return first * cosine - second * signed, second * cosine + first * signed


def gather_body(values, rank, out):
    chosen = pick_columns(rank[0], out.shape[2])
    out[0] = dot_nn(values[0].astype(BF), chosen).astype(BF)


def gather_tokens(values, rank_column, picks):
    count, width, length = values.shape
    return pl.pallas_call(
        gather_body,
        grid=(count,),
        in_specs=[
            pl.BlockSpec((1, width, length), lambda i: (i, 0, 0)),
            pl.BlockSpec((1, length, 1), lambda i: (i, 0, 0)),
        ],
        out_specs=pl.BlockSpec((1, width, picks), lambda i: (i, 0, 0)),
        out_shape=struct((count, width, picks), BF),
        compiler_params=params(),
        cost_estimate=cost(2 * count * width * length * picks, 6 * values.size),
        name="gather_tokens",
    )(values, rank_column)


def scatter_body(who, base, rank, *refs):
    *pieces, out = refs
    chosen = pick_rows(rank[0], pieces[0].shape[1])
    count = len(pieces)
    for k, piece in enumerate(pieces):

        @pl.when((pl.program_id(0) ^ lax.rem(who[0], count)) == k)
        def _():
            out[0] = base[0] + dot_nn(piece[...], chosen)


def scatter_tokens(who, base, pieces, rank_row):
    count, width, length = base.shape
    picks = pieces[0].shape[1]
    return pl.pallas_call(
        scatter_body,
        grid_spec=pltpu.PrefetchScalarGridSpec(
            num_scalar_prefetch=1,
            grid=(count,),
            in_specs=[
                pl.BlockSpec((1, width, length), lambda i, who: (i, 0, 0)),
                pl.BlockSpec((1, 1, length), lambda i, who: (i, 0, 0)),
            ]
            + [whole((width, picks))] * count,
            out_specs=pl.BlockSpec((1, width, length), lambda i, who: (i, 0, 0)),
        ),
        out_shape=struct(base.shape, F32),
        compiler_params=params(),
        cost_estimate=cost(2 * count * width * length * picks, 10 * base.size),
        name="scatter_tokens",
    )(who, base, rank_row, *pieces)


def join_body(who, *refs):
    *pieces, w = refs
    even = who[2] == 0
    count = len(pieces) // 2
    for k, (own, other) in enumerate(zip(pieces[:count], pieces[count:])):
        first, second = own[0].astype(F32), other[0].astype(F32)
        both = [jnp.where(even, first, second), jnp.where(even, second, first)]
        height = 2 * first.shape[0]
        place = pl.ds(pl.multiple_of((who[1] ^ k) * height, 16), height)
        w[0, place] = jnp.concatenate(both, axis=0).astype(BF)


def join(who, own, other):
    blocks, height, part = own[0].shape
    width = 2 * len(own) * height
    piece = pl.BlockSpec((1, height, part), lambda i, who: (i, 0, 0))
    return pl.pallas_call(
        join_body,
        grid_spec=pltpu.PrefetchScalarGridSpec(
            num_scalar_prefetch=1,
            grid=(blocks,),
            in_specs=[piece] * (2 * len(own)),
            out_specs=pl.BlockSpec((1, width, part), lambda i, who: (i ^ who[0], 0, 0)),
        ),
        out_shape=struct((blocks, width, part), BF),
        compiler_params=params(),
        cost_estimate=cost(0, 4 * blocks * width * part),
        name="join",
    )(who, *own, *other)


def project_body(
    x, rank, gain, router, cos_k, sin_k, cos_q, sin_q, w,
    picked, prob, q_out, kt_out, k_out, vt_out, v_out,
    normed, normed_picked, q_raw, kv_raw,
):
    step = pl.program_id(0)
    width = x.shape[0]
    q_part = width // pl.num_programs(0)
    kv_part = KVH * HD // pl.num_programs(0)

    @pl.when(step == 0)
    def _():
        full = x[...].astype(F32)
        inverse = lax.rsqrt(jnp.sum(full * full, axis=0, keepdims=True) / width + EPSILON)
        normed[...] = (full * inverse * gain[:, :1]).astype(BF)
        chosen = pick_columns(rank[:, :1], picked.shape[1])
        part = dot_nn(x[...], chosen)
        picked[...] = part.astype(BF)
        inverse = lax.rsqrt(jnp.sum(part * part, axis=0, keepdims=True) / width + EPSILON)
        normed_picked[...] = (part * inverse * gain[:, :1]).astype(BF)
        logit = jnp.sum(part * router[:, :1], axis=0, keepdims=True)
        prob[...] = jax.nn.sigmoid(logit)

    q_raw[pl.ds(pl.multiple_of(step * q_part, 8), q_part)] = dot_tn(
        w[0, :, :q_part], normed_picked[...]
    ).astype(BF)
    kv = dot_tn(w[0, :, q_part : q_part + 2 * kv_part], normed[...]).astype(BF)
    kv_raw[0, pl.ds(pl.multiple_of(step * kv_part, 8), kv_part)] = kv[:kv_part]
    kv_raw[1, pl.ds(pl.multiple_of(step * kv_part, 8), kv_part)] = kv[kv_part:]

    @pl.when(step == pl.num_programs(0) - 1)
    def _():
        half = HD // 2
        for head in range(H):
            at = head * HD
            a, b = turn(
                q_raw[at : at + half].astype(F32),
                q_raw[at + half : at + HD].astype(F32),
                cos_q[...], sin_q[...], 1.0,
            )
            scale = HD ** (-0.5)
            q_out[at : at + half] = (a.astype(BF).astype(F32) * scale).astype(BF)
            q_out[at + half : at + HD] = (b.astype(BF).astype(F32) * scale).astype(BF)
        for head in range(KVH):
            at = head * HD
            a, b = turn(
                kv_raw[0, at : at + half].astype(F32),
                kv_raw[0, at + half : at + HD].astype(F32),
                cos_k[...], sin_k[...], 1.0,
            )
            turned = jnp.concatenate([a, b], axis=0)
            kt_out[at : at + HD] = turned.astype(BF)
            k_out[head] = turned.T.astype(BF)
            value = kv_raw[1, at : at + HD]
            vt_out[at : at + HD] = value
            v_out[head] = value.astype(F32).T.astype(BF)


def project(x, rank_column, gain, router, tables_k, tables_q, w):
    width, length = x.shape
    picks = tables_q[0].shape[1]
    blocks, _, part = w.shape
    kv = KVH * HD
    half = HD // 2
    return pl.pallas_call(
        project_body,
        grid=(blocks,),
        in_specs=[
            whole((width, length)),
            whole((length, LANES)),
            whole((width, LANES)),
            whole((width, LANES)),
            whole((half, length)),
            whole((half, length)),
            whole((half, picks)),
            whole((half, picks)),
            pl.BlockSpec((1, width, part), lambda i: (i, 0, 0)),
        ],
        out_specs=[
            whole((width, picks)),
            whole((1, picks)),
            whole((width, picks)),
            whole((kv, length)),
            whole((KVH, length, HD)),
            whole((kv, length)),
            whole((KVH, length, HD)),
        ],
        scratch_shapes=[
            pltpu.VMEM((width, length), BF),
            pltpu.VMEM((width, picks), BF),
            pltpu.VMEM((width, picks), BF),
            pltpu.VMEM((2, kv, length), BF),
        ],
        out_shape=[
            struct((width, picks), BF),
            struct((1, picks), F32),
            struct((width, picks), BF),
            struct((kv, length), BF),
            struct((KVH, length, HD), BF),
            struct((kv, length), BF),
            struct((KVH, length, HD), BF),
        ],
        compiler_params=params(),
        cost_estimate=cost(
            2 * width * (length * picks + picks * width + length * 2 * kv),
            2 * (2 * blocks * width * part + 4 * x.size),
        ),
        name="project",
    )(x, rank_column, gain, router, *tables_k, *tables_q, w)


def reach_of(block, length, picks):
    return max((block + 1) * QBLOCK + length - picks, length // 2)


def clear_of(block):
    return block * QBLOCK


def block_scores(q, k, limit, block, reach):
    scores = dot_nn(k[:reach], q)
    clear = clear_of(block)
    tail = scores[clear:] if clear else scores
    key = lax.broadcasted_iota(jnp.int32, tail.shape, 0) + clear
    tail = jnp.where(key <= limit, tail, NEG)
    return jnp.concatenate([scores[:clear], tail], axis=0) if clear else tail


def side_by_side(value, cols):
    return jnp.concatenate(
        [value[head * HD : (head + 1) * HD, cols] for head in range(GROUP)], axis=1
    )


def attend_body(q, k, vt, limit, out, total):
    length = k.shape[1]
    picks = q.shape[1]
    for block in range(picks // QBLOCK):
        cols = slice(block * QBLOCK, (block + 1) * QBLOCK)
        reach = reach_of(block, length, picks)
        limits = jnp.concatenate([limit[:, cols]] * GROUP, axis=1)
        scores = block_scores(side_by_side(q, cols), k[0], limits, block, reach)
        top = jnp.max(scores, axis=0, keepdims=True)
        weight = jnp.exp(scores - top)
        mass = jnp.sum(weight, axis=0, keepdims=True)
        mixed = (dot_nn(vt[:, :reach], weight.astype(BF)) / mass).astype(BF)
        logs = top + jnp.log(mass)
        for head in range(GROUP):
            part = slice(head * QBLOCK, (head + 1) * QBLOCK)
            out[head * HD : (head + 1) * HD, cols] = mixed[:, part]
            total[0, head : head + 1, cols] = logs[:, part]


def attend(q, k, vt, limit):
    width, picks = q.shape
    length = k.shape[1]
    part = GROUP * HD
    return pl.pallas_call(
        attend_body,
        grid=(KVH,),
        in_specs=[
            pl.BlockSpec((part, picks), lambda i: (i, 0)),
            pl.BlockSpec((1, length, HD), lambda i: (i, 0, 0)),
            pl.BlockSpec((HD, length), lambda i: (i, 0)),
            whole((1, picks)),
        ],
        out_specs=[
            pl.BlockSpec((part, picks), lambda i: (i, 0)),
            pl.BlockSpec((1, GROUP, picks), lambda i: (i, 0, 0)),
        ],
        out_shape=[struct((width, picks), BF), struct((KVH, GROUP, picks), F32)],
        compiler_params=params(),
        cost_estimate=cost(
            16 * width * length * picks, 4 * width * picks, H * length * picks
        ),
        name="attend",
    )(q, k, vt, limit)


def attend_back_body(
    q, k, kt, v, limit, total, grad, mixed, cos_k, sin_k, cos_q, sin_q,
    gq_out, gk_out, gv_out, gk, gv,
):
    length = k.shape[1]
    picks = q.shape[1]
    half = HD // 2
    gk[...] = jnp.zeros_like(gk)
    gv[...] = jnp.zeros_like(gv)
    for block in range(picks // QBLOCK):
        cols = slice(block * QBLOCK, (block + 1) * QBLOCK)
        reach = reach_of(block, length, picks)
        limits = jnp.concatenate([limit[:, cols]] * GROUP, axis=1)
        q_part, g_part = side_by_side(q, cols), side_by_side(grad, cols)
        scores = block_scores(q_part, k[0], limits, block, reach)
        logs = jnp.concatenate([total[0, head : head + 1, cols] for head in range(GROUP)], axis=1)
        weight = jnp.exp(scores - logs)
        delta = jnp.sum(
            g_part.astype(F32) * side_by_side(mixed, cols).astype(F32), axis=0, keepdims=True
        )
        pull = dot_nn(v[0, :reach], g_part)
        back = (weight * (pull - delta)).astype(BF)
        gq = dot_nn(kt[:, :reach], back) * HD ** (-0.5)
        gk[:reach] += dot_nt(back, q_part)
        gv[:reach] += dot_nt(weight.astype(BF), g_part)
        for head in range(GROUP):
            part = slice(head * QBLOCK, (head + 1) * QBLOCK)
            a, b = turn(gq[:half, part], gq[half:, part], cos_q[:, cols], sin_q[:, cols], -1.0)
            gq_out[head * HD : head * HD + half, cols] = a.astype(BF)
            gq_out[head * HD + half : (head + 1) * HD, cols] = b.astype(BF)
    turned = gk[...].T
    a, b = turn(turned[:half], turned[half:], cos_k[...], sin_k[...], -1.0)
    gk_out[:half] = a.astype(BF)
    gk_out[half:] = b.astype(BF)
    gv_out[...] = gv[...].T.astype(BF)


def attend_back(first, count, q, k, kt, v, limit, total, grad, mixed, tables_k, tables_q):
    picks = q.shape[1]
    length = k.shape[1]
    part = GROUP * HD
    half = HD // 2
    wide = pl.BlockSpec((part, picks), lambda i: (first + i, 0))
    tall = pl.BlockSpec((1, length, HD), lambda i: (first + i, 0, 0))
    flat = pl.BlockSpec((HD, length), lambda i: (first + i, 0))
    return pl.pallas_call(
        attend_back_body,
        grid=(count,),
        in_specs=[
            wide, tall, flat, tall, whole((1, picks)),
            pl.BlockSpec((1, GROUP, picks), lambda i: (first + i, 0, 0)),
            wide, wide,
            whole((half, length)), whole((half, length)),
            whole((half, picks)), whole((half, picks)),
        ],
        out_specs=[
            pl.BlockSpec((part, picks), lambda i: (i, 0)),
            pl.BlockSpec((HD, length), lambda i: (i, 0)),
            pl.BlockSpec((HD, length), lambda i: (i, 0)),
        ],
        out_shape=[
            struct((count * part, picks), BF),
            struct((count * HD, length), BF),
            struct((count * HD, length), BF),
        ],
        scratch_shapes=[pltpu.VMEM((length, HD), F32), pltpu.VMEM((length, HD), F32)],
        compiler_params=params(),
        cost_estimate=cost(
            40 * count * part * length * picks, 8 * count * part * picks, count * GROUP * length * picks
        ),
        name="attend_back",
    )(q, k, kt, v, limit, total, grad, mixed, *tables_k, *tables_q)


def merge_body(mixed, picked, gain, w, branch, inverse_out, normed, hidden, square):
    step = pl.program_id(0)
    width = mixed.shape[0]
    part = width // pl.num_programs(0)
    rows = pl.ds(pl.multiple_of(step * part, 8), part)

    @pl.when(step == 0)
    def _():
        square[...] = jnp.zeros_like(square)

    value = dot_tn(w[0, :, w.shape[2] - part :], mixed[...])
    branch[...] = value
    total = picked[rows, :].astype(F32) + value
    hidden[rows, :] = total
    square[...] += jnp.sum(total * total, axis=0, keepdims=True)

    @pl.when(step == pl.num_programs(0) - 1)
    def _():
        inverse = lax.rsqrt(square[...] / width + EPSILON)
        inverse_out[...] = inverse
        normed[...] = (hidden[...] * inverse * gain[:, :1]).astype(BF)


def merge(mixed, picked, gain, w):
    width, picks = mixed.shape
    blocks, _, wide = w.shape
    part = width // blocks
    return pl.pallas_call(
        merge_body,
        grid=(blocks,),
        in_specs=[
            whole((width, picks)),
            whole((width, picks)),
            whole((width, LANES)),
            pl.BlockSpec((1, width, wide), lambda i: (i, 0, 0)),
        ],
        out_specs=[
            pl.BlockSpec((part, picks), lambda i: (i, 0)),
            whole((1, picks)),
            whole((width, picks)),
        ],
        out_shape=[
            struct((width, picks), F32),
            struct((1, picks), F32),
            struct((width, picks), BF),
        ],
        scratch_shapes=[pltpu.VMEM((width, picks), F32), pltpu.VMEM((1, picks), F32)],
        compiler_params=params(),
        cost_estimate=cost(2 * width * width * picks, 14 * width * picks + 2 * w.size),
        name="merge",
    )(mixed, picked, gain, w)


def down_half(part):
    return -(-part // 32) * 16


def ffn_weights(who, first, blocks, sources, w_pair, w_down, done):
    step, steps = pl.program_id(0), pl.num_programs(0)
    slot = lax.rem(step, 2)
    width, hidden = w_pair.shape[1], w_down.shape[2]
    gates, ups = slice(0, hidden), slice(hidden, 2 * hidden)

    def copies(step, at):
        turn = blocks - 1 - first - step
        block = turn ^ who[0]
        if len(sources) == 2:
            some = [
                (sources[0].at[block], w_pair.at[at]),
                (sources[1].at[block], w_down.at[at]),
            ]
        else:
            (source,) = sources
            pairs, _, columns, _, _ = source.shape
            height, part = width // pairs, width // columns
            half = down_half(part)
            some = []
            for i in range(pairs):
                place = slice(i * height, (i + 1) * height)
                some.append((source.at[i, 0, turn, :height], w_pair.at[at, place, gates]))
                some.append((source.at[i, 1, turn, :height], w_pair.at[at, place, ups]))
            for c in range(columns):
                begin = pl.multiple_of((c ^ who[0]) * part, 16)
                top = pl.ds(begin, half)
                some.append((source.at[block, 0, c, height : height + half], w_down.at[at, top]))
                end = pl.ds(pl.multiple_of(begin + half, 16), part - half)
                rest = slice(height + 2 * half - part, height + half)
                some.append((source.at[block, 1, c, rest], w_down.at[at, end]))
        return [
            pltpu.make_async_copy(source, target, done.at[at, i])
            for i, (source, target) in enumerate(some)
        ]

    @pl.when(step == 0)
    def _():
        for copy in copies(step, slot):
            copy.start()

    @pl.when(step + 1 < steps)
    def _():
        for copy in copies(step + 1, 1 - slot):
            copy.start()

    for copy in copies(step, slot):
        copy.wait()
    return slot


def ffn_scratch(width, sources):
    hidden = sources[-1].shape[-1]
    count = 2
    if len(sources) == 1:
        count = 2 * (sources[0].shape[0] + sources[0].shape[2])
    return [
        pltpu.VMEM((2, width, 2 * hidden), BF),
        pltpu.VMEM((2, width, hidden), BF),
        pltpu.SemaphoreType.DMA((2, count)),
    ]


def ffn_body(many, who, normed, branch, prob, *refs):
    sources, refs = refs[:many], refs[many:]
    gate_out, up_out, active_out, delta, both_out, forward, *buffers = refs
    w_pair, w_down, _ = buffers
    hidden = w_down.shape[2]
    slot = ffn_weights(who, 0, pl.num_programs(0), sources, *buffers)

    @pl.when(pl.program_id(0) == 0)
    def _():
        forward[...] = branch[...]

    tokens = normed[...]
    pair = dot_tn(w_pair[slot], tokens)
    gate, up = pair[:hidden], pair[hidden:]
    active = (gate * jax.nn.sigmoid(gate) * up).astype(BF)
    gate_out[0] = gate.astype(BF)
    up_out[0] = up.astype(BF)
    active_out[0] = active
    forward[...] += dot_nn(w_down[slot], active)

    @pl.when(pl.program_id(0) == pl.num_programs(0) - 1)
    def _():
        both = forward[...]
        delta[...] = (prob[...] * both).astype(BF)
        both_out[...] = both.astype(BF)


def ffn(who, normed, branch, prob, blocks, hidden, sources):
    width, picks = normed.shape
    full, row = whole((width, picks)), whole((1, picks))
    far = pl.BlockSpec(memory_space=pl.ANY)
    kept = pl.BlockSpec((1, hidden, picks), lambda i, who: (i, 0, 0))
    kept_shape = struct((blocks, hidden, picks), BF)
    low = struct((width, picks), BF)
    return pl.pallas_call(
        functools.partial(ffn_body, len(sources)),
        grid_spec=pltpu.PrefetchScalarGridSpec(
            num_scalar_prefetch=1,
            grid=(blocks,),
            in_specs=[full, full, row] + [far] * len(sources),
            out_specs=[kept] * 3 + [full, full],
            scratch_shapes=[pltpu.VMEM((width, picks), F32)] + ffn_scratch(width, sources),
        ),
        out_shape=[kept_shape] * 3 + [low, low],
        compiler_params=params(60),
        cost_estimate=cost(
            6 * width * hidden * blocks * picks, 6 * width * hidden * blocks + 8 * width * picks
        ),
        name="ffn",
    )(who, normed, branch, prob, *sources)


def down_grad_body(who, grad_ffn, active, keep, send):
    here, columns, half, lanes = keep.shape
    part = grad_ffn.shape[0] // columns
    even = who[2] == 0
    for c in range(columns):
        value = dot_nt(grad_ffn[c * part : (c + 1) * part], active[0])
        low, high = value[:half].astype(BF), value[part - half :].astype(BF)
        mine, other = jnp.where(even, low, high), jnp.where(even, high, low)
        for i in range(here):
            at = i ^ lax.rem(who[1], here) if here > 1 else 0
            keep[at, c ^ who[0]] = mine[:, i * lanes : (i + 1) * lanes]
            send[at, c ^ who[0]] = other[:, i * lanes : (i + 1) * lanes]


def down_grad(who, grad_ffn, active, pairs, columns):
    width, picks = grad_ffn.shape
    blocks, hidden, _ = active.shape
    here = pairs // blocks
    tile = (columns, down_half(width // columns), hidden // here)
    block = pl.BlockSpec(
        (here,) + tile, lambda i, who: ((blocks - 1 - i) ^ who[0] ^ lax.div(who[1], here), 0, 0, 0)
    )
    return pl.pallas_call(
        down_grad_body,
        grid_spec=pltpu.PrefetchScalarGridSpec(
            num_scalar_prefetch=1,
            grid=(blocks,),
            in_specs=[
                whole((width, picks)),
                pl.BlockSpec((1, hidden, picks), lambda i, who: (i, 0, 0)),
            ],
            out_specs=[block, block],
        ),
        out_shape=[struct((pairs,) + tile, BF)] * 2,
        compiler_params=params(),
        cost_estimate=cost(2 * blocks * hidden * width * picks, 6 * blocks * hidden * width),
        name="down_grad",
    )(who, grad_ffn, active)


def ffn_back_body(first, blocks, last, many, who, normed, grad_ffn, gate_in, up_in, *refs):
    sources, refs = refs[:many], refs[many:]
    if first:
        carried, refs = refs[0], refs[1:]
    if last:
        (branch, both_in, picked, cot, prob, inverse, gain, router), refs = refs[:8], refs[8:]
    keep_pair, send_pair, refs = refs[0], refs[1], refs[2:]
    outs, backward, buffers = refs[:-4], refs[-4], refs[-3:]
    w_pair, w_down, _ = buffers
    hidden = w_down.shape[2]
    slot = ffn_weights(who, first, blocks, sources, *buffers)
    width = normed.shape[0]
    even = who[2] == 0

    @pl.when(pl.program_id(0) == 0)
    def _():
        backward[...] = carried[...] if first else jnp.zeros_like(backward)

    pull = dot_tn(w_down[slot], grad_ffn[...])
    gate = gate_in[0].astype(F32)
    sigmoid = jax.nn.sigmoid(gate)
    silu = gate * sigmoid
    grad_gate = (pull * up_in[0].astype(F32) * (sigmoid + silu * (1.0 - sigmoid))).astype(BF)
    grad_up = (pull * silu).astype(BF)
    tokens = normed[...]
    grads = jnp.concatenate([grad_gate, grad_up], axis=0)
    backward[...] += dot_nn(w_pair[slot], grads)
    for_pair = dot_nt(tokens, grads).astype(BF)
    for_gate, for_up = for_pair[:, :hidden], for_pair[:, hidden:]
    pieces, _, height, _ = keep_pair.shape
    for i in range(pieces):
        place = slice(i * height, (i + 1) * height)
        at = i ^ who[1] if pieces > 1 else 0
        keep_pair[at, 0] = jnp.where(even, for_gate[place], for_up[place])
        send_pair[at, 0] = jnp.where(even, for_up[place], for_gate[place])

    @pl.when(pl.program_id(0) == pl.num_programs(0) - 1)
    def _():
        if not last:
            outs[0][...] = backward[...]
            return
        grad_attn, rest_out, gain_out, router_out = outs
        share = prob[...]
        cot_full = cot[...].astype(F32)
        slope = share * (1.0 - share) * jnp.sum(
            cot_full * both_in[...].astype(F32), axis=0, keepdims=True
        )
        token = picked[...].astype(F32)
        router_out[...] = jnp.sum(slope * token, axis=1, keepdims=True)
        merged = token + branch[...]
        inv = inverse[...]
        grad_norm = backward[...]
        gain_out[...] = jnp.sum(grad_norm * merged * inv, axis=1, keepdims=True)
        unit = grad_norm * gain[:, :1]
        along = jnp.sum(unit * merged, axis=0, keepdims=True) / width
        grad_hidden = inv * unit - merged * (inv * inv * inv * along)
        grad_attn[...] = (grad_hidden + share * cot_full).astype(BF)
        rest_out[...] = (grad_hidden + slope * router[:, :1]).astype(BF)


def ffn_back(who, first, count, last, pieces, normed, grad_ffn, gate, up, sources, carried, tail):
    width, picks = normed.shape
    hidden = gate.shape[1]
    height = width // pieces
    full, row, column = whole((width, picks)), whole((1, picks)), whole((width, 1))
    far = pl.BlockSpec(memory_space=pl.ANY)
    kept = pl.BlockSpec((1, hidden, picks), lambda i, who: (i + first, 0, 0))
    tall = pl.BlockSpec((pieces, 1, height, hidden), lambda i, who: (0, i, 0, 0))
    tall_shape = struct((pieces, count, height, hidden), BF)
    low, thin = struct((width, picks), BF), struct((width, 1), F32)
    extra = ([carried] if first else []) + (list(tail) if last else [])
    extra_specs = ([full] if first else []) + ([full] * 4 + [row] * 2 + [whole((width, LANES))] * 2 if last else [])
    return pl.pallas_call(
        functools.partial(ffn_back_body, first, gate.shape[0], last, len(sources)),
        grid_spec=pltpu.PrefetchScalarGridSpec(
            num_scalar_prefetch=1,
            grid=(count,),
            in_specs=[full, full, kept, kept] + [far] * len(sources) + extra_specs,
            out_specs=[tall, tall] + ([full, full, column, column] if last else [full]),
            scratch_shapes=[pltpu.VMEM((width, picks), F32)] + ffn_scratch(width, sources),
        ),
        out_shape=[tall_shape, tall_shape]
        + ([low, low, thin, thin] if last else [struct((width, picks), F32)]),
        compiler_params=params(60),
        cost_estimate=cost(
            10 * width * hidden * count * picks, 10 * width * hidden * count + 12 * width * picks
        ),
        name="ffn_back",
    )(who, normed, grad_ffn, gate, up, *sources, *extra)


def merge_back_body(mixed, grad, w, gw, grad_mixed, total):
    step = pl.program_id(0)
    part = gw.shape[2]
    rows = pl.ds(pl.multiple_of(step * part, 8), part)
    piece = grad[rows, :]
    gw[0] = dot_nt(mixed[...], piece).astype(BF)
    value = dot_nn(w[0, :, w.shape[2] - part :], piece)

    @pl.when(step == 0)
    def _():
        total[...] = value

    @pl.when(step > 0)
    def _():
        total[...] += value

    @pl.when(step == pl.num_programs(0) - 1)
    def _():
        grad_mixed[...] = total[...].astype(BF)


def merge_back(mixed, grad, w):
    width, picks = mixed.shape
    blocks, _, wide = w.shape
    part = width // blocks
    block = pl.BlockSpec((1, width, part), lambda i: (i, 0, 0))
    wide_block = pl.BlockSpec((1, width, wide), lambda i: (i, 0, 0))
    return pl.pallas_call(
        merge_back_body,
        grid=(blocks,),
        in_specs=[whole((width, picks)), whole((width, picks)), wide_block],
        out_specs=[block, whole((width, picks))],
        out_shape=[struct((blocks, width, part), BF), struct((width, picks), BF)],
        scratch_shapes=[pltpu.VMEM((width, picks), F32)],
        compiler_params=params(),
        cost_estimate=cost(4 * width * width * picks, 6 * width * picks + 4 * w.size),
        name="merge_back",
    )(mixed, grad, w)


def mixing_grad_body(
    who, x, rank, gain, *refs
):
    gq, gk, gv, refs = refs[:2], refs[2:4], refs[4:6], refs[6:]
    gw_out, w, keep, send, grads_out, gain_out, normed, gq_full, gkv_full = refs
    step = pl.program_id(0)
    width = x.shape[0]
    q_part = width // pl.num_programs(0)
    kv_part = KVH * HD // pl.num_programs(0)
    even = who[2] == 0

    @pl.when(step == 0)
    def _():
        full = x[...].astype(F32)
        inverse = lax.rsqrt(jnp.sum(full * full, axis=0, keepdims=True) / width + EPSILON)
        normed[...] = (full * inverse * gain[:, :1]).astype(BF)
        chosen = pick_rows(rank[...], gq[0].shape[1])
        at = 0
        for piece in gq:
            gq_full[at : at + piece.shape[0]] = dot_nn(piece[...], chosen).astype(BF)
            at += piece.shape[0]
        for i, pieces in enumerate((gk, gv)):
            at = 0
            for piece in pieces:
                gkv_full[i, at : at + piece.shape[0]] = piece[...]
                at += piece.shape[0]

    q_rows = pl.ds(pl.multiple_of(step * q_part, 8), q_part)
    kv_rows = pl.ds(pl.multiple_of(step * kv_part, 8), kv_part)
    grads = jnp.concatenate(
        [gq_full[q_rows, :], gkv_full[0, kv_rows, :], gkv_full[1, kv_rows, :]], axis=0
    )
    grads_out[0] = grads
    value = dot_nt(normed[...], grads)
    share = jnp.sum(
        value * w[0, :, : grads.shape[0]].astype(F32), axis=1, keepdims=True
    ) / gain[:, :1]
    gain_out[...] = jnp.where(step == 0, share, gain_out[...] + share)
    value = jnp.concatenate([value, gw_out[0].astype(F32)], axis=1)
    pairs = keep.shape[0]
    rows = width // (2 * pairs)
    for pair in range(pairs):
        low = value[2 * pair * rows : (2 * pair + 1) * rows]
        high = value[(2 * pair + 1) * rows : (2 * pair + 2) * rows]
        keep[pair ^ who[1], 0, :rows] = jnp.where(even, low, high).astype(BF)
        send[pair ^ who[1], 0, :rows] = jnp.where(even, high, low).astype(BF)


def mixing_grad(who, x, rank_row, gain, gq, gk, gv, gw_out, w, pairs):
    width, length = x.shape
    picks = gq[0].shape[1]
    blocks, _, out_part = gw_out.shape
    kv = KVH * HD
    part = (width + 2 * kv) // blocks
    rows = width // (2 * pairs) + VECTOR_ROWS
    split = pl.BlockSpec((pairs, 1, rows, part + out_part), lambda i, who: (0, i ^ who[0], 0, 0))
    split_shape = struct((pairs, blocks, rows, part + out_part), BF)
    return pl.pallas_call(
        mixing_grad_body,
        grid_spec=pltpu.PrefetchScalarGridSpec(
            num_scalar_prefetch=1,
            grid=(blocks,),
            in_specs=[
                whole((width, length)),
                whole((1, length)),
                whole((width, LANES)),
                *(whole(piece.shape) for piece in (*gq, *gk, *gv)),
                pl.BlockSpec((1, width, out_part), lambda i, who: (i, 0, 0)),
                pl.BlockSpec((1,) + w.shape[1:], lambda i, who: (i, 0, 0)),
            ],
            out_specs=[
                split,
                split,
                pl.BlockSpec((1, part, length), lambda i, who: (i, 0, 0)),
                whole((width, 1)),
            ],
            scratch_shapes=[
                pltpu.VMEM((width, length), BF),
                pltpu.VMEM((width, length), BF),
                pltpu.VMEM((2, kv, length), BF),
            ],
        ),
        out_shape=[
            split_shape,
            split_shape,
            struct((blocks, part, length), BF),
            struct((width, 1), F32),
        ],
        compiler_params=params(),
        cost_estimate=cost(2 * width * length * (picks + width + 2 * kv), 10 * x.size),
        name="mixing_grad",
    )(who, x, rank_row, gain, *gq, *gk, *gv, gw_out, w)


def project_back_body(x, rank, gain, grads, rest, w, out, total):
    step = pl.program_id(0)
    width = x.shape[0]
    part = grads.shape[1]

    @pl.when(step == 0)
    def _():
        total[...] = jnp.zeros_like(total)

    total[...] += dot_nn(w[0, :, :part], grads[0])

    @pl.when(step == pl.num_programs(0) - 1)
    def _():
        full = x[...].astype(F32)
        inv = lax.rsqrt(jnp.sum(full * full, axis=0, keepdims=True) / width + EPSILON)
        grad_norm = total[...]
        unit = grad_norm * gain[:, :1]
        along = jnp.sum(unit * full, axis=0, keepdims=True) / width
        chosen = pick_rows(rank[...], rest.shape[1])
        out[...] = (
            inv * unit - full * (inv * inv * inv * along) + dot_nn(rest[...], chosen)
        ).astype(BF)


def project_back(x, rank_row, gain, grads, rest, w):
    width, length = x.shape
    picks = rest.shape[1]
    blocks, part, _ = grads.shape
    return pl.pallas_call(
        project_back_body,
        grid=(blocks,),
        in_specs=[
            whole((width, length)),
            whole((1, length)),
            whole((width, LANES)),
            pl.BlockSpec((1, part, length), lambda i: (i, 0, 0)),
            whole((width, picks)),
            pl.BlockSpec((1,) + w.shape[1:], lambda i: (i, 0, 0)),
        ],
        out_specs=whole((width, length)),
        out_shape=struct((width, length), BF),
        scratch_shapes=[pltpu.VMEM((width, length), F32)],
        compiler_params=params(),
        cost_estimate=cost(2 * width * length * (picks + blocks * part), 10 * x.size + 2 * w.size),
        name="project_back",
    )(x, rank_row, gain, grads, rest, w)


def columns(value):
    return jnp.broadcast_to(value[:, None], (value.shape[0], LANES))


def hold(*values):
    return lax.optimization_barrier(values)


def swap(value):
    count = lax.axis_size("row")
    return lax.ppermute(value, "row", [(i, i ^ 1) for i in range(count)])


def partner(value, axis, k):
    count = lax.axis_size(axis)
    far = k if axis == "col" else 2 * k
    return lax.ppermute(value, axis, [(i, i ^ far) for i in range(count)])


def collect(value, axis, partners):
    return [partner(value, axis, k) if k else value for k in partners]


def spread(values, axis):
    return [values[0]] + [partner(value, axis, k) for k, value in enumerate(values) if k]


def add_up(values):
    return sum(value.astype(F32) for value in values)


def pack(first, second):
    if first.shape[1] == second.shape[1]:
        return [jnp.concatenate([first, second], axis=0)]
    return [first, second]


def unpack(values, rows):
    return (values[0][:rows], values[0][rows:]) if len(values) == 1 else tuple(values)


def pair_up(keep, got):
    return [add_up((a, b)).astype(BF) for a, b in zip(keep, got)]


def to_owner(value):
    copies = lax.axis_size("col") // value.shape[0]
    if copies > 1:
        value = jnp.concatenate([value] * copies, axis=0)
    moved = lax.all_to_all(value, "col", split_axis=0, concat_axis=1, tiled=True)
    return moved[0]


def from_owner(value, sequences):
    count = lax.axis_size("col")
    value = value.reshape(count, value.shape[0] // count, value.shape[1])
    moved = lax.all_to_all(value, "col", split_axis=0, concat_axis=0, tiled=True)
    return moved[:sequences]


def rope_tables(positions):
    half = HD // 2
    frequency = jnp.exp(jnp.arange(half, dtype=F32) * (-2.0 * math.log(ROPE_BASE) / HD))
    angles = frequency[:, None] * positions.astype(F32)[None, :]
    return jnp.cos(angles), jnp.sin(angles)


def on_device(
    resid, cotangent, prefix, slot, chosen, norm1_gain, norm2_gain, router,
    w_query, w_key, w_value, w_out, w_gate, w_up, w_down,
):
    col_count, row_count = lax.axis_size("col"), lax.axis_size("row")
    column = lax.axis_index("col")
    sequences, part, length = resid.shape
    width = part * col_count
    picks = chosen.shape[2]
    copies = col_count // sequences
    own = lax.rem(column, sequences)
    rows, hidden = w_gate.shape
    down_rows = w_down.shape[0]
    pairs = row_count // 2
    mixing_part = part + 2 * w_key.shape[1] + part

    own_pair_index = lax.axis_index("row") >> 1
    core = lax.axis_index("row") & 1
    even = core == 0
    who = jnp.stack([column, own_pair_index, core]).astype(jnp.int32)
    aligned = 2 * rows % 16 == 0 and hidden % 128 == 0

    half = col_count // 2

    mine = jnp.where(even, w_gate, w_up)
    other = swap(jnp.where(even, w_up, w_gate))
    pair = jnp.concatenate([jnp.where(even, mine, other), jnp.where(even, other, mine)], axis=0)
    down_rows_kept = down_half(part)
    turned = w_down.T
    low, high = turned[:down_rows_kept], turned[part - down_rows_kept :]
    mine, other = jnp.where(even, low, high), swap(jnp.where(even, high, low))
    down = jnp.concatenate([jnp.where(even, mine, other), jnp.where(even, other, mine)], axis=1)
    mixing = jnp.concatenate([w_query, w_key, w_value, w_out], axis=1)
    mixing, pair, down = hold(collect(mixing, "col", range(col_count)), pair, down)
    mixing, x = jnp.stack(mixing), resid.astype(BF)
    if aligned:
        sources = jnp.concatenate([pair, down], axis=0)
        sources, mixing, x = hold(
            collect(sources, "col", range(col_count)), collect(mixing, "row", range(pairs)), x
        )
        sources = lax.all_gather(jnp.stack(sources), "row", axis=0)
        sources = (sources.reshape((pairs, 2) + sources.shape[1:]),)
    else:
        mixing, x = hold(collect(mixing, "row", range(pairs)), x)
        pair_all = lax.all_gather(pair, ("row", "col"), axis=0)
        pair_all = pair_all.reshape(pairs, 2, col_count, 2 * rows, hidden).transpose(2, 0, 3, 1, 4)
        down_all = lax.all_gather(down, ("row", "col"), axis=0)
        down_all = down_all.reshape((col_count, pairs // col_count, 2, col_count) + down.shape)
        down_all = jnp.concatenate(
            [down_all[:, :, 0], down_all[:, :, 1, :, 2 * down_rows_kept - part :]], axis=3
        )
        sources = (
            pair_all.reshape(col_count, width, 2 * hidden),
            down_all.transpose(0, 2, 3, 1, 4).reshape(col_count, width, hidden),
        )
    every = jnp.arange(length, dtype=jnp.int32)
    chosen_of = chosen[:, 0][slot]
    selected = jnp.any(every[None, :, None] == chosen_of[:, None, :], axis=2)
    before = (every[:, None] < every[None, :]).astype(BF)
    places = jnp.dot(selected.astype(BF), before, preferred_element_type=F32)
    ranks = jnp.where(selected, places.astype(jnp.int32), -1)
    rank = lax.dynamic_index_in_dim(ranks, own, 0, keepdims=False)
    prefix_len = lax.dynamic_index_in_dim(prefix, own, 0, keepdims=False)
    place = jnp.arange(picks, dtype=jnp.int32)
    spot = jnp.sum(jnp.where(rank[None, :] == place[:, None], every[None, :], 0), axis=1)
    limit = jnp.maximum(spot, prefix_len - 1)[None, :]
    tables_k = rope_tables(every)
    tables_q = rope_tables(spot)
    gain_one, gain_two, router = columns(norm1_gain), columns(norm2_gain), columns(router)
    cot = gather_tokens(cotangent, ranks[:, :, None], picks)

    mixing_other, mixing, rank_column, gain_one, gain_two, router = hold(
        [swap(piece) for piece in mixing], mixing, columns(rank), gain_one, gain_two, router
    )
    if aligned:
        mixing = join(who, mixing, mixing_other)
    else:
        order = jnp.arange(pairs) ^ own_pair_index
        mixing = jnp.stack([jnp.stack(mixing), jnp.stack(mixing_other)])[jnp.stack([core, 1 - core])]
        mixing = mixing[:, order].transpose(2, 1, 0, 3, 4).reshape(col_count, width, mixing_part)
        mixing = mixing[jnp.arange(col_count) ^ column]
    (
        x, mixing, cot, limit, tables_k, tables_q, rank_column, gain_one, gain_two, router,
    ) = hold(
        to_owner(x), mixing, cot, limit, tables_k, tables_q, rank_column, gain_one, gain_two, router
    )
    cot = to_owner(cot)
    picked, prob, q, kt, k, vt, v = project(
        x, rank_column, gain_one, router, tables_k, tables_q, mixing
    )
    mixed, mass = attend(q, k, vt, limit)
    (branch, inverse, normed), cot = hold(merge(mixed, picked, gain_two, mixing), cot)
    gate, up, active, delta, both = ffn(who, normed, branch, prob, col_count, hidden, sources)
    grad_ffn = (prob * cot.astype(F32)).astype(BF)
    (keep_down, send_down), delta, gate = hold(
        down_grad(who, grad_ffn, active, pairs, col_count), delta, gate
    )
    delta = [
        lax.dynamic_slice_in_dim(delta, (column ^ k) * part, part, 0) for k in range(sequences)
    ]
    delta, keep_down, send_down = hold(delta, keep_down, send_down)
    delta = [partner(value, "col", k) if k else value for k, value in enumerate(delta)]
    pieces = pairs if aligned else 1
    back_args = (pieces, normed, grad_ffn, gate, up, sources)
    tail = (branch, both, picked, cot, prob, inverse, gain_two, router)

    def by_pairs(value):
        if aligned:
            return value
        value = value[0].reshape(half, pairs, 2 * rows, hidden).transpose(1, 0, 2, 3)
        return value[jnp.arange(pairs) ^ own_pair_index]

    got_down, (keep_low, send_low, carried), keep_down, near = hold(
        swap(send_down),
        ffn_back(who, 0, half, False, *back_args, None, None),
        keep_down,
        delta[1:-1],
    )
    delta[1:-1] = near
    sum_down = pair_up(keep_down, got_down)
    sum_down, send_low, keep_low, carried = hold(sum_down, send_low, keep_low, carried)
    (
        got_low, sum_down, delta,
        (keep_high, send_high, grad_attn, rest, gain_two_grad, router_grad), keep_low,
    ) = hold(
        swap(send_low),
        spread(sum_down, "row"),
        delta,
        ffn_back(who, half, half, True, *back_args, carried, tail),
        keep_low,
    )
    sum_low = pair_up(by_pairs(keep_low), by_pairs(got_low))
    sum_down = list(add_up(sum_down).astype(BF))
    sum_low, sum_down, send_high, keep_high, grad_attn = hold(
        sum_low, sum_down, send_high, keep_high, grad_attn
    )
    sum_low = spread(sum_low, "row")
    got_high, (gw_out, grad_mixed), keep_high = hold(
        swap(send_high), merge_back(mixed, grad_attn, mixing), keep_high
    )
    sum_high = pair_up(by_pairs(keep_high), by_pairs(got_high))
    sum_high, grad_mixed = hold(sum_high, grad_mixed)
    heads = (q, k, kt, v, limit, mass, grad_mixed, mixed, tables_k, tables_q)
    most = (KVH + 1) // 2
    down_far, sum_low, one, sum_high = hold(
        [partner(sum_down[k], "col", k) for k in range(half, col_count)],
        sum_low,
        attend_back(0, most, *heads),
        sum_high,
    )
    far = list(add_up(sum_low).astype(BF))
    far, one, grad_mixed = hold(far, one, grad_mixed)
    far = [partner(value, "col", col_count - 1 - i) for i, value in enumerate(far)]
    heads = heads[:6] + (grad_mixed,) + heads[7:]
    sum_high = spread(sum_high, "row")
    (two,) = hold(attend_back(most, KVH - most, *heads))
    gq, gk, gv = zip(one, two)
    far, sum_high, (*gw_mixing, grads, gain_one_grad) = hold(
        far,
        sum_high,
        mixing_grad(who, x, rank[None, :], gain_one, gq, gk, gv, gw_out, mixing, pairs),
    )
    *near, sum_pair = add_up(sum_high).astype(BF)
    near = [pack(value, sum_down[half - 1 - i]) for i, value in enumerate(near)]
    vectors = jnp.concatenate([gain_one_grad, gain_two_grad, router_grad], axis=1).T.astype(BF)
    vectors = vectors.reshape(3, col_count, part).transpose(1, 0, 2)
    vectors = vectors[jnp.arange(col_count) ^ column]
    vectors = jnp.pad(vectors, ((0, 0), (0, VECTOR_ROWS - 3), (0, mixing_part - part)))
    vectors = jnp.broadcast_to(vectors[None], (pairs,) + vectors.shape)
    keep_mixing, send_mixing = (
        lax.dynamic_update_slice(value, vectors, (0, 0, rows, 0)) for value in gw_mixing
    )
    near, keep_mixing, send_mixing, grads = hold(near, keep_mixing, send_mixing, grads)
    got_mixing, near, back, keep_mixing = hold(
        swap(send_mixing),
        [
            [partner(value, "col", half - 1 - i) for value in values]
            for i, values in enumerate(near)
        ],
        project_back(x, rank[None, :], gain_one, grads, rest, mixing),
        keep_mixing,
    )
    back = from_owner(back, sequences)
    sum_mixing = pair_up(keep_mixing, got_mixing)
    sum_mixing, near, delta, sum_pair = hold(sum_mixing, near, delta, sum_pair)
    block_out = scatter_tokens(who, resid, delta, ranks[:, None, :])
    sum_mixing, block_out, near, sum_pair, far = hold(
        spread(sum_mixing, "row"), block_out, near, sum_pair, far
    )
    sum_mixing = add_up(sum_mixing).astype(BF)
    parts = [unpack(values, 2 * rows) for values in near]
    sum_pair = add_up([sum_pair] + [first for first, _ in parts] + far)
    sum_down = add_up([sum_down[0]] + [second for _, second in parts] + down_far)

    lanes = sum_down.shape[1] // 2
    first, second = sum_down[:, :lanes], sum_down[:, lanes:]
    mine, other = jnp.where(even, first, second), jnp.where(even, second, first)
    other = swap(other.astype(BF)).astype(F32)
    top, end = jnp.where(even, mine, other), jnp.where(even, other, mine)
    gw_down = jnp.concatenate([top, end[2 * down_rows_kept - part :]], axis=0).T

    gw_mixing = add_up(spread(list(sum_mixing), "col"))

    sum_pair = sum_pair.reshape(2, rows, hidden)
    mine = jnp.where(even, sum_pair[0], sum_pair[1])
    other = jnp.where(even, sum_pair[1], sum_pair[0]).astype(BF)
    other = swap(other).astype(F32)
    gw_gate, gw_up = jnp.where(even, mine, other), jnp.where(even, other, mine)
    if copies > 1:
        gw_gate, gw_up, gw_down, gw_mixing = (
            a / copies for a in (gw_gate, gw_up, gw_down, gw_mixing)
        )

    resid_grad = cotangent + back.astype(F32)
    kv_part = w_key.shape[1]
    ends = (part, part + kv_part, part + 2 * kv_part)
    return (
        block_out, resid_grad,
        gw_mixing[rows, :part], gw_mixing[rows + 1, :part], gw_mixing[rows + 2, :part],
        gw_mixing[:rows, : ends[0]], gw_mixing[:rows, ends[0] : ends[1]],
        gw_mixing[:rows, ends[1] : ends[2]], gw_mixing[:rows, ends[2] :],
        gw_gate, gw_up, gw_down,
    )


def solution(mesh):
    block = P("row", "col")
    placed = (
        P("row", "col", None), P("row", "col", None), P("row"), P("row"), P(None, "row", None),
        P(), P(), P(),
        block, block, block, block, block, block, block,
    )
    given = (
        P("row", "col", None), P("row", "col", None), P("col"), P("col"), P("col"),
        block, block, block, block, block, block, block,
    )
    return jax.shard_map(
        on_device, mesh=mesh, in_specs=placed, out_specs=given, check_vma=False
    )
```

```python
import functools
import math

import jax
import jax.numpy as jnp
from jax import lax
from jax.experimental import pallas as pl
from jax.experimental.pallas import tpu as pltpu
from jax.sharding import PartitionSpec as P

H = 15
KVH = 5
HD = 64
GROUP = H // KVH
QBLOCK = 256

EPSILON = 1e-05
ROPE_BASE = 10000.0
NEG = -1e30
VECTOR_ROWS = 8
LANES = 128

BF = jnp.bfloat16
F32 = jnp.float32
MIB = 1 << 20


def dot_nn(a, b):
    return lax.dot_general(a, b, (((1,), (0,)), ((), ())), preferred_element_type=F32)


def dot_tn(a, b):
    return lax.dot_general(a, b, (((0,), (0,)), ((), ())), preferred_element_type=F32)


def dot_nt(a, b):
    return lax.dot_general(a, b, (((1,), (1,)), ((), ())), preferred_element_type=F32)


def params(limit=56):
    return pltpu.CompilerParams(
        dimension_semantics=("arbitrary",), vmem_limit_bytes=limit * MIB
    )


def cost(flops, nbytes, exps=0):
    return pl.CostEstimate(
        flops=int(flops) // 32,
        bytes_accessed=int(nbytes) // 32,
        transcendentals=int(exps) // 32,
    )


def struct(shape, dtype):
    return jax.ShapeDtypeStruct(shape, dtype)


def whole(shape):
    return pl.BlockSpec(shape, lambda i, *_: (0,) * len(shape))


def pick_columns(rank_column, picks):
    place = lax.broadcasted_iota(jnp.int32, (rank_column.shape[0], picks), 1)
    return jnp.where(rank_column == place, 1.0, 0.0).astype(BF)


def pick_rows(rank_row, picks):
    place = lax.broadcasted_iota(jnp.int32, (picks, rank_row.shape[1]), 0)
    return jnp.where(rank_row == place, 1.0, 0.0).astype(BF)


def turn(first, second, cosine, sine, direction):
    signed = sine * direction
    return first * cosine - second * signed, second * cosine + first * signed


def gather_body(values, rank, out):
    chosen = pick_columns(rank[0], out.shape[2])
    out[0] = dot_nn(values[0].astype(BF), chosen).astype(BF)


def gather_tokens(values, rank_column, picks):
    count, width, length = values.shape
    return pl.pallas_call(
        gather_body,
        grid=(count,),
        in_specs=[
            pl.BlockSpec((1, width, length), lambda i: (i, 0, 0)),
            pl.BlockSpec((1, length, 1), lambda i: (i, 0, 0)),
        ],
        out_specs=pl.BlockSpec((1, width, picks), lambda i: (i, 0, 0)),
        out_shape=struct((count, width, picks), BF),
        compiler_params=params(),
        cost_estimate=cost(2 * count * width * length * picks, 6 * values.size),
        name="gather_tokens",
    )(values, rank_column)


def scatter_body(who, base, rank, *refs):
    *pieces, out, values = refs
    count = len(pieces)
    for k, piece in enumerate(pieces):

        @pl.when((pl.program_id(0) ^ lax.rem(who[0], count)) == k)
        def _():
            values[...] = piece[...]

    out[0] = base[0] + dot_nn(values[...], pick_rows(rank[0], values.shape[1]))


def scatter_tokens(who, base, pieces, rank_row):
    count, width, length = base.shape
    picks = pieces[0].shape[1]
    return pl.pallas_call(
        scatter_body,
        grid_spec=pltpu.PrefetchScalarGridSpec(
            num_scalar_prefetch=1,
            grid=(count,),
            in_specs=[
                pl.BlockSpec((1, width, length), lambda i, who: (i, 0, 0)),
                pl.BlockSpec((1, 1, length), lambda i, who: (i, 0, 0)),
            ]
            + [whole((width, picks))] * count,
            out_specs=pl.BlockSpec((1, width, length), lambda i, who: (i, 0, 0)),
            scratch_shapes=[pltpu.VMEM((width, picks), BF)],
        ),
        out_shape=struct(base.shape, F32),
        compiler_params=params(),
        cost_estimate=cost(2 * count * width * length * picks, 10 * base.size),
        name="scatter_tokens",
    )(who, base, rank_row, *pieces)


def join_body(who, *refs):
    *pieces, w = refs
    even = who[2] == 0
    count = len(pieces) // 2
    for k, (own, other) in enumerate(zip(pieces[:count], pieces[count:])):
        first, second = own[0].astype(F32), other[0].astype(F32)
        both = [jnp.where(even, first, second), jnp.where(even, second, first)]
        height = 2 * first.shape[0]
        place = pl.ds(pl.multiple_of((who[1] ^ k) * height, 16), height)
        w[0, place] = jnp.concatenate(both, axis=0).astype(BF)


def join(who, own, other):
    blocks, height, part = own[0].shape
    width = 2 * len(own) * height
    piece = pl.BlockSpec((1, height, part), lambda i, who: (i, 0, 0))
    return pl.pallas_call(
        join_body,
        grid_spec=pltpu.PrefetchScalarGridSpec(
            num_scalar_prefetch=1,
            grid=(blocks,),
            in_specs=[piece] * (2 * len(own)),
            out_specs=pl.BlockSpec((1, width, part), lambda i, who: (i ^ who[0], 0, 0)),
        ),
        out_shape=struct((blocks, width, part), BF),
        compiler_params=params(),
        cost_estimate=cost(0, 4 * blocks * width * part),
        name="join",
    )(who, *own, *other)


def project_body(
    x, rank, gain, router, cos_k, sin_k, cos_q, sin_q, w,
    picked, prob, q_out, kt_out, k_out, vt_out, v_out,
    normed, normed_picked, q_raw, kv_raw,
):
    step = pl.program_id(0)
    width = x.shape[0]
    q_part = width // pl.num_programs(0)
    kv_part = KVH * HD // pl.num_programs(0)

    @pl.when(step == 0)
    def _():
        full = x[...].astype(F32)
        inverse = lax.rsqrt(jnp.sum(full * full, axis=0, keepdims=True) / width + EPSILON)
        normed[...] = (full * inverse * gain[:, :1]).astype(BF)
        chosen = pick_columns(rank[:, :1], picked.shape[1])
        part = dot_nn(x[...], chosen)
        picked[...] = part.astype(BF)
        inverse = lax.rsqrt(jnp.sum(part * part, axis=0, keepdims=True) / width + EPSILON)
        normed_picked[...] = (part * inverse * gain[:, :1]).astype(BF)
        logit = jnp.sum(part * router[:, :1], axis=0, keepdims=True)
        prob[...] = jax.nn.sigmoid(logit)

    q_raw[pl.ds(pl.multiple_of(step * q_part, 8), q_part)] = dot_tn(
        w[0, :, :q_part], normed_picked[...]
    ).astype(BF)
    kv = dot_tn(w[0, :, q_part : q_part + 2 * kv_part], normed[...]).astype(BF)
    kv_raw[0, pl.ds(pl.multiple_of(step * kv_part, 8), kv_part)] = kv[:kv_part]
    kv_raw[1, pl.ds(pl.multiple_of(step * kv_part, 8), kv_part)] = kv[kv_part:]

    @pl.when(step == pl.num_programs(0) - 1)
    def _():
        half = HD // 2
        for head in range(H):
            at = head * HD
            a, b = turn(
                q_raw[at : at + half].astype(F32),
                q_raw[at + half : at + HD].astype(F32),
                cos_q[...], sin_q[...], 1.0,
            )
            scale = HD ** (-0.5)
            q_out[at : at + half] = (a.astype(BF).astype(F32) * scale).astype(BF)
            q_out[at + half : at + HD] = (b.astype(BF).astype(F32) * scale).astype(BF)
        for head in range(KVH):
            at = head * HD
            a, b = turn(
                kv_raw[0, at : at + half].astype(F32),
                kv_raw[0, at + half : at + HD].astype(F32),
                cos_k[...], sin_k[...], 1.0,
            )
            turned = jnp.concatenate([a, b], axis=0)
            kt_out[at : at + HD] = turned.astype(BF)
            k_out[head] = turned.T.astype(BF)
            value = kv_raw[1, at : at + HD]
            vt_out[at : at + HD] = value
            v_out[head] = value.astype(F32).T.astype(BF)


def project(x, rank_column, gain, router, tables_k, tables_q, w):
    width, length = x.shape
    picks = tables_q[0].shape[1]
    blocks, _, part = w.shape
    kv = KVH * HD
    half = HD // 2
    return pl.pallas_call(
        project_body,
        grid=(blocks,),
        in_specs=[
            whole((width, length)),
            whole((length, LANES)),
            whole((width, LANES)),
            whole((width, LANES)),
            whole((half, length)),
            whole((half, length)),
            whole((half, picks)),
            whole((half, picks)),
            pl.BlockSpec((1, width, part), lambda i: (i, 0, 0)),
        ],
        out_specs=[
            whole((width, picks)),
            whole((1, picks)),
            whole((width, picks)),
            whole((kv, length)),
            whole((KVH, length, HD)),
            whole((kv, length)),
            whole((KVH, length, HD)),
        ],
        scratch_shapes=[
            pltpu.VMEM((width, length), BF),
            pltpu.VMEM((width, picks), BF),
            pltpu.VMEM((width, picks), BF),
            pltpu.VMEM((2, kv, length), BF),
        ],
        out_shape=[
            struct((width, picks), BF),
            struct((1, picks), F32),
            struct((width, picks), BF),
            struct((kv, length), BF),
            struct((KVH, length, HD), BF),
            struct((kv, length), BF),
            struct((KVH, length, HD), BF),
        ],
        compiler_params=params(),
        cost_estimate=cost(
            2 * width * (length * picks + picks * width + length * 2 * kv),
            2 * (2 * blocks * width * part + 4 * x.size),
        ),
        name="project",
    )(x, rank_column, gain, router, *tables_k, *tables_q, w)


def reach_of(block, length, picks):
    return max((block + 1) * QBLOCK + length - picks, length // 2)


def clear_of(block):
    return block * QBLOCK


def block_scores(q, k, limit, block, reach):
    scores = dot_nn(k[:reach], q)
    clear = clear_of(block)
    tail = scores[clear:] if clear else scores
    key = lax.broadcasted_iota(jnp.int32, tail.shape, 0) + clear
    tail = jnp.where(key <= limit, tail, NEG)
    return jnp.concatenate([scores[:clear], tail], axis=0) if clear else tail


def side_by_side(value, cols):
    return jnp.concatenate(
        [value[head * HD : (head + 1) * HD, cols] for head in range(GROUP)], axis=1
    )


def attend_body(q, k, vt, limit, out, total):
    length = k.shape[1]
    picks = q.shape[1]
    for block in range(picks // QBLOCK):
        cols = slice(block * QBLOCK, (block + 1) * QBLOCK)
        reach = reach_of(block, length, picks)
        limits = jnp.concatenate([limit[:, cols]] * GROUP, axis=1)
        scores = block_scores(side_by_side(q, cols), k[0], limits, block, reach)
        top = jnp.max(scores, axis=0, keepdims=True)
        weight = jnp.exp(scores - top)
        mass = jnp.sum(weight, axis=0, keepdims=True)
        mixed = (dot_nn(vt[:, :reach], weight.astype(BF)) / mass).astype(BF)
        logs = top + jnp.log(mass)
        for head in range(GROUP):
            part = slice(head * QBLOCK, (head + 1) * QBLOCK)
            out[head * HD : (head + 1) * HD, cols] = mixed[:, part]
            total[0, head : head + 1, cols] = logs[:, part]


def attend(q, k, vt, limit):
    width, picks = q.shape
    length = k.shape[1]
    part = GROUP * HD
    return pl.pallas_call(
        attend_body,
        grid=(KVH,),
        in_specs=[
            pl.BlockSpec((part, picks), lambda i: (i, 0)),
            pl.BlockSpec((1, length, HD), lambda i: (i, 0, 0)),
            pl.BlockSpec((HD, length), lambda i: (i, 0)),
            whole((1, picks)),
        ],
        out_specs=[
            pl.BlockSpec((part, picks), lambda i: (i, 0)),
            pl.BlockSpec((1, GROUP, picks), lambda i: (i, 0, 0)),
        ],
        out_shape=[struct((width, picks), BF), struct((KVH, GROUP, picks), F32)],
        compiler_params=params(),
        cost_estimate=cost(
            16 * width * length * picks, 4 * width * picks, H * length * picks
        ),
        name="attend",
    )(q, k, vt, limit)


def attend_back_body(
    q, k, kt, v, limit, total, grad, mixed, cos_k, sin_k, cos_q, sin_q,
    gq_out, gk_out, gv_out, gk, gv,
):
    length = k.shape[1]
    picks = q.shape[1]
    half = HD // 2
    gk[...] = jnp.zeros_like(gk)
    gv[...] = jnp.zeros_like(gv)
    for block in range(picks // QBLOCK):
        cols = slice(block * QBLOCK, (block + 1) * QBLOCK)
        reach = reach_of(block, length, picks)
        limits = jnp.concatenate([limit[:, cols]] * GROUP, axis=1)
        q_part, g_part = side_by_side(q, cols), side_by_side(grad, cols)
        scores = block_scores(q_part, k[0], limits, block, reach)
        logs = jnp.concatenate([total[0, head : head + 1, cols] for head in range(GROUP)], axis=1)
        weight = jnp.exp(scores - logs)
        delta = jnp.sum(
            g_part.astype(F32) * side_by_side(mixed, cols).astype(F32), axis=0, keepdims=True
        )
        pull = dot_nn(v[0, :reach], g_part)
        back = (weight * (pull - delta)).astype(BF)
        gq = dot_nn(kt[:, :reach], back) * HD ** (-0.5)
        gk[:reach] += dot_nt(back, q_part)
        gv[:reach] += dot_nt(weight.astype(BF), g_part)
        for head in range(GROUP):
            part = slice(head * QBLOCK, (head + 1) * QBLOCK)
            a, b = turn(gq[:half, part], gq[half:, part], cos_q[:, cols], sin_q[:, cols], -1.0)
            gq_out[head * HD : head * HD + half, cols] = a.astype(BF)
            gq_out[head * HD + half : (head + 1) * HD, cols] = b.astype(BF)
    turned = gk[...].T
    a, b = turn(turned[:half], turned[half:], cos_k[...], sin_k[...], -1.0)
    gk_out[:half] = a.astype(BF)
    gk_out[half:] = b.astype(BF)
    gv_out[...] = gv[...].T.astype(BF)


def attend_back(first, count, q, k, kt, v, limit, total, grad, mixed, tables_k, tables_q):
    picks = q.shape[1]
    length = k.shape[1]
    part = GROUP * HD
    half = HD // 2
    wide = pl.BlockSpec((part, picks), lambda i: (first + i, 0))
    tall = pl.BlockSpec((1, length, HD), lambda i: (first + i, 0, 0))
    flat = pl.BlockSpec((HD, length), lambda i: (first + i, 0))
    return pl.pallas_call(
        attend_back_body,
        grid=(count,),
        in_specs=[
            wide, tall, flat, tall, whole((1, picks)),
            pl.BlockSpec((1, GROUP, picks), lambda i: (first + i, 0, 0)),
            wide, wide,
            whole((half, length)), whole((half, length)),
            whole((half, picks)), whole((half, picks)),
        ],
        out_specs=[
            pl.BlockSpec((part, picks), lambda i: (i, 0)),
            pl.BlockSpec((HD, length), lambda i: (i, 0)),
            pl.BlockSpec((HD, length), lambda i: (i, 0)),
        ],
        out_shape=[
            struct((count * part, picks), BF),
            struct((count * HD, length), BF),
            struct((count * HD, length), BF),
        ],
        scratch_shapes=[pltpu.VMEM((length, HD), F32), pltpu.VMEM((length, HD), F32)],
        compiler_params=params(),
        cost_estimate=cost(
            40 * count * part * length * picks, 8 * count * part * picks, count * GROUP * length * picks
        ),
        name="attend_back",
    )(q, k, kt, v, limit, total, grad, mixed, *tables_k, *tables_q)


def merge_body(mixed, picked, gain, w, branch, inverse_out, normed, hidden, square):
    step = pl.program_id(0)
    width = mixed.shape[0]
    part = width // pl.num_programs(0)
    rows = pl.ds(pl.multiple_of(step * part, 8), part)

    @pl.when(step == 0)
    def _():
        square[...] = jnp.zeros_like(square)

    value = dot_tn(w[0, :, w.shape[2] - part :], mixed[...])
    branch[...] = value
    total = picked[rows, :].astype(F32) + value
    hidden[rows, :] = total
    square[...] += jnp.sum(total * total, axis=0, keepdims=True)

    @pl.when(step == pl.num_programs(0) - 1)
    def _():
        inverse = lax.rsqrt(square[...] / width + EPSILON)
        inverse_out[...] = inverse
        normed[...] = (hidden[...] * inverse * gain[:, :1]).astype(BF)


def merge(mixed, picked, gain, w):
    width, picks = mixed.shape
    blocks, _, wide = w.shape
    part = width // blocks
    return pl.pallas_call(
        merge_body,
        grid=(blocks,),
        in_specs=[
            whole((width, picks)),
            whole((width, picks)),
            whole((width, LANES)),
            pl.BlockSpec((1, width, wide), lambda i: (i, 0, 0)),
        ],
        out_specs=[
            pl.BlockSpec((part, picks), lambda i: (i, 0)),
            whole((1, picks)),
            whole((width, picks)),
        ],
        out_shape=[
            struct((width, picks), F32),
            struct((1, picks), F32),
            struct((width, picks), BF),
        ],
        scratch_shapes=[pltpu.VMEM((width, picks), F32), pltpu.VMEM((1, picks), F32)],
        compiler_params=params(),
        cost_estimate=cost(2 * width * width * picks, 14 * width * picks + 2 * w.size),
        name="merge",
    )(mixed, picked, gain, w)


def down_half(part):
    return -(-part // 32) * 16


def ffn_weights(who, first, blocks, sources, w_pair, w_down, done):
    step, steps = pl.program_id(0), pl.num_programs(0)
    slot = lax.rem(step, 2)
    width, hidden = w_pair.shape[1], w_down.shape[2]
    gates, ups = slice(0, hidden), slice(hidden, 2 * hidden)

    def copies(step, at):
        turn = blocks - 1 - first - step
        block = turn ^ who[0]
        if len(sources) == 2:
            some = [
                (sources[0].at[block], w_pair.at[at]),
                (sources[1].at[block], w_down.at[at]),
            ]
        else:
            (source,) = sources
            pairs, _, columns, _, _ = source.shape
            height, part = width // pairs, width // columns
            half = down_half(part)
            some = []
            for i in range(pairs):
                place = slice(i * height, (i + 1) * height)
                some.append((source.at[i, 0, turn, :height], w_pair.at[at, place, gates]))
                some.append((source.at[i, 1, turn, :height], w_pair.at[at, place, ups]))
            for c in range(columns):
                begin = pl.multiple_of((c ^ who[0]) * part, 16)
                top = pl.ds(begin, half)
                some.append((source.at[block, 0, c, height : height + half], w_down.at[at, top]))
                end = pl.ds(pl.multiple_of(begin + half, 16), part - half)
                rest = slice(height + 2 * half - part, height + half)
                some.append((source.at[block, 1, c, rest], w_down.at[at, end]))
        return [
            pltpu.make_async_copy(source, target, done.at[at, i])
            for i, (source, target) in enumerate(some)
        ]

    @pl.when(step == 0)
    def _():
        for copy in copies(step, slot):
            copy.start()

    @pl.when(step + 1 < steps)
    def _():
        for copy in copies(step + 1, 1 - slot):
            copy.start()

    for copy in copies(step, slot):
        copy.wait()
    return slot


def ffn_scratch(width, sources):
    hidden = sources[-1].shape[-1]
    count = 2
    if len(sources) == 1:
        count = 2 * (sources[0].shape[0] + sources[0].shape[2])
    return [
        pltpu.VMEM((2, width, 2 * hidden), BF),
        pltpu.VMEM((2, width, hidden), BF),
        pltpu.SemaphoreType.DMA((2, count)),
    ]


def ffn_body(many, who, normed, branch, prob, *refs):
    sources, refs = refs[:many], refs[many:]
    gate_out, up_out, active_out, delta, both_out, forward, *buffers = refs
    w_pair, w_down, _ = buffers
    hidden = w_down.shape[2]
    slot = ffn_weights(who, 0, pl.num_programs(0), sources, *buffers)

    @pl.when(pl.program_id(0) == 0)
    def _():
        forward[...] = branch[...]

    tokens = normed[...]
    pair = dot_tn(w_pair[slot], tokens)
    gate, up = pair[:hidden], pair[hidden:]
    active = (gate * jax.nn.sigmoid(gate) * up).astype(BF)
    gate_out[0] = gate.astype(BF)
    up_out[0] = up.astype(BF)
    active_out[0] = active
    forward[...] += dot_nn(w_down[slot], active)

    @pl.when(pl.program_id(0) == pl.num_programs(0) - 1)
    def _():
        both = forward[...]
        delta[...] = (prob[...] * both).astype(BF)
        both_out[...] = both.astype(BF)


def ffn(who, normed, branch, prob, blocks, hidden, sources):
    width, picks = normed.shape
    full, row = whole((width, picks)), whole((1, picks))
    far = pl.BlockSpec(memory_space=pl.ANY)
    kept = pl.BlockSpec((1, hidden, picks), lambda i, who: (i, 0, 0))
    kept_shape = struct((blocks, hidden, picks), BF)
    low = struct((width, picks), BF)
    return pl.pallas_call(
        functools.partial(ffn_body, len(sources)),
        grid_spec=pltpu.PrefetchScalarGridSpec(
            num_scalar_prefetch=1,
            grid=(blocks,),
            in_specs=[full, full, row] + [far] * len(sources),
            out_specs=[kept] * 3 + [full, full],
            scratch_shapes=[pltpu.VMEM((width, picks), F32)] + ffn_scratch(width, sources),
        ),
        out_shape=[kept_shape] * 3 + [low, low],
        compiler_params=params(60),
        cost_estimate=cost(
            6 * width * hidden * blocks * picks, 6 * width * hidden * blocks + 8 * width * picks
        ),
        name="ffn",
    )(who, normed, branch, prob, *sources)


def down_grad_body(who, grad_ffn, active, keep, send):
    here, columns, half, lanes = keep.shape
    part = grad_ffn.shape[0] // columns
    even = who[2] == 0
    for c in range(columns):
        value = dot_nt(grad_ffn[c * part : (c + 1) * part], active[0])
        low, high = value[:half].astype(BF), value[part - half :].astype(BF)
        mine, other = jnp.where(even, low, high), jnp.where(even, high, low)
        for i in range(here):
            at = i ^ lax.rem(who[1], here) if here > 1 else 0
            keep[at, c ^ who[0]] = mine[:, i * lanes : (i + 1) * lanes]
            send[at, c ^ who[0]] = other[:, i * lanes : (i + 1) * lanes]


def down_grad(who, grad_ffn, active, pairs, columns):
    width, picks = grad_ffn.shape
    blocks, hidden, _ = active.shape
    here = pairs // blocks
    tile = (columns, down_half(width // columns), hidden // here)
    block = pl.BlockSpec(
        (here,) + tile, lambda i, who: ((blocks - 1 - i) ^ who[0] ^ lax.div(who[1], here), 0, 0, 0)
    )
    return pl.pallas_call(
        down_grad_body,
        grid_spec=pltpu.PrefetchScalarGridSpec(
            num_scalar_prefetch=1,
            grid=(blocks,),
            in_specs=[
                whole((width, picks)),
                pl.BlockSpec((1, hidden, picks), lambda i, who: (i, 0, 0)),
            ],
            out_specs=[block, block],
        ),
        out_shape=[struct((pairs,) + tile, BF)] * 2,
        compiler_params=params(),
        cost_estimate=cost(2 * blocks * hidden * width * picks, 6 * blocks * hidden * width),
        name="down_grad",
    )(who, grad_ffn, active)


def ffn_back_body(first, blocks, last, many, who, normed, grad_ffn, gate_in, up_in, *refs):
    sources, refs = refs[:many], refs[many:]
    if first:
        carried, refs = refs[0], refs[1:]
    if last:
        (branch, both_in, picked, cot, prob, inverse, gain, router), refs = refs[:8], refs[8:]
    keep_pair, send_pair, refs = refs[0], refs[1], refs[2:]
    outs, backward, buffers = refs[:-4], refs[-4], refs[-3:]
    w_pair, w_down, _ = buffers
    hidden = w_down.shape[2]
    slot = ffn_weights(who, first, blocks, sources, *buffers)
    width = normed.shape[0]
    even = who[2] == 0

    @pl.when(pl.program_id(0) == 0)
    def _():
        backward[...] = carried[...] if first else jnp.zeros_like(backward)

    pull = dot_tn(w_down[slot], grad_ffn[...])
    gate = gate_in[0].astype(F32)
    sigmoid = jax.nn.sigmoid(gate)
    silu = gate * sigmoid
    grad_gate = (pull * up_in[0].astype(F32) * (sigmoid + silu * (1.0 - sigmoid))).astype(BF)
    grad_up = (pull * silu).astype(BF)
    tokens = normed[...]
    grads = jnp.concatenate([grad_gate, grad_up], axis=0)
    backward[...] += dot_nn(w_pair[slot], grads)
    for_pair = dot_nt(tokens, grads).astype(BF)
    for_gate, for_up = for_pair[:, :hidden], for_pair[:, hidden:]
    pieces, _, height, _ = keep_pair.shape
    for i in range(pieces):
        place = slice(i * height, (i + 1) * height)
        at = i ^ who[1] if pieces > 1 else 0
        keep_pair[at, 0] = jnp.where(even, for_gate[place], for_up[place])
        send_pair[at, 0] = jnp.where(even, for_up[place], for_gate[place])

    @pl.when(pl.program_id(0) == pl.num_programs(0) - 1)
    def _():
        if not last:
            outs[0][...] = backward[...]
            return
        grad_attn, rest_out, gain_out, router_out = outs
        share = prob[...]
        cot_full = cot[...].astype(F32)
        slope = share * (1.0 - share) * jnp.sum(
            cot_full * both_in[...].astype(F32), axis=0, keepdims=True
        )
        token = picked[...].astype(F32)
        router_out[...] = jnp.sum(slope * token, axis=1, keepdims=True)
        merged = token + branch[...]
        inv = inverse[...]
        grad_norm = backward[...]
        gain_out[...] = jnp.sum(grad_norm * merged * inv, axis=1, keepdims=True)
        unit = grad_norm * gain[:, :1]
        along = jnp.sum(unit * merged, axis=0, keepdims=True) / width
        grad_hidden = inv * unit - merged * (inv * inv * inv * along)
        grad_attn[...] = (grad_hidden + share * cot_full).astype(BF)
        rest_out[...] = (grad_hidden + slope * router[:, :1]).astype(BF)


def ffn_back(who, first, count, last, pieces, normed, grad_ffn, gate, up, sources, carried, tail):
    width, picks = normed.shape
    hidden = gate.shape[1]
    height = width // pieces
    full, row, column = whole((width, picks)), whole((1, picks)), whole((width, 1))
    far = pl.BlockSpec(memory_space=pl.ANY)
    kept = pl.BlockSpec((1, hidden, picks), lambda i, who: (i + first, 0, 0))
    tall = pl.BlockSpec((pieces, 1, height, hidden), lambda i, who: (0, i, 0, 0))
    tall_shape = struct((pieces, count, height, hidden), BF)
    low, thin = struct((width, picks), BF), struct((width, 1), F32)
    extra = ([carried] if first else []) + (list(tail) if last else [])
    extra_specs = ([full] if first else []) + ([full] * 4 + [row] * 2 + [whole((width, LANES))] * 2 if last else [])
    return pl.pallas_call(
        functools.partial(ffn_back_body, first, gate.shape[0], last, len(sources)),
        grid_spec=pltpu.PrefetchScalarGridSpec(
            num_scalar_prefetch=1,
            grid=(count,),
            in_specs=[full, full, kept, kept] + [far] * len(sources) + extra_specs,
            out_specs=[tall, tall] + ([full, full, column, column] if last else [full]),
            scratch_shapes=[pltpu.VMEM((width, picks), F32)] + ffn_scratch(width, sources),
        ),
        out_shape=[tall_shape, tall_shape]
        + ([low, low, thin, thin] if last else [struct((width, picks), F32)]),
        compiler_params=params(60),
        cost_estimate=cost(
            10 * width * hidden * count * picks, 10 * width * hidden * count + 12 * width * picks
        ),
        name="ffn_back",
    )(who, normed, grad_ffn, gate, up, *sources, *extra)


def merge_back_body(mixed, grad, w, gw, grad_mixed, total):
    step = pl.program_id(0)
    part = gw.shape[2]
    rows = pl.ds(pl.multiple_of(step * part, 8), part)
    piece = grad[rows, :]
    gw[0] = dot_nt(mixed[...], piece).astype(BF)
    value = dot_nn(w[0, :, w.shape[2] - part :], piece)

    @pl.when(step == 0)
    def _():
        total[...] = value

    @pl.when(step > 0)
    def _():
        total[...] += value

    @pl.when(step == pl.num_programs(0) - 1)
    def _():
        grad_mixed[...] = total[...].astype(BF)


def merge_back(mixed, grad, w):
    width, picks = mixed.shape
    blocks, _, wide = w.shape
    part = width // blocks
    block = pl.BlockSpec((1, width, part), lambda i: (i, 0, 0))
    wide_block = pl.BlockSpec((1, width, wide), lambda i: (i, 0, 0))
    return pl.pallas_call(
        merge_back_body,
        grid=(blocks,),
        in_specs=[whole((width, picks)), whole((width, picks)), wide_block],
        out_specs=[block, whole((width, picks))],
        out_shape=[struct((blocks, width, part), BF), struct((width, picks), BF)],
        scratch_shapes=[pltpu.VMEM((width, picks), F32)],
        compiler_params=params(),
        cost_estimate=cost(4 * width * width * picks, 6 * width * picks + 4 * w.size),
        name="merge_back",
    )(mixed, grad, w)


def mixing_grad_body(
    who, x, rank, gain, *refs
):
    gq, gk, gv, refs = refs[:2], refs[2:4], refs[4:6], refs[6:]
    gw_out, w, keep, send, grads_out, gain_out, normed, gq_full, gkv_full = refs
    step = pl.program_id(0)
    width = x.shape[0]
    q_part = width // pl.num_programs(0)
    kv_part = KVH * HD // pl.num_programs(0)
    even = who[2] == 0

    @pl.when(step == 0)
    def _():
        full = x[...].astype(F32)
        inverse = lax.rsqrt(jnp.sum(full * full, axis=0, keepdims=True) / width + EPSILON)
        normed[...] = (full * inverse * gain[:, :1]).astype(BF)
        chosen = pick_rows(rank[...], gq[0].shape[1])
        at = 0
        for piece in gq:
            gq_full[at : at + piece.shape[0]] = dot_nn(piece[...], chosen).astype(BF)
            at += piece.shape[0]
        for i, pieces in enumerate((gk, gv)):
            at = 0
            for piece in pieces:
                gkv_full[i, at : at + piece.shape[0]] = piece[...]
                at += piece.shape[0]

    q_rows = pl.ds(pl.multiple_of(step * q_part, 8), q_part)
    kv_rows = pl.ds(pl.multiple_of(step * kv_part, 8), kv_part)
    grads = jnp.concatenate(
        [gq_full[q_rows, :], gkv_full[0, kv_rows, :], gkv_full[1, kv_rows, :]], axis=0
    )
    grads_out[0] = grads
    value = dot_nt(normed[...], grads)
    share = jnp.sum(
        value * w[0, :, : grads.shape[0]].astype(F32), axis=1, keepdims=True
    ) / gain[:, :1]
    gain_out[...] = jnp.where(step == 0, share, gain_out[...] + share)
    value = jnp.concatenate([value, gw_out[0].astype(F32)], axis=1)
    pairs = keep.shape[0]
    rows = width // (2 * pairs)
    for pair in range(pairs):
        low = value[2 * pair * rows : (2 * pair + 1) * rows]
        high = value[(2 * pair + 1) * rows : (2 * pair + 2) * rows]
        keep[pair ^ who[1], 0, :rows] = jnp.where(even, low, high).astype(BF)
        send[pair ^ who[1], 0, :rows] = jnp.where(even, high, low).astype(BF)


def mixing_grad(who, x, rank_row, gain, gq, gk, gv, gw_out, w, pairs):
    width, length = x.shape
    picks = gq[0].shape[1]
    blocks, _, out_part = gw_out.shape
    kv = KVH * HD
    part = (width + 2 * kv) // blocks
    rows = width // (2 * pairs) + VECTOR_ROWS
    split = pl.BlockSpec((pairs, 1, rows, part + out_part), lambda i, who: (0, i ^ who[0], 0, 0))
    split_shape = struct((pairs, blocks, rows, part + out_part), BF)
    return pl.pallas_call(
        mixing_grad_body,
        grid_spec=pltpu.PrefetchScalarGridSpec(
            num_scalar_prefetch=1,
            grid=(blocks,),
            in_specs=[
                whole((width, length)),
                whole((1, length)),
                whole((width, LANES)),
                *(whole(piece.shape) for piece in (*gq, *gk, *gv)),
                pl.BlockSpec((1, width, out_part), lambda i, who: (i, 0, 0)),
                pl.BlockSpec((1,) + w.shape[1:], lambda i, who: (i, 0, 0)),
            ],
            out_specs=[
                split,
                split,
                pl.BlockSpec((1, part, length), lambda i, who: (i, 0, 0)),
                whole((width, 1)),
            ],
            scratch_shapes=[
                pltpu.VMEM((width, length), BF),
                pltpu.VMEM((width, length), BF),
                pltpu.VMEM((2, kv, length), BF),
            ],
        ),
        out_shape=[
            split_shape,
            split_shape,
            struct((blocks, part, length), BF),
            struct((width, 1), F32),
        ],
        compiler_params=params(),
        cost_estimate=cost(2 * width * length * (picks + width + 2 * kv), 10 * x.size),
        name="mixing_grad",
    )(who, x, rank_row, gain, *gq, *gk, *gv, gw_out, w)


def project_back_body(x, rank, gain, grads, rest, w, out, total):
    step = pl.program_id(0)
    width = x.shape[0]
    part = grads.shape[1]

    @pl.when(step == 0)
    def _():
        total[...] = jnp.zeros_like(total)

    total[...] += dot_nn(w[0, :, :part], grads[0])

    @pl.when(step == pl.num_programs(0) - 1)
    def _():
        full = x[...].astype(F32)
        inv = lax.rsqrt(jnp.sum(full * full, axis=0, keepdims=True) / width + EPSILON)
        grad_norm = total[...]
        unit = grad_norm * gain[:, :1]
        along = jnp.sum(unit * full, axis=0, keepdims=True) / width
        chosen = pick_rows(rank[...], rest.shape[1])
        out[...] = (
            inv * unit - full * (inv * inv * inv * along) + dot_nn(rest[...], chosen)
        ).astype(BF)


def project_back(x, rank_row, gain, grads, rest, w):
    width, length = x.shape
    picks = rest.shape[1]
    blocks, part, _ = grads.shape
    return pl.pallas_call(
        project_back_body,
        grid=(blocks,),
        in_specs=[
            whole((width, length)),
            whole((1, length)),
            whole((width, LANES)),
            pl.BlockSpec((1, part, length), lambda i: (i, 0, 0)),
            whole((width, picks)),
            pl.BlockSpec((1,) + w.shape[1:], lambda i: (i, 0, 0)),
        ],
        out_specs=whole((width, length)),
        out_shape=struct((width, length), BF),
        scratch_shapes=[pltpu.VMEM((width, length), F32)],
        compiler_params=params(),
        cost_estimate=cost(2 * width * length * (picks + blocks * part), 10 * x.size + 2 * w.size),
        name="project_back",
    )(x, rank_row, gain, grads, rest, w)


def columns(value):
    return jnp.broadcast_to(value[:, None], (value.shape[0], LANES))


def hold(*values):
    return lax.optimization_barrier(values)


def swap(value):
    count = lax.axis_size("row")
    return lax.ppermute(value, "row", [(i, i ^ 1) for i in range(count)])


def partner(value, axis, k):
    count = lax.axis_size(axis)
    far = k if axis == "col" else 2 * k
    return lax.ppermute(value, axis, [(i, i ^ far) for i in range(count)])


def collect(value, axis, partners):
    return [partner(value, axis, k) if k else value for k in partners]


def spread(values, axis):
    return [values[0]] + [partner(value, axis, k) for k, value in enumerate(values) if k]


def scatter_col(value, other):
    while value.shape[0] > 1:
        keep, send = value[0::2], value[1::2]
        step = lax.axis_size("col") // value.shape[0]
        got, other = hold(partner(send, "col", step), other)
        value = add_up((keep, got))
        if value.shape[0] > 1:
            value = value.astype(BF)
    return value[0], other


def add_up(values):
    return sum(value.astype(F32) for value in values)


def pack(first, second):
    if first.shape[1] == second.shape[1]:
        return [jnp.concatenate([first, second], axis=0)]
    return [first, second]


def unpack(values, rows):
    return (values[0][:rows], values[0][rows:]) if len(values) == 1 else tuple(values)


def pair_up(keep, got):
    return [add_up((a, b)).astype(BF) for a, b in zip(keep, got)]


def to_owner(value):
    copies = lax.axis_size("col") // value.shape[0]
    if copies > 1:
        value = jnp.concatenate([value] * copies, axis=0)
    moved = lax.all_to_all(value, "col", split_axis=0, concat_axis=1, tiled=True)
    return moved[0]


def from_owner(value, sequences):
    count = lax.axis_size("col")
    value = value.reshape(count, value.shape[0] // count, value.shape[1])
    moved = lax.all_to_all(value, "col", split_axis=0, concat_axis=0, tiled=True)
    return moved[:sequences]


def rope_tables(positions):
    half = HD // 2
    frequency = jnp.exp(jnp.arange(half, dtype=F32) * (-2.0 * math.log(ROPE_BASE) / HD))
    angles = frequency[:, None] * positions.astype(F32)[None, :]
    return jnp.cos(angles), jnp.sin(angles)


def on_device(
    resid, cotangent, prefix, slot, chosen, norm1_gain, norm2_gain, router,
    w_query, w_key, w_value, w_out, w_gate, w_up, w_down,
):
    col_count, row_count = lax.axis_size("col"), lax.axis_size("row")
    column = lax.axis_index("col")
    sequences, part, length = resid.shape
    width = part * col_count
    picks = chosen.shape[2]
    copies = col_count // sequences
    own = lax.rem(column, sequences)
    rows, hidden = w_gate.shape
    down_rows = w_down.shape[0]
    pairs = row_count // 2
    mixing_part = part + 2 * w_key.shape[1] + part

    own_pair_index = lax.axis_index("row") >> 1
    core = lax.axis_index("row") & 1
    even = core == 0
    who = jnp.stack([column, own_pair_index, core]).astype(jnp.int32)
    aligned = 2 * rows % 16 == 0 and hidden % 128 == 0

    half = col_count // 2

    mine = jnp.where(even, w_gate, w_up)
    other = swap(jnp.where(even, w_up, w_gate))
    pair = jnp.concatenate([jnp.where(even, mine, other), jnp.where(even, other, mine)], axis=0)
    down_rows_kept = down_half(part)
    turned = w_down.T
    low, high = turned[:down_rows_kept], turned[part - down_rows_kept :]
    mine, other = jnp.where(even, low, high), swap(jnp.where(even, high, low))
    down = jnp.concatenate([jnp.where(even, mine, other), jnp.where(even, other, mine)], axis=1)
    mixing = jnp.concatenate([w_query, w_key, w_value, w_out], axis=1)
    mixing, pair, down = hold(collect(mixing, "col", range(col_count)), pair, down)
    mixing, x = jnp.stack(mixing), resid.astype(BF)
    if aligned:
        sources = jnp.concatenate([pair, down], axis=0)
        sources, mixing, x = hold(
            collect(sources, "col", range(col_count)), collect(mixing, "row", range(pairs)), x
        )
        sources = lax.all_gather(jnp.stack(sources), "row", axis=0)
        sources = (sources.reshape((pairs, 2) + sources.shape[1:]),)
    else:
        mixing, x = hold(collect(mixing, "row", range(pairs)), x)
        pair_all = lax.all_gather(pair, ("row", "col"), axis=0)
        pair_all = pair_all.reshape(pairs, 2, col_count, 2 * rows, hidden).transpose(2, 0, 3, 1, 4)
        down_all = lax.all_gather(down, ("row", "col"), axis=0)
        down_all = down_all.reshape((col_count, pairs // col_count, 2, col_count) + down.shape)
        down_all = jnp.concatenate(
            [down_all[:, :, 0], down_all[:, :, 1, :, 2 * down_rows_kept - part :]], axis=3
        )
        sources = (
            pair_all.reshape(col_count, width, 2 * hidden),
            down_all.transpose(0, 2, 3, 1, 4).reshape(col_count, width, hidden),
        )
    every = jnp.arange(length, dtype=jnp.int32)
    chosen_of = chosen[:, 0][slot]
    selected = jnp.any(every[None, :, None] == chosen_of[:, None, :], axis=2)
    before = (every[:, None] < every[None, :]).astype(BF)
    places = jnp.dot(selected.astype(BF), before, preferred_element_type=F32)
    ranks = jnp.where(selected, places.astype(jnp.int32), -1)
    rank = lax.dynamic_index_in_dim(ranks, own, 0, keepdims=False)
    prefix_len = lax.dynamic_index_in_dim(prefix, own, 0, keepdims=False)
    place = jnp.arange(picks, dtype=jnp.int32)
    spot = jnp.sum(jnp.where(rank[None, :] == place[:, None], every[None, :], 0), axis=1)
    limit = jnp.maximum(spot, prefix_len - 1)[None, :]
    tables_k = rope_tables(every)
    tables_q = rope_tables(spot)
    gain_one, gain_two, router = columns(norm1_gain), columns(norm2_gain), columns(router)
    cot = gather_tokens(cotangent, ranks[:, :, None], picks)

    mixing_other, mixing, rank_column, gain_one, gain_two, router = hold(
        [swap(piece) for piece in mixing], mixing, columns(rank), gain_one, gain_two, router
    )
    if aligned:
        mixing = join(who, mixing, mixing_other)
    else:
        order = jnp.arange(pairs) ^ own_pair_index
        mixing = jnp.stack([jnp.stack(mixing), jnp.stack(mixing_other)])[jnp.stack([core, 1 - core])]
        mixing = mixing[:, order].transpose(2, 1, 0, 3, 4).reshape(col_count, width, mixing_part)
        mixing = mixing[jnp.arange(col_count) ^ column]
    (
        x, mixing, cot, limit, tables_k, tables_q, rank_column, gain_one, gain_two, router,
    ) = hold(
        to_owner(x), mixing, cot, limit, tables_k, tables_q, rank_column, gain_one, gain_two, router
    )
    cot = to_owner(cot)
    picked, prob, q, kt, k, vt, v = project(
        x, rank_column, gain_one, router, tables_k, tables_q, mixing
    )
    mixed, mass = attend(q, k, vt, limit)
    (branch, inverse, normed), cot = hold(merge(mixed, picked, gain_two, mixing), cot)
    gate, up, active, delta, both = ffn(who, normed, branch, prob, col_count, hidden, sources)
    grad_ffn = (prob * cot.astype(F32)).astype(BF)
    (keep_down, send_down), delta, gate = hold(
        down_grad(who, grad_ffn, active, pairs, col_count), delta, gate
    )
    delta = [
        lax.dynamic_slice_in_dim(delta, (column ^ k) * part, part, 0) for k in range(sequences)
    ]
    delta, keep_down, send_down = hold(delta, keep_down, send_down)
    delta = [partner(value, "col", k) if k else value for k, value in enumerate(delta)]
    pieces = pairs if aligned else 1
    back_args = (pieces, normed, grad_ffn, gate, up, sources)
    tail = (branch, both, picked, cot, prob, inverse, gain_two, router)

    def by_pairs(value):
        if aligned:
            return value
        value = value[0].reshape(half, pairs, 2 * rows, hidden).transpose(1, 0, 2, 3)
        return value[jnp.arange(pairs) ^ own_pair_index]

    got_down, (keep_low, send_low, carried), keep_down, near = hold(
        swap(send_down),
        ffn_back(who, 0, half, False, *back_args, None, None),
        keep_down,
        delta[1:-1],
    )
    delta[1:-1] = near
    sum_down = pair_up(keep_down, got_down)
    sum_down, send_low, keep_low, carried = hold(sum_down, send_low, keep_low, carried)
    (
        got_low, sum_down, delta,
        (keep_high, send_high, grad_attn, rest, gain_two_grad, router_grad), keep_low,
    ) = hold(
        swap(send_low),
        spread(sum_down, "row"),
        delta,
        ffn_back(who, half, half, True, *back_args, carried, tail),
        keep_low,
    )
    sum_low = pair_up(by_pairs(keep_low), by_pairs(got_low))
    sum_down = list(add_up(sum_down).astype(BF))
    sum_low, sum_down, send_high, keep_high, grad_attn = hold(
        sum_low, sum_down, send_high, keep_high, grad_attn
    )
    sum_low = spread(sum_low, "row")
    got_high, (gw_out, grad_mixed), keep_high = hold(
        swap(send_high), merge_back(mixed, grad_attn, mixing), keep_high
    )
    sum_high = pair_up(by_pairs(keep_high), by_pairs(got_high))
    sum_high, grad_mixed = hold(sum_high, grad_mixed)
    heads = (q, k, kt, v, limit, mass, grad_mixed, mixed, tables_k, tables_q)
    most = (KVH + 1) // 2
    down_far, sum_low, one, sum_high = hold(
        [partner(sum_down[k], "col", k) for k in range(half, col_count)],
        sum_low,
        attend_back(0, most, *heads),
        sum_high,
    )
    far = list(add_up(sum_low).astype(BF))
    far, one, grad_mixed = hold(far, one, grad_mixed)
    far = [partner(value, "col", col_count - 1 - i) for i, value in enumerate(far)]
    heads = heads[:6] + (grad_mixed,) + heads[7:]
    sum_high = spread(sum_high, "row")
    (two,) = hold(attend_back(most, KVH - most, *heads))
    gq, gk, gv = zip(one, two)
    far, sum_high, (*gw_mixing, grads, gain_one_grad) = hold(
        far,
        sum_high,
        mixing_grad(who, x, rank[None, :], gain_one, gq, gk, gv, gw_out, mixing, pairs),
    )
    *near, sum_pair = add_up(sum_high).astype(BF)
    near = [pack(value, sum_down[half - 1 - i]) for i, value in enumerate(near)]
    vectors = jnp.concatenate([gain_one_grad, gain_two_grad, router_grad], axis=1).T.astype(BF)
    vectors = vectors.reshape(3, col_count, part).transpose(1, 0, 2)
    vectors = vectors[jnp.arange(col_count) ^ column]
    vectors = jnp.pad(vectors, ((0, 0), (0, VECTOR_ROWS - 3), (0, mixing_part - part)))
    vectors = jnp.broadcast_to(vectors[None], (pairs,) + vectors.shape)
    keep_mixing, send_mixing = (
        lax.dynamic_update_slice(value, vectors, (0, 0, rows, 0)) for value in gw_mixing
    )
    near, keep_mixing, send_mixing, grads = hold(near, keep_mixing, send_mixing, grads)
    got_mixing, near, back, keep_mixing = hold(
        swap(send_mixing),
        [
            [partner(value, "col", half - 1 - i) for value in values]
            for i, values in enumerate(near)
        ],
        project_back(x, rank[None, :], gain_one, grads, rest, mixing),
        keep_mixing,
    )
    back = from_owner(back, sequences)
    sum_mixing = pair_up(keep_mixing, got_mixing)
    sum_mixing, near, delta, sum_pair = hold(sum_mixing, near, delta, sum_pair)
    block_out = scatter_tokens(who, resid, delta, ranks[:, None, :])
    sum_mixing, block_out, near, sum_pair, far = hold(
        spread(sum_mixing, "row"), block_out, near, sum_pair, far
    )
    sum_mixing = add_up(sum_mixing).astype(BF)
    parts = [unpack(values, 2 * rows) for values in near]
    sum_pair = add_up([sum_pair] + [first for first, _ in parts] + far)
    sum_down = add_up([sum_down[0]] + [second for _, second in parts] + down_far)

    lanes = sum_down.shape[1] // 2
    first, second = sum_down[:, :lanes], sum_down[:, lanes:]
    mine, other = jnp.where(even, first, second), jnp.where(even, second, first)
    other = swap(other.astype(BF)).astype(F32)
    top, end = jnp.where(even, mine, other), jnp.where(even, other, mine)
    gw_down = jnp.concatenate([top, end[2 * down_rows_kept - part :]], axis=0).T

    gw_mixing, resid_grad = scatter_col(sum_mixing, cotangent + back.astype(F32))

    sum_pair = sum_pair.reshape(2, rows, hidden)
    mine = jnp.where(even, sum_pair[0], sum_pair[1])
    other = jnp.where(even, sum_pair[1], sum_pair[0]).astype(BF)
    other = swap(other).astype(F32)
    gw_gate, gw_up = jnp.where(even, mine, other), jnp.where(even, other, mine)
    if copies > 1:
        gw_gate, gw_up, gw_down, gw_mixing = (
            a / copies for a in (gw_gate, gw_up, gw_down, gw_mixing)
        )

    kv_part = w_key.shape[1]
    ends = (part, part + kv_part, part + 2 * kv_part)
    return (
        block_out, resid_grad,
        gw_mixing[rows, :part], gw_mixing[rows + 1, :part], gw_mixing[rows + 2, :part],
        gw_mixing[:rows, : ends[0]], gw_mixing[:rows, ends[0] : ends[1]],
        gw_mixing[:rows, ends[1] : ends[2]], gw_mixing[:rows, ends[2] :],
        gw_gate, gw_up, gw_down,
    )


def solution(mesh):
    block = P("row", "col")
    placed = (
        P("row", "col", None), P("row", "col", None), P("row"), P("row"), P(None, "row", None),
        P(), P(), P(),
        block, block, block, block, block, block, block,
    )
    given = (
        P("row", "col", None), P("row", "col", None), P("col"), P("col"), P("col"),
        block, block, block, block, block, block, block,
    )
    return jax.shard_map(
        on_device, mesh=mesh, in_specs=placed, out_specs=given, check_vma=False
    )
```

```python
import functools
import math

import jax
import jax.numpy as jnp
from jax import lax
from jax.experimental import pallas as pl
from jax.experimental.pallas import tpu as pltpu
from jax.sharding import PartitionSpec as P

H = 15
KVH = 5
HD = 64
GROUP = H // KVH
QBLOCK = 256

EPSILON = 1e-05
ROPE_BASE = 10000.0
NEG = -1e30
VECTOR_ROWS = 8
LANES = 128

BF = jnp.bfloat16
F32 = jnp.float32
MIB = 1 << 20


def dot_nn(a, b):
    return lax.dot_general(a, b, (((1,), (0,)), ((), ())), preferred_element_type=F32)


def dot_tn(a, b):
    return lax.dot_general(a, b, (((0,), (0,)), ((), ())), preferred_element_type=F32)


def dot_nt(a, b):
    return lax.dot_general(a, b, (((1,), (1,)), ((), ())), preferred_element_type=F32)


def params(limit=56):
    return pltpu.CompilerParams(
        dimension_semantics=("arbitrary",), vmem_limit_bytes=limit * MIB
    )


def cost(flops, nbytes, exps=0):
    return pl.CostEstimate(
        flops=int(flops) // 32,
        bytes_accessed=int(nbytes) // 32,
        transcendentals=int(exps) // 32,
    )


def struct(shape, dtype):
    return jax.ShapeDtypeStruct(shape, dtype)


def whole(shape):
    return pl.BlockSpec(shape, lambda i, *_: (0,) * len(shape))


def pick_columns(rank_column, picks):
    place = lax.broadcasted_iota(jnp.int32, (rank_column.shape[0], picks), 1)
    return jnp.where(rank_column == place, 1.0, 0.0).astype(BF)


def pick_rows(rank_row, picks):
    place = lax.broadcasted_iota(jnp.int32, (picks, rank_row.shape[1]), 0)
    return jnp.where(rank_row == place, 1.0, 0.0).astype(BF)


def turn(first, second, cosine, sine, direction):
    signed = sine * direction
    return first * cosine - second * signed, second * cosine + first * signed


def gather_body(values, rank, out):
    chosen = pick_columns(rank[0], out.shape[2])
    out[0] = dot_nn(values[0].astype(BF), chosen).astype(BF)


def gather_tokens(values, rank_column, picks):
    count, width, length = values.shape
    return pl.pallas_call(
        gather_body,
        grid=(count,),
        in_specs=[
            pl.BlockSpec((1, width, length), lambda i: (i, 0, 0)),
            pl.BlockSpec((1, length, 1), lambda i: (i, 0, 0)),
        ],
        out_specs=pl.BlockSpec((1, width, picks), lambda i: (i, 0, 0)),
        out_shape=struct((count, width, picks), BF),
        compiler_params=params(),
        cost_estimate=cost(2 * count * width * length * picks, 6 * values.size),
        name="gather_tokens",
    )(values, rank_column)


def scatter_body(who, base, rank, *refs):
    *pieces, out, values = refs
    count = len(pieces)
    for k, piece in enumerate(pieces):

        @pl.when((pl.program_id(0) ^ lax.rem(who[0], count)) == k)
        def _():
            values[...] = piece[...]

    out[0] = base[0] + dot_nn(values[...], pick_rows(rank[0], values.shape[1]))


def scatter_tokens(who, base, pieces, rank_row):
    count, width, length = base.shape
    picks = pieces[0].shape[1]
    return pl.pallas_call(
        scatter_body,
        grid_spec=pltpu.PrefetchScalarGridSpec(
            num_scalar_prefetch=1,
            grid=(count,),
            in_specs=[
                pl.BlockSpec((1, width, length), lambda i, who: (i, 0, 0)),
                pl.BlockSpec((1, 1, length), lambda i, who: (i, 0, 0)),
            ]
            + [whole((width, picks))] * count,
            out_specs=pl.BlockSpec((1, width, length), lambda i, who: (i, 0, 0)),
            scratch_shapes=[pltpu.VMEM((width, picks), BF)],
        ),
        out_shape=struct(base.shape, F32),
        compiler_params=params(),
        cost_estimate=cost(2 * count * width * length * picks, 10 * base.size),
        name="scatter_tokens",
    )(who, base, rank_row, *pieces)


def join_body(who, *refs):
    *pieces, w = refs
    even = who[2] == 0
    count = len(pieces) // 2
    for k, (own, other) in enumerate(zip(pieces[:count], pieces[count:])):
        first, second = own[0].astype(F32), other[0].astype(F32)
        both = [jnp.where(even, first, second), jnp.where(even, second, first)]
        height = 2 * first.shape[0]
        place = pl.ds(pl.multiple_of((who[1] ^ k) * height, 16), height)
        w[0, place] = jnp.concatenate(both, axis=0).astype(BF)


def join(who, own, other):
    blocks, height, part = own[0].shape
    width = 2 * len(own) * height
    piece = pl.BlockSpec((1, height, part), lambda i, who: (i, 0, 0))
    return pl.pallas_call(
        join_body,
        grid_spec=pltpu.PrefetchScalarGridSpec(
            num_scalar_prefetch=1,
            grid=(blocks,),
            in_specs=[piece] * (2 * len(own)),
            out_specs=pl.BlockSpec((1, width, part), lambda i, who: (i ^ who[0], 0, 0)),
        ),
        out_shape=struct((blocks, width, part), BF),
        compiler_params=params(),
        cost_estimate=cost(0, 4 * blocks * width * part),
        name="join",
    )(who, *own, *other)


def project_body(
    x, rank, gain, router, cos_k, sin_k, cos_q, sin_q, w,
    picked, prob, q_out, kt_out, k_out, vt_out, v_out,
    normed, normed_picked, q_raw, kv_raw,
):
    step = pl.program_id(0)
    width = x.shape[0]
    q_part = width // pl.num_programs(0)
    kv_part = KVH * HD // pl.num_programs(0)

    @pl.when(step == 0)
    def _():
        full = x[...].astype(F32)
        inverse = lax.rsqrt(jnp.sum(full * full, axis=0, keepdims=True) / width + EPSILON)
        normed[...] = (full * inverse * gain[:, :1]).astype(BF)
        chosen = pick_columns(rank[:, :1], picked.shape[1])
        part = dot_nn(x[...], chosen)
        picked[...] = part.astype(BF)
        inverse = lax.rsqrt(jnp.sum(part * part, axis=0, keepdims=True) / width + EPSILON)
        normed_picked[...] = (part * inverse * gain[:, :1]).astype(BF)
        logit = jnp.sum(part * router[:, :1], axis=0, keepdims=True)
        prob[...] = jax.nn.sigmoid(logit)

    q_raw[pl.ds(pl.multiple_of(step * q_part, 8), q_part)] = dot_tn(
        w[0, :, :q_part], normed_picked[...]
    ).astype(BF)
    kv = dot_tn(w[0, :, q_part : q_part + 2 * kv_part], normed[...]).astype(BF)
    kv_raw[0, pl.ds(pl.multiple_of(step * kv_part, 8), kv_part)] = kv[:kv_part]
    kv_raw[1, pl.ds(pl.multiple_of(step * kv_part, 8), kv_part)] = kv[kv_part:]

    @pl.when(step == pl.num_programs(0) - 1)
    def _():
        half = HD // 2

        @pl.loop(0, H)
        def _(head):
            at = pl.multiple_of(head * HD, HD)
            low, high = pl.ds(at, half), pl.ds(pl.multiple_of(at + half, half), half)
            a, b = turn(
                q_raw[low].astype(F32), q_raw[high].astype(F32), cos_q[...], sin_q[...], 1.0
            )
            scale = HD ** (-0.5)
            q_out[low] = (a.astype(BF).astype(F32) * scale).astype(BF)
            q_out[high] = (b.astype(BF).astype(F32) * scale).astype(BF)

        @pl.loop(0, KVH)
        def _(head):
            at = pl.multiple_of(head * HD, HD)
            low, high = pl.ds(at, half), pl.ds(pl.multiple_of(at + half, half), half)
            a, b = turn(
                kv_raw[0, low].astype(F32), kv_raw[0, high].astype(F32), cos_k[...], sin_k[...], 1.0
            )
            turned = jnp.concatenate([a, b], axis=0)
            kt_out[pl.ds(at, HD)] = turned.astype(BF)
            k_out[head] = turned.T.astype(BF)
            value = kv_raw[1, pl.ds(at, HD)]
            vt_out[pl.ds(at, HD)] = value
            v_out[head] = value.astype(F32).T.astype(BF)


def project(x, rank_column, gain, router, tables_k, tables_q, w):
    width, length = x.shape
    picks = tables_q[0].shape[1]
    blocks, _, part = w.shape
    kv = KVH * HD
    half = HD // 2
    return pl.pallas_call(
        project_body,
        grid=(blocks,),
        in_specs=[
            whole((width, length)),
            whole((length, LANES)),
            whole((width, LANES)),
            whole((width, LANES)),
            whole((half, length)),
            whole((half, length)),
            whole((half, picks)),
            whole((half, picks)),
            pl.BlockSpec((1, width, part), lambda i: (i, 0, 0)),
        ],
        out_specs=[
            whole((width, picks)),
            whole((1, picks)),
            whole((width, picks)),
            whole((kv, length)),
            whole((KVH, length, HD)),
            whole((kv, length)),
            whole((KVH, length, HD)),
        ],
        scratch_shapes=[
            pltpu.VMEM((width, length), BF),
            pltpu.VMEM((width, picks), BF),
            pltpu.VMEM((width, picks), BF),
            pltpu.VMEM((2, kv, length), BF),
        ],
        out_shape=[
            struct((width, picks), BF),
            struct((1, picks), F32),
            struct((width, picks), BF),
            struct((kv, length), BF),
            struct((KVH, length, HD), BF),
            struct((kv, length), BF),
            struct((KVH, length, HD), BF),
        ],
        compiler_params=params(),
        cost_estimate=cost(
            2 * width * (length * picks + picks * width + length * 2 * kv),
            2 * (2 * blocks * width * part + 4 * x.size),
        ),
        name="project",
    )(x, rank_column, gain, router, *tables_k, *tables_q, w)


def reach_of(block, length, picks):
    return max((block + 1) * QBLOCK + length - picks, length // 2)


def clear_of(block):
    return block * QBLOCK


def block_scores(q, k, limit, block, reach):
    scores = dot_nn(k[:reach], q)
    clear = clear_of(block)
    tail = scores[clear:] if clear else scores
    key = lax.broadcasted_iota(jnp.int32, tail.shape, 0) + clear
    tail = jnp.where(key <= limit, tail, NEG)
    return jnp.concatenate([scores[:clear], tail], axis=0) if clear else tail


def side_by_side(value, cols):
    return jnp.concatenate(
        [value[head * HD : (head + 1) * HD, cols] for head in range(GROUP)], axis=1
    )


def attend_body(q, k, vt, limit, out, total):
    length = k.shape[1]
    picks = q.shape[1]
    for block in range(picks // QBLOCK):
        cols = slice(block * QBLOCK, (block + 1) * QBLOCK)
        reach = reach_of(block, length, picks)
        limits = jnp.concatenate([limit[:, cols]] * GROUP, axis=1)
        scores = block_scores(side_by_side(q, cols), k[0], limits, block, reach)
        top = jnp.max(scores, axis=0, keepdims=True)
        weight = jnp.exp(scores - top)
        mass = jnp.sum(weight, axis=0, keepdims=True)
        mixed = (dot_nn(vt[:, :reach], weight.astype(BF)) / mass).astype(BF)
        logs = top + jnp.log(mass)
        for head in range(GROUP):
            part = slice(head * QBLOCK, (head + 1) * QBLOCK)
            out[head * HD : (head + 1) * HD, cols] = mixed[:, part]
            total[0, head : head + 1, cols] = logs[:, part]


def attend(q, k, vt, limit):
    width, picks = q.shape
    length = k.shape[1]
    part = GROUP * HD
    return pl.pallas_call(
        attend_body,
        grid=(KVH,),
        in_specs=[
            pl.BlockSpec((part, picks), lambda i: (i, 0)),
            pl.BlockSpec((1, length, HD), lambda i: (i, 0, 0)),
            pl.BlockSpec((HD, length), lambda i: (i, 0)),
            whole((1, picks)),
        ],
        out_specs=[
            pl.BlockSpec((part, picks), lambda i: (i, 0)),
            pl.BlockSpec((1, GROUP, picks), lambda i: (i, 0, 0)),
        ],
        out_shape=[struct((width, picks), BF), struct((KVH, GROUP, picks), F32)],
        compiler_params=params(),
        cost_estimate=cost(
            16 * width * length * picks, 4 * width * picks, H * length * picks
        ),
        name="attend",
    )(q, k, vt, limit)


def attend_back_body(
    q, k, kt, v, limit, total, grad, mixed, cos_k, sin_k, cos_q, sin_q,
    gq_out, gk_out, gv_out, gk, gv,
):
    length = k.shape[1]
    picks = q.shape[1]
    half = HD // 2
    gk[...] = jnp.zeros_like(gk)
    gv[...] = jnp.zeros_like(gv)
    for block in range(picks // QBLOCK):
        cols = slice(block * QBLOCK, (block + 1) * QBLOCK)
        reach = reach_of(block, length, picks)
        limits = jnp.concatenate([limit[:, cols]] * GROUP, axis=1)
        q_part, g_part = side_by_side(q, cols), side_by_side(grad, cols)
        scores = block_scores(q_part, k[0], limits, block, reach)
        logs = jnp.concatenate([total[0, head : head + 1, cols] for head in range(GROUP)], axis=1)
        weight = jnp.exp(scores - logs)
        delta = jnp.sum(
            g_part.astype(F32) * side_by_side(mixed, cols).astype(F32), axis=0, keepdims=True
        )
        pull = dot_nn(v[0, :reach], g_part)
        back = (weight * (pull - delta)).astype(BF)
        gq = dot_nn(kt[:, :reach], back) * HD ** (-0.5)
        gk[:reach] += dot_nt(back, q_part)
        gv[:reach] += dot_nt(weight.astype(BF), g_part)
        for head in range(GROUP):
            part = slice(head * QBLOCK, (head + 1) * QBLOCK)
            a, b = turn(gq[:half, part], gq[half:, part], cos_q[:, cols], sin_q[:, cols], -1.0)
            gq_out[head * HD : head * HD + half, cols] = a.astype(BF)
            gq_out[head * HD + half : (head + 1) * HD, cols] = b.astype(BF)
    turned = gk[...].T
    a, b = turn(turned[:half], turned[half:], cos_k[...], sin_k[...], -1.0)
    gk_out[:half] = a.astype(BF)
    gk_out[half:] = b.astype(BF)
    gv_out[...] = gv[...].T.astype(BF)


def attend_back(first, count, q, k, kt, v, limit, total, grad, mixed, tables_k, tables_q):
    picks = q.shape[1]
    length = k.shape[1]
    part = GROUP * HD
    half = HD // 2
    wide = pl.BlockSpec((part, picks), lambda i: (first + i, 0))
    tall = pl.BlockSpec((1, length, HD), lambda i: (first + i, 0, 0))
    flat = pl.BlockSpec((HD, length), lambda i: (first + i, 0))
    return pl.pallas_call(
        attend_back_body,
        grid=(count,),
        in_specs=[
            wide, tall, flat, tall, whole((1, picks)),
            pl.BlockSpec((1, GROUP, picks), lambda i: (first + i, 0, 0)),
            wide, wide,
            whole((half, length)), whole((half, length)),
            whole((half, picks)), whole((half, picks)),
        ],
        out_specs=[
            pl.BlockSpec((part, picks), lambda i: (i, 0)),
            pl.BlockSpec((HD, length), lambda i: (i, 0)),
            pl.BlockSpec((HD, length), lambda i: (i, 0)),
        ],
        out_shape=[
            struct((count * part, picks), BF),
            struct((count * HD, length), BF),
            struct((count * HD, length), BF),
        ],
        scratch_shapes=[pltpu.VMEM((length, HD), F32), pltpu.VMEM((length, HD), F32)],
        compiler_params=params(),
        cost_estimate=cost(
            40 * count * part * length * picks, 8 * count * part * picks, count * GROUP * length * picks
        ),
        name="attend_back",
    )(q, k, kt, v, limit, total, grad, mixed, *tables_k, *tables_q)


def merge_body(mixed, picked, gain, w, branch, inverse_out, normed, hidden, square):
    step = pl.program_id(0)
    width = mixed.shape[0]
    part = width // pl.num_programs(0)
    rows = pl.ds(pl.multiple_of(step * part, 8), part)

    @pl.when(step == 0)
    def _():
        square[...] = jnp.zeros_like(square)

    value = dot_tn(w[0, :, w.shape[2] - part :], mixed[...])
    branch[...] = value
    total = picked[rows, :].astype(F32) + value
    hidden[rows, :] = total
    square[...] += jnp.sum(total * total, axis=0, keepdims=True)

    @pl.when(step == pl.num_programs(0) - 1)
    def _():
        inverse = lax.rsqrt(square[...] / width + EPSILON)
        inverse_out[...] = inverse
        normed[...] = (hidden[...] * inverse * gain[:, :1]).astype(BF)


def merge(mixed, picked, gain, w):
    width, picks = mixed.shape
    blocks, _, wide = w.shape
    part = width // blocks
    return pl.pallas_call(
        merge_body,
        grid=(blocks,),
        in_specs=[
            whole((width, picks)),
            whole((width, picks)),
            whole((width, LANES)),
            pl.BlockSpec((1, width, wide), lambda i: (i, 0, 0)),
        ],
        out_specs=[
            pl.BlockSpec((part, picks), lambda i: (i, 0)),
            whole((1, picks)),
            whole((width, picks)),
        ],
        out_shape=[
            struct((width, picks), F32),
            struct((1, picks), F32),
            struct((width, picks), BF),
        ],
        scratch_shapes=[pltpu.VMEM((width, picks), F32), pltpu.VMEM((1, picks), F32)],
        compiler_params=params(),
        cost_estimate=cost(2 * width * width * picks, 14 * width * picks + 2 * w.size),
        name="merge",
    )(mixed, picked, gain, w)


def down_half(part):
    return -(-part // 32) * 16


def ffn_weights(who, first, blocks, sources, w_pair, w_down, done):
    step, steps = pl.program_id(0), pl.num_programs(0)
    slot = lax.rem(step, 2)
    width, hidden = w_pair.shape[1], w_down.shape[2]
    gates, ups = slice(0, hidden), slice(hidden, 2 * hidden)

    def copies(step, at):
        turn = blocks - 1 - first - step
        block = turn ^ who[0]
        if len(sources) == 2:
            some = [
                (sources[0].at[block], w_pair.at[at]),
                (sources[1].at[block], w_down.at[at]),
            ]
        else:
            (source,) = sources
            pairs, _, columns, _, _ = source.shape
            height, part = width // pairs, width // columns
            half = down_half(part)
            some = []
            for i in range(pairs):
                place = slice(i * height, (i + 1) * height)
                some.append((source.at[i, 0, turn, :height], w_pair.at[at, place, gates]))
                some.append((source.at[i, 1, turn, :height], w_pair.at[at, place, ups]))
            for c in range(columns):
                begin = pl.multiple_of((c ^ who[0]) * part, 16)
                top = pl.ds(begin, half)
                some.append((source.at[block, 0, c, height : height + half], w_down.at[at, top]))
                end = pl.ds(pl.multiple_of(begin + half, 16), part - half)
                rest = slice(height + 2 * half - part, height + half)
                some.append((source.at[block, 1, c, rest], w_down.at[at, end]))
        return [
            pltpu.make_async_copy(source, target, done.at[at, i])
            for i, (source, target) in enumerate(some)
        ]

    @pl.when(step == 0)
    def _():
        for copy in copies(step, slot):
            copy.start()

    @pl.when(step + 1 < steps)
    def _():
        for copy in copies(step + 1, 1 - slot):
            copy.start()

    for copy in copies(step, slot):
        copy.wait()
    return slot


def ffn_scratch(width, sources):
    hidden = sources[-1].shape[-1]
    count = 2
    if len(sources) == 1:
        count = 2 * (sources[0].shape[0] + sources[0].shape[2])
    return [
        pltpu.VMEM((2, width, 2 * hidden), BF),
        pltpu.VMEM((2, width, hidden), BF),
        pltpu.SemaphoreType.DMA((2, count)),
    ]


def ffn_body(many, who, normed, branch, prob, cot, *refs):
    sources, refs = refs[:many], refs[many:]
    gate_out, up_out, active_out, delta, both_out, grad_ffn, forward, *buffers = refs
    w_pair, w_down, _ = buffers
    hidden = w_down.shape[2]
    slot = ffn_weights(who, 0, pl.num_programs(0), sources, *buffers)

    @pl.when(pl.program_id(0) == 0)
    def _():
        forward[...] = branch[...]
        grad_ffn[...] = (prob[...] * cot[...].astype(F32)).astype(BF)

    tokens = normed[...]
    pair = dot_tn(w_pair[slot], tokens)
    gate, up = pair[:hidden], pair[hidden:]
    active = (gate * jax.nn.sigmoid(gate) * up).astype(BF)
    gate_out[0] = gate.astype(BF)
    up_out[0] = up.astype(BF)
    active_out[0] = active
    forward[...] += dot_nn(w_down[slot], active)

    @pl.when(pl.program_id(0) == pl.num_programs(0) - 1)
    def _():
        both = forward[...]
        delta[...] = (prob[...] * both).astype(BF)
        both_out[...] = both.astype(BF)


def ffn(who, normed, branch, prob, cot, blocks, hidden, sources):
    width, picks = normed.shape
    full, row = whole((width, picks)), whole((1, picks))
    far = pl.BlockSpec(memory_space=pl.ANY)
    kept = pl.BlockSpec((1, hidden, picks), lambda i, who: (i, 0, 0))
    kept_shape = struct((blocks, hidden, picks), BF)
    low = struct((width, picks), BF)
    return pl.pallas_call(
        functools.partial(ffn_body, len(sources)),
        grid_spec=pltpu.PrefetchScalarGridSpec(
            num_scalar_prefetch=1,
            grid=(blocks,),
            in_specs=[full, full, row, full] + [far] * len(sources),
            out_specs=[kept] * 3 + [full] * 3,
            scratch_shapes=[pltpu.VMEM((width, picks), F32)] + ffn_scratch(width, sources),
        ),
        out_shape=[kept_shape] * 3 + [low] * 3,
        compiler_params=params(60),
        cost_estimate=cost(
            6 * width * hidden * blocks * picks, 6 * width * hidden * blocks + 8 * width * picks
        ),
        name="ffn",
    )(who, normed, branch, prob, cot, *sources)


def down_grad_body(who, grad_ffn, active, keep, send):
    here, columns, half, lanes = keep.shape
    part = grad_ffn.shape[0] // columns
    even = who[2] == 0
    for c in range(columns):
        value = dot_nt(grad_ffn[c * part : (c + 1) * part], active[0])
        low, high = value[:half].astype(BF), value[part - half :].astype(BF)
        mine, other = jnp.where(even, low, high), jnp.where(even, high, low)
        for i in range(here):
            at = i ^ lax.rem(who[1], here) if here > 1 else 0
            keep[at, c ^ who[0]] = mine[:, i * lanes : (i + 1) * lanes]
            send[at, c ^ who[0]] = other[:, i * lanes : (i + 1) * lanes]


def down_grad(who, grad_ffn, active, pairs, columns):
    width, picks = grad_ffn.shape
    blocks, hidden, _ = active.shape
    here = pairs // blocks
    tile = (columns, down_half(width // columns), hidden // here)
    block = pl.BlockSpec(
        (here,) + tile, lambda i, who: ((blocks - 1 - i) ^ who[0] ^ lax.div(who[1], here), 0, 0, 0)
    )
    return pl.pallas_call(
        down_grad_body,
        grid_spec=pltpu.PrefetchScalarGridSpec(
            num_scalar_prefetch=1,
            grid=(blocks,),
            in_specs=[
                whole((width, picks)),
                pl.BlockSpec((1, hidden, picks), lambda i, who: (i, 0, 0)),
            ],
            out_specs=[block, block],
        ),
        out_shape=[struct((pairs,) + tile, BF)] * 2,
        compiler_params=params(),
        cost_estimate=cost(2 * blocks * hidden * width * picks, 6 * blocks * hidden * width),
        name="down_grad",
    )(who, grad_ffn, active)


def ffn_back_body(first, blocks, last, many, who, normed, grad_ffn, gate_in, up_in, *refs):
    sources, refs = refs[:many], refs[many:]
    if first:
        carried, refs = refs[0], refs[1:]
    if last:
        (branch, both_in, picked, cot, prob, inverse, gain, router), refs = refs[:8], refs[8:]
    keep_pair, send_pair, refs = refs[0], refs[1], refs[2:]
    outs, backward, buffers = refs[:-4], refs[-4], refs[-3:]
    w_pair, w_down, _ = buffers
    hidden = w_down.shape[2]
    slot = ffn_weights(who, first, blocks, sources, *buffers)
    width = normed.shape[0]
    even = who[2] == 0

    @pl.when(pl.program_id(0) == 0)
    def _():
        backward[...] = carried[...] if first else jnp.zeros_like(backward)

    pull = dot_tn(w_down[slot], grad_ffn[...])
    gate = gate_in[0].astype(F32)
    sigmoid = jax.nn.sigmoid(gate)
    silu = gate * sigmoid
    grad_gate = (pull * up_in[0].astype(F32) * (sigmoid + silu * (1.0 - sigmoid))).astype(BF)
    grad_up = (pull * silu).astype(BF)
    tokens = normed[...]
    grads = jnp.concatenate([grad_gate, grad_up], axis=0)
    backward[...] += dot_nn(w_pair[slot], grads)
    for_pair = dot_nt(tokens, grads).astype(BF)
    for_gate, for_up = for_pair[:, :hidden], for_pair[:, hidden:]
    pieces, _, height, _ = keep_pair.shape
    for i in range(pieces):
        place = slice(i * height, (i + 1) * height)
        at = i ^ who[1] if pieces > 1 else 0
        keep_pair[at, 0] = jnp.where(even, for_gate[place], for_up[place])
        send_pair[at, 0] = jnp.where(even, for_up[place], for_gate[place])

    @pl.when(pl.program_id(0) == pl.num_programs(0) - 1)
    def _():
        if not last:
            outs[0][...] = backward[...]
            return
        grad_attn, rest_out, gain_out, router_out = outs
        share = prob[...]
        cot_full = cot[...].astype(F32)
        slope = share * (1.0 - share) * jnp.sum(
            cot_full * both_in[...].astype(F32), axis=0, keepdims=True
        )
        token = picked[...].astype(F32)
        router_out[...] = jnp.sum(slope * token, axis=1, keepdims=True)
        merged = token + branch[...]
        inv = inverse[...]
        grad_norm = backward[...]
        gain_out[...] = jnp.sum(grad_norm * merged * inv, axis=1, keepdims=True)
        unit = grad_norm * gain[:, :1]
        along = jnp.sum(unit * merged, axis=0, keepdims=True) / width
        grad_hidden = inv * unit - merged * (inv * inv * inv * along)
        grad_attn[...] = (grad_hidden + share * cot_full).astype(BF)
        rest_out[...] = (grad_hidden + slope * router[:, :1]).astype(BF)


def ffn_back(who, first, count, last, pieces, normed, grad_ffn, gate, up, sources, carried, tail):
    width, picks = normed.shape
    hidden = gate.shape[1]
    height = width // pieces
    full, row, column = whole((width, picks)), whole((1, picks)), whole((width, 1))
    far = pl.BlockSpec(memory_space=pl.ANY)
    kept = pl.BlockSpec((1, hidden, picks), lambda i, who: (i + first, 0, 0))
    tall = pl.BlockSpec((pieces, 1, height, hidden), lambda i, who: (0, i, 0, 0))
    tall_shape = struct((pieces, count, height, hidden), BF)
    low, thin = struct((width, picks), BF), struct((width, 1), F32)
    extra = ([carried] if first else []) + (list(tail) if last else [])
    extra_specs = ([full] if first else []) + ([full] * 4 + [row] * 2 + [whole((width, LANES))] * 2 if last else [])
    return pl.pallas_call(
        functools.partial(ffn_back_body, first, gate.shape[0], last, len(sources)),
        grid_spec=pltpu.PrefetchScalarGridSpec(
            num_scalar_prefetch=1,
            grid=(count,),
            in_specs=[full, full, kept, kept] + [far] * len(sources) + extra_specs,
            out_specs=[tall, tall] + ([full, full, column, column] if last else [full]),
            scratch_shapes=[pltpu.VMEM((width, picks), F32)] + ffn_scratch(width, sources),
        ),
        out_shape=[tall_shape, tall_shape]
        + ([low, low, thin, thin] if last else [struct((width, picks), F32)]),
        compiler_params=params(60),
        cost_estimate=cost(
            10 * width * hidden * count * picks, 10 * width * hidden * count + 12 * width * picks
        ),
        name="ffn_back",
    )(who, normed, grad_ffn, gate, up, *sources, *extra)


def merge_back_body(mixed, grad, w, gw, grad_mixed, total):
    step = pl.program_id(0)
    part = gw.shape[2]
    rows = pl.ds(pl.multiple_of(step * part, 8), part)
    piece = grad[rows, :]
    gw[0] = dot_nt(mixed[...], piece).astype(BF)
    value = dot_nn(w[0, :, w.shape[2] - part :], piece)

    @pl.when(step == 0)
    def _():
        total[...] = value

    @pl.when(step > 0)
    def _():
        total[...] += value

    @pl.when(step == pl.num_programs(0) - 1)
    def _():
        grad_mixed[...] = total[...].astype(BF)


def merge_back(mixed, grad, w):
    width, picks = mixed.shape
    blocks, _, wide = w.shape
    part = width // blocks
    block = pl.BlockSpec((1, width, part), lambda i: (i, 0, 0))
    wide_block = pl.BlockSpec((1, width, wide), lambda i: (i, 0, 0))
    return pl.pallas_call(
        merge_back_body,
        grid=(blocks,),
        in_specs=[whole((width, picks)), whole((width, picks)), wide_block],
        out_specs=[block, whole((width, picks))],
        out_shape=[struct((blocks, width, part), BF), struct((width, picks), BF)],
        scratch_shapes=[pltpu.VMEM((width, picks), F32)],
        compiler_params=params(),
        cost_estimate=cost(4 * width * width * picks, 6 * width * picks + 4 * w.size),
        name="merge_back",
    )(mixed, grad, w)


def mixing_grad_body(
    who, x, rank, gain, *refs
):
    gq, gk, gv, refs = refs[:2], refs[2:4], refs[4:6], refs[6:]
    gw_out, w, keep, send, grads_out, gain_out, normed, gq_full, gkv_full = refs
    step = pl.program_id(0)
    width = x.shape[0]
    q_part = width // pl.num_programs(0)
    kv_part = KVH * HD // pl.num_programs(0)
    even = who[2] == 0

    @pl.when(step == 0)
    def _():
        full = x[...].astype(F32)
        inverse = lax.rsqrt(jnp.sum(full * full, axis=0, keepdims=True) / width + EPSILON)
        normed[...] = (full * inverse * gain[:, :1]).astype(BF)
        chosen = pick_rows(rank[...], gq[0].shape[1])
        at = 0
        for piece in gq:
            gq_full[at : at + piece.shape[0]] = dot_nn(piece[...], chosen).astype(BF)
            at += piece.shape[0]
        for i, pieces in enumerate((gk, gv)):
            at = 0
            for piece in pieces:
                gkv_full[i, at : at + piece.shape[0]] = piece[...]
                at += piece.shape[0]

    q_rows = pl.ds(pl.multiple_of(step * q_part, 8), q_part)
    kv_rows = pl.ds(pl.multiple_of(step * kv_part, 8), kv_part)
    grads = jnp.concatenate(
        [gq_full[q_rows, :], gkv_full[0, kv_rows, :], gkv_full[1, kv_rows, :]], axis=0
    )
    grads_out[0] = grads
    value = dot_nt(normed[...], grads)
    share = jnp.sum(
        value * w[0, :, : grads.shape[0]].astype(F32), axis=1, keepdims=True
    ) / gain[:, :1]
    gain_out[...] = jnp.where(step == 0, share, gain_out[...] + share)
    value = jnp.concatenate([value, gw_out[0].astype(F32)], axis=1)
    pairs = keep.shape[0]
    rows = width // (2 * pairs)
    for pair in range(pairs):
        low = value[2 * pair * rows : (2 * pair + 1) * rows]
        high = value[(2 * pair + 1) * rows : (2 * pair + 2) * rows]
        keep[pair ^ who[1], 0, :rows] = jnp.where(even, low, high).astype(BF)
        send[pair ^ who[1], 0, :rows] = jnp.where(even, high, low).astype(BF)


def mixing_grad(who, x, rank_row, gain, gq, gk, gv, gw_out, w, pairs):
    width, length = x.shape
    picks = gq[0].shape[1]
    blocks, _, out_part = gw_out.shape
    kv = KVH * HD
    part = (width + 2 * kv) // blocks
    rows = width // (2 * pairs) + VECTOR_ROWS
    split = pl.BlockSpec((pairs, 1, rows, part + out_part), lambda i, who: (0, i ^ who[0], 0, 0))
    split_shape = struct((pairs, blocks, rows, part + out_part), BF)
    return pl.pallas_call(
        mixing_grad_body,
        grid_spec=pltpu.PrefetchScalarGridSpec(
            num_scalar_prefetch=1,
            grid=(blocks,),
            in_specs=[
                whole((width, length)),
                whole((1, length)),
                whole((width, LANES)),
                *(whole(piece.shape) for piece in (*gq, *gk, *gv)),
                pl.BlockSpec((1, width, out_part), lambda i, who: (i, 0, 0)),
                pl.BlockSpec((1,) + w.shape[1:], lambda i, who: (i, 0, 0)),
            ],
            out_specs=[
                split,
                split,
                pl.BlockSpec((1, part, length), lambda i, who: (i, 0, 0)),
                whole((width, 1)),
            ],
            scratch_shapes=[
                pltpu.VMEM((width, length), BF),
                pltpu.VMEM((width, length), BF),
                pltpu.VMEM((2, kv, length), BF),
            ],
        ),
        out_shape=[
            split_shape,
            split_shape,
            struct((blocks, part, length), BF),
            struct((width, 1), F32),
        ],
        compiler_params=params(),
        cost_estimate=cost(2 * width * length * (picks + width + 2 * kv), 10 * x.size),
        name="mixing_grad",
    )(who, x, rank_row, gain, *gq, *gk, *gv, gw_out, w)


def project_back_body(x, rank, gain, grads, rest, w, out, total):
    step = pl.program_id(0)
    width = x.shape[0]
    part = grads.shape[1]

    @pl.when(step == 0)
    def _():
        total[...] = jnp.zeros_like(total)

    total[...] += dot_nn(w[0, :, :part], grads[0])

    @pl.when(step == pl.num_programs(0) - 1)
    def _():
        full = x[...].astype(F32)
        inv = lax.rsqrt(jnp.sum(full * full, axis=0, keepdims=True) / width + EPSILON)
        grad_norm = total[...]
        unit = grad_norm * gain[:, :1]
        along = jnp.sum(unit * full, axis=0, keepdims=True) / width
        chosen = pick_rows(rank[...], rest.shape[1])
        out[...] = (
            inv * unit - full * (inv * inv * inv * along) + dot_nn(rest[...], chosen)
        ).astype(BF)


def project_back(x, rank_row, gain, grads, rest, w):
    width, length = x.shape
    picks = rest.shape[1]
    blocks, part, _ = grads.shape
    return pl.pallas_call(
        project_back_body,
        grid=(blocks,),
        in_specs=[
            whole((width, length)),
            whole((1, length)),
            whole((width, LANES)),
            pl.BlockSpec((1, part, length), lambda i: (i, 0, 0)),
            whole((width, picks)),
            pl.BlockSpec((1,) + w.shape[1:], lambda i: (i, 0, 0)),
        ],
        out_specs=whole((width, length)),
        out_shape=struct((width, length), BF),
        scratch_shapes=[pltpu.VMEM((width, length), F32)],
        compiler_params=params(),
        cost_estimate=cost(2 * width * length * (picks + blocks * part), 10 * x.size + 2 * w.size),
        name="project_back",
    )(x, rank_row, gain, grads, rest, w)


def columns(value):
    return jnp.broadcast_to(value[:, None], (value.shape[0], LANES))


def hold(*values):
    return lax.optimization_barrier(values)


def swap(value):
    count = lax.axis_size("row")
    return lax.ppermute(value, "row", [(i, i ^ 1) for i in range(count)])


def partner(value, axis, k):
    count = lax.axis_size(axis)
    far = k if axis == "col" else 2 * k
    return lax.ppermute(value, axis, [(i, i ^ far) for i in range(count)])


def collect(value, axis, partners):
    return [partner(value, axis, k) if k else value for k in partners]


def spread(values, axis):
    return [values[0]] + [partner(value, axis, k) for k, value in enumerate(values) if k]


def scatter_col(value, other):
    while value.shape[0] > 1:
        keep, send = value[0::2], value[1::2]
        step = lax.axis_size("col") // value.shape[0]
        got, other = hold(partner(send, "col", step), other)
        value = add_up((keep, got))
        if value.shape[0] > 1:
            value = value.astype(BF)
    return value[0], other


def add_up(values):
    return sum(value.astype(F32) for value in values)


def pack(first, second):
    if first.shape[1] == second.shape[1]:
        return [jnp.concatenate([first, second], axis=0)]
    return [first, second]


def unpack(values, rows):
    return (values[0][:rows], values[0][rows:]) if len(values) == 1 else tuple(values)


def pair_up(keep, got):
    return [add_up((a, b)).astype(BF) for a, b in zip(keep, got)]


def to_owner(value):
    copies = lax.axis_size("col") // value.shape[0]
    if copies > 1:
        value = jnp.concatenate([value] * copies, axis=0)
    moved = lax.all_to_all(value, "col", split_axis=0, concat_axis=1, tiled=True)
    return moved[0]


def from_owner(value, sequences):
    count = lax.axis_size("col")
    value = value.reshape(count, value.shape[0] // count, value.shape[1])
    moved = lax.all_to_all(value, "col", split_axis=0, concat_axis=0, tiled=True)
    return moved[:sequences]


def rope_tables(positions):
    half = HD // 2
    frequency = jnp.exp(jnp.arange(half, dtype=F32) * (-2.0 * math.log(ROPE_BASE) / HD))
    angles = frequency[:, None] * positions.astype(F32)[None, :]
    return jnp.cos(angles), jnp.sin(angles)


def on_device(
    resid, cotangent, prefix, slot, chosen, norm1_gain, norm2_gain, router,
    w_query, w_key, w_value, w_out, w_gate, w_up, w_down,
):
    col_count, row_count = lax.axis_size("col"), lax.axis_size("row")
    column = lax.axis_index("col")
    sequences, part, length = resid.shape
    width = part * col_count
    picks = chosen.shape[2]
    copies = col_count // sequences
    own = lax.rem(column, sequences)
    rows, hidden = w_gate.shape
    down_rows = w_down.shape[0]
    pairs = row_count // 2
    mixing_part = part + 2 * w_key.shape[1] + part

    own_pair_index = lax.axis_index("row") >> 1
    core = lax.axis_index("row") & 1
    even = core == 0
    who = jnp.stack([column, own_pair_index, core]).astype(jnp.int32)
    aligned = 2 * rows % 16 == 0 and hidden % 128 == 0

    half = col_count // 2

    mine = jnp.where(even, w_gate, w_up)
    other = swap(jnp.where(even, w_up, w_gate))
    pair = jnp.concatenate([jnp.where(even, mine, other), jnp.where(even, other, mine)], axis=0)
    down_rows_kept = down_half(part)
    turned = w_down.T
    low, high = turned[:down_rows_kept], turned[part - down_rows_kept :]
    mine, other = jnp.where(even, low, high), swap(jnp.where(even, high, low))
    down = jnp.concatenate([jnp.where(even, mine, other), jnp.where(even, other, mine)], axis=1)
    mixing = jnp.concatenate([w_query, w_key, w_value, w_out], axis=1)
    mixing, pair, down = hold(collect(mixing, "col", range(col_count)), pair, down)
    mixing, x = jnp.stack(mixing), resid.astype(BF)
    if aligned:
        sources = jnp.concatenate([pair, down], axis=0)
        sources, mixing, x = hold(
            collect(sources, "col", range(col_count)), collect(mixing, "row", range(pairs)), x
        )
        sources = lax.all_gather(jnp.stack(sources), "row", axis=0)
        sources = (sources.reshape((pairs, 2) + sources.shape[1:]),)
    else:
        mixing, x = hold(collect(mixing, "row", range(pairs)), x)
        pair_all = lax.all_gather(pair, ("row", "col"), axis=0)
        pair_all = pair_all.reshape(pairs, 2, col_count, 2 * rows, hidden).transpose(2, 0, 3, 1, 4)
        down_all = lax.all_gather(down, ("row", "col"), axis=0)
        down_all = down_all.reshape((col_count, pairs // col_count, 2, col_count) + down.shape)
        down_all = jnp.concatenate(
            [down_all[:, :, 0], down_all[:, :, 1, :, 2 * down_rows_kept - part :]], axis=3
        )
        sources = (
            pair_all.reshape(col_count, width, 2 * hidden),
            down_all.transpose(0, 2, 3, 1, 4).reshape(col_count, width, hidden),
        )
    every = jnp.arange(length, dtype=jnp.int32)
    chosen_of = chosen[:, 0][slot]
    selected = jnp.any(every[None, :, None] == chosen_of[:, None, :], axis=2)
    before = (every[:, None] < every[None, :]).astype(BF)
    places = jnp.dot(selected.astype(BF), before, preferred_element_type=F32)
    ranks = jnp.where(selected, places.astype(jnp.int32), -1)
    rank = lax.dynamic_index_in_dim(ranks, own, 0, keepdims=False)
    prefix_len = lax.dynamic_index_in_dim(prefix, own, 0, keepdims=False)
    place = jnp.arange(picks, dtype=jnp.int32)
    spot = jnp.sum(jnp.where(rank[None, :] == place[:, None], every[None, :], 0), axis=1)
    limit = jnp.maximum(spot, prefix_len - 1)[None, :]
    tables_k = rope_tables(every)
    tables_q = rope_tables(spot)
    gain_one, gain_two, router = columns(norm1_gain), columns(norm2_gain), columns(router)
    cot = gather_tokens(cotangent, ranks[:, :, None], picks)

    mixing_other, mixing, rank_column, gain_one, gain_two, router = hold(
        [swap(piece) for piece in mixing], mixing, columns(rank), gain_one, gain_two, router
    )
    if aligned:
        mixing = join(who, mixing, mixing_other)
    else:
        order = jnp.arange(pairs) ^ own_pair_index
        mixing = jnp.stack([jnp.stack(mixing), jnp.stack(mixing_other)])[jnp.stack([core, 1 - core])]
        mixing = mixing[:, order].transpose(2, 1, 0, 3, 4).reshape(col_count, width, mixing_part)
        mixing = mixing[jnp.arange(col_count) ^ column]
    (
        x, mixing, cot, limit, tables_k, tables_q, rank_column, gain_one, gain_two, router,
    ) = hold(
        to_owner(x), mixing, cot, limit, tables_k, tables_q, rank_column, gain_one, gain_two, router
    )
    cot = to_owner(cot)
    picked, prob, q, kt, k, vt, v = project(
        x, rank_column, gain_one, router, tables_k, tables_q, mixing
    )
    mixed, mass = attend(q, k, vt, limit)
    (branch, inverse, normed), cot = hold(merge(mixed, picked, gain_two, mixing), cot)
    gate, up, active, delta, both, grad_ffn = ffn(
        who, normed, branch, prob, cot, col_count, hidden, sources
    )
    (keep_down, send_down), delta, gate = hold(
        down_grad(who, grad_ffn, active, pairs, col_count), delta, gate
    )
    delta = [
        lax.dynamic_slice_in_dim(delta, (column ^ k) * part, part, 0) for k in range(sequences)
    ]
    delta, keep_down, send_down = hold(delta, keep_down, send_down)
    delta = [partner(value, "col", k) if k else value for k, value in enumerate(delta)]
    pieces = pairs if aligned else 1
    back_args = (pieces, normed, grad_ffn, gate, up, sources)
    tail = (branch, both, picked, cot, prob, inverse, gain_two, router)

    def by_pairs(value):
        if aligned:
            return value
        value = value[0].reshape(half, pairs, 2 * rows, hidden).transpose(1, 0, 2, 3)
        return value[jnp.arange(pairs) ^ own_pair_index]

    got_down, (keep_low, send_low, carried), keep_down, near = hold(
        swap(send_down),
        ffn_back(who, 0, half, False, *back_args, None, None),
        keep_down,
        delta[1:-1],
    )
    delta[1:-1] = near
    sum_down = pair_up(keep_down, got_down)
    sum_down, send_low, keep_low, carried = hold(sum_down, send_low, keep_low, carried)
    (
        got_low, sum_down, delta,
        (keep_high, send_high, grad_attn, rest, gain_two_grad, router_grad), keep_low,
    ) = hold(
        swap(send_low),
        spread(sum_down, "row"),
        delta,
        ffn_back(who, half, half, True, *back_args, carried, tail),
        keep_low,
    )
    sum_low = pair_up(by_pairs(keep_low), by_pairs(got_low))
    sum_down = list(add_up(sum_down).astype(BF))
    sum_low, sum_down, send_high, keep_high, grad_attn = hold(
        sum_low, sum_down, send_high, keep_high, grad_attn
    )
    sum_low = spread(sum_low, "row")
    got_high, (gw_out, grad_mixed), keep_high = hold(
        swap(send_high), merge_back(mixed, grad_attn, mixing), keep_high
    )
    sum_high = pair_up(by_pairs(keep_high), by_pairs(got_high))
    sum_high, grad_mixed = hold(sum_high, grad_mixed)
    heads = (q, k, kt, v, limit, mass, grad_mixed, mixed, tables_k, tables_q)
    most = (KVH + 1) // 2
    down_far, sum_low, one, sum_high = hold(
        [partner(sum_down[k], "col", k) for k in range(half, col_count)],
        sum_low,
        attend_back(0, most, *heads),
        sum_high,
    )
    far = list(add_up(sum_low).astype(BF))
    far, one, grad_mixed = hold(far, one, grad_mixed)
    far = [partner(value, "col", col_count - 1 - i) for i, value in enumerate(far)]
    heads = heads[:6] + (grad_mixed,) + heads[7:]
    sum_high = spread(sum_high, "row")
    (two,) = hold(attend_back(most, KVH - most, *heads))
    gq, gk, gv = zip(one, two)
    far, sum_high, (*gw_mixing, grads, gain_one_grad) = hold(
        far,
        sum_high,
        mixing_grad(who, x, rank[None, :], gain_one, gq, gk, gv, gw_out, mixing, pairs),
    )
    *near, sum_pair = add_up(sum_high).astype(BF)
    near = [pack(value, sum_down[half - 1 - i]) for i, value in enumerate(near)]
    vectors = jnp.concatenate([gain_one_grad, gain_two_grad, router_grad], axis=1).T.astype(BF)
    vectors = vectors.reshape(3, col_count, part).transpose(1, 0, 2)
    vectors = vectors[jnp.arange(col_count) ^ column]
    vectors = jnp.pad(vectors, ((0, 0), (0, VECTOR_ROWS - 3), (0, mixing_part - part)))
    vectors = jnp.broadcast_to(vectors[None], (pairs,) + vectors.shape)
    keep_mixing, send_mixing = (
        lax.dynamic_update_slice(value, vectors, (0, 0, rows, 0)) for value in gw_mixing
    )
    near, keep_mixing, send_mixing, grads = hold(near, keep_mixing, send_mixing, grads)
    got_mixing, near, back, keep_mixing = hold(
        swap(send_mixing),
        [
            [partner(value, "col", half - 1 - i) for value in values]
            for i, values in enumerate(near)
        ],
        project_back(x, rank[None, :], gain_one, grads, rest, mixing),
        keep_mixing,
    )
    back = from_owner(back, sequences)
    sum_mixing = pair_up(keep_mixing, got_mixing)
    sum_mixing, near, delta, sum_pair = hold(sum_mixing, near, delta, sum_pair)
    block_out = scatter_tokens(who, resid, delta, ranks[:, None, :])
    sum_mixing, block_out, near, sum_pair, far = hold(
        spread(sum_mixing, "row"), block_out, near, sum_pair, far
    )
    sum_mixing = add_up(sum_mixing).astype(BF)
    parts = [unpack(values, 2 * rows) for values in near]
    sum_pair = add_up([sum_pair] + [first for first, _ in parts] + far)
    sum_down = add_up([sum_down[0]] + [second for _, second in parts] + down_far)

    lanes = sum_down.shape[1] // 2
    first, second = sum_down[:, :lanes], sum_down[:, lanes:]
    mine, other = jnp.where(even, first, second), jnp.where(even, second, first)
    other = swap(other.astype(BF)).astype(F32)
    top, end = jnp.where(even, mine, other), jnp.where(even, other, mine)
    gw_down = jnp.concatenate([top, end[2 * down_rows_kept - part :]], axis=0).T

    gw_mixing, resid_grad = scatter_col(sum_mixing, cotangent + back.astype(F32))

    sum_pair = sum_pair.reshape(2, rows, hidden)
    mine = jnp.where(even, sum_pair[0], sum_pair[1])
    other = jnp.where(even, sum_pair[1], sum_pair[0]).astype(BF)
    other = swap(other).astype(F32)
    gw_gate, gw_up = jnp.where(even, mine, other), jnp.where(even, other, mine)
    if copies > 1:
        gw_gate, gw_up, gw_down, gw_mixing = (
            a / copies for a in (gw_gate, gw_up, gw_down, gw_mixing)
        )

    kv_part = w_key.shape[1]
    ends = (part, part + kv_part, part + 2 * kv_part)
    return (
        block_out, resid_grad,
        gw_mixing[rows, :part], gw_mixing[rows + 1, :part], gw_mixing[rows + 2, :part],
        gw_mixing[:rows, : ends[0]], gw_mixing[:rows, ends[0] : ends[1]],
        gw_mixing[:rows, ends[1] : ends[2]], gw_mixing[:rows, ends[2] :],
        gw_gate, gw_up, gw_down,
    )


def solution(mesh):
    block = P("row", "col")
    placed = (
        P("row", "col", None), P("row", "col", None), P("row"), P("row"), P(None, "row", None),
        P(), P(), P(),
        block, block, block, block, block, block, block,
    )
    given = (
        P("row", "col", None), P("row", "col", None), P("col"), P("col"), P("col"),
        block, block, block, block, block, block, block,
    )
    return jax.shard_map(
        on_device, mesh=mesh, in_specs=placed, out_specs=given, check_vma=False
    )
```
